32 devices in a mesh: items: 8 (over z, y), narrow: 4 (over x, core).
Axes of the slice: x: 2, y: 2, z: 4, core: 2. Of those that a mesh axis runs over, the one named last changes fastest.
Arguments:
- tokens: bfloat16 [32, 512, 768], P('items', 'narrow'), may hold values from -6 to 6
- memory: bfloat16 [32, 2048, 768], P('items', 'narrow'), may hold values from -6 to 6
- mem_count: int32 [32], P('items'), may hold values from 768 to 2048, as said below
- cotangent: bfloat16 [32, 512, 768], P('items', 'narrow'), may hold values from -6 to 6
- gain_self: float32 [768], replicated, may hold values from 0.1 to 1.9
- self_query: bfloat16 [768, 768], replicated, may hold values from -0.0546875 to 0.0546875
- self_key: bfloat16 [768, 768], replicated, may hold values from -0.21875 to 0.21875
- self_value: bfloat16 [768, 768], replicated, may hold values from -0.21875 to 0.21875
- self_out: bfloat16 [768, 768], replicated, may hold values from -0.625 to 0.625
- gain_cross: float32 [768], replicated, may hold values from 0.1 to 1.9
- cross_query: bfloat16 [768, 768], replicated, may hold values from -0.0546875 to 0.0546875
- cross_key: bfloat16 [768, 768], replicated, may hold values from -0.21875 to 0.21875
- cross_value: bfloat16 [768, 768], replicated, may hold values from -0.21875 to 0.21875
- cross_out: bfloat16 [768, 768], replicated, may hold values from -1.25 to 1.25
- gain_feed: float32 [768], replicated, may hold values from 0.1 to 1.9
- gate_weight: bfloat16 [768, 2048], replicated, may hold values from -0.21875 to 0.21875
- up_weight: bfloat16 [768, 2048], replicated, may hold values from -0.21875 to 0.21875
- down_weight: bfloat16 [2048, 768], replicated, may hold values from -0.1875 to 0.1875
Outputs:
- result: bfloat16 [32, 512, 768], P('items', 'narrow')
- tokens_grad: float32 [32, 512, 768], P('items', 'narrow')
- memory_grad: float32 [32, 2048, 768], P('items', 'narrow')
- gain_self_grad: float32 [768], replicated
- self_query_grad: float32 [768, 768], P('items', 'narrow')
- self_key_grad: float32 [768, 768], P('items', 'narrow')
- self_value_grad: float32 [768, 768], P('items', 'narrow')
- self_out_grad: float32 [768, 768], P('items', 'narrow')
- gain_cross_grad: float32 [768], replicated
- cross_query_grad: float32 [768, 768], P('items', 'narrow')
- cross_key_grad: float32 [768, 768], P('items', 'narrow')
- cross_value_grad: float32 [768, 768], P('items', 'narrow')
- cross_out_grad: float32 [768, 768], P('items', 'narrow')
- gain_feed_grad: float32 [768], replicated
- gate_weight_grad: float32 [768, 2048], P('items', 'narrow')
- up_weight_grad: float32 [768, 2048], P('items', 'narrow')
- down_weight_grad: float32 [2048, 768], P('items', 'narrow')
The draws below stay inside these ranges and needn't reach their ends.
Inputs may be any that keep to these rules, and one draw needn't show every extreme that they name: `mem_count`: each item's count is 2048, 1024 or 768; memory rows at and past the count are padding, and every draw has items with 2048 and with 768 patches.
All inputs are finite; a program needn't handle non-finite values.
Results may differ from the reference program's by a relative error of at most 0.02555.
The reference program's roundings to bfloat16 on the way count: a program that leaves them out, or rounds other values in their place, can miss the bound.
Values may be sent and summed in bfloat16 or wider, within the bound.
No kernel may reach another device: no remote copies, remote signals or barrier semaphores. Data moves between devices by JAX's collectives and lax.ppermute only.
A program may use at most 320 MiB of HBM per device.

```python
import jax
import jax.numpy as jnp
from jax import lax

D = 768
H = 12
HD = 64
FF = 2048
TAB = 512
MEM = 2048
ITEMS = 32


def draw_mem_count(key, part):
    bucket = jax.random.randint(jax.random.fold_in(key, 11), (ITEMS,), 0, 3)
    counts = jnp.where(bucket == 0, MEM, jnp.where(bucket == 1, MEM // 2, 3 * MEM // 8))
    full_item = jax.random.randint(jax.random.fold_in(key, 12), (), 0, ITEMS)
    offset = jax.random.randint(jax.random.fold_in(key, 13), (), 1, ITEMS)
    second = (full_item + offset) % ITEMS
    item_index = jnp.arange(ITEMS)
    counts = jnp.where(item_index == full_item, MEM, counts)
    counts = jnp.where(item_index == second, 3 * MEM // 8, counts)
    return counts.astype(jnp.int32)


def spiked(entries, own_key, source, target, shards_of, factor):
    owner, partner = [(jnp.arange(entries.shape[axis_at]) // (entries.shape[axis_at] // shards_of)).reshape([-1 if axis == axis_at else 1 for axis in range(entries.ndim)]) for axis_at in (source, target)]
    chosen = jax.random.permutation(own_key, shards_of)[partner]
    strong = (owner == chosen) | (owner == (partner + shards_of // 2) % shards_of)
    return jnp.where(strong, factor * entries, entries)


def level_of(stream_key, shape, cuts, least, high):
    def one(dim, parts):
        steps = jax.random.uniform(jax.random.fold_in(jax.random.fold_in(stream_key, 6), dim), (parts,), jnp.float32, least / len(cuts), high / len(cuts))
        return jnp.repeat(jnp.exp(steps), shape[dim] // parts).reshape((-1,) + (1,) * (len(shape) - dim - 1))

    loudness = one(*cuts[0])
    for cut in cuts[1:]:
        loudness = loudness * one(*cut)
    return loudness


def normal_values(stream_key, extent, spread, most, cuts=(), dtype=jnp.bfloat16):
    array = jax.random.normal(stream_key, extent, jnp.float32) * spread
    if len(cuts) > 0:
        array = level_of(stream_key, extent, cuts, -0.22, 0.18) * array
    return jnp.clip(array, min=-most, max=most).astype(dtype)


def bell_draw_with(own_key, shape, width, reach, cuts, heavy, dtype=jnp.bfloat16):
    values = width * jax.random.normal(own_key, shape, jnp.float32)
    if cuts:
        values = values * level_of(own_key, shape, cuts, -0.22, 0.18)
    return jnp.clip(spiked(values, jax.random.fold_in(own_key, 3), *heavy), -reach, reach).astype(dtype)


def setup_inputs(seed: int = 0) -> dict:
    key_of = jax.random.split(jax.random.key(seed), 19)
    tokens = bell_draw_with(key_of[0], (ITEMS, TAB, D), 1.0, 6.0, ((0, 8), (1, 4)), (0, 2, 8, 2.0))
    memory = normal_values(key_of[1], (ITEMS, MEM, D), 1.0, 6.0, ((0, 8), (1, 4)))
    mem_count = draw_mem_count(jax.random.fold_in(key_of[18], 71), 0)
    cotangent = normal_values(key_of[3], (ITEMS, TAB, D), 1.0, 6.0, ((0, 8), (1, 4)))
    gain_self = jnp.clip(1.0 + 0.18 * jax.random.normal(key_of[4], (D,), jnp.float32), 0.1, 1.9)
    self_query = normal_values(key_of[5], (D, D), (16 * D) ** -0.5, 0.0546875)
    self_key = normal_values(key_of[6], (D, D), D ** -0.5, 0.21875)
    self_value = normal_values(key_of[7], (D, D), D ** -0.5, 0.21875)
    self_out = normal_values(key_of[8], (D, D), (D // 8) ** -0.5, 0.625)
    gain_cross = jnp.clip(1.0 + 0.18 * jax.random.normal(key_of[9], (D,), jnp.float32), 0.1, 1.9)
    cross_query = normal_values(key_of[10], (D, D), (16 * D) ** -0.5, 0.0546875)
    cross_key = normal_values(key_of[11], (D, D), D ** -0.5, 0.21875)
    cross_value = normal_values(key_of[12], (D, D), D ** -0.5, 0.21875)
    cross_out = normal_values(key_of[13], (D, D), (D // 32) ** -0.5, 1.25)
    gain_feed = jnp.clip(1.0 + 0.18 * jax.random.normal(key_of[14], (D,), jnp.float32), 0.1, 1.9)
    gate_weight = normal_values(key_of[15], (D, FF), D ** -0.5, 0.21875)
    up_weight = normal_values(key_of[16], (D, FF), D ** -0.5, 0.21875)
    down_weight = normal_values(key_of[17], (FF, D), (FF // 2) ** -0.5, 0.1875)
    return dict(tokens=tokens, memory=memory, mem_count=mem_count, cotangent=cotangent, gain_self=gain_self, self_query=self_query, self_key=self_key, self_value=self_value, self_out=self_out, gain_cross=gain_cross, cross_query=cross_query, cross_key=cross_key, cross_value=cross_value, cross_out=cross_out, gain_feed=gain_feed, gate_weight=gate_weight, up_weight=up_weight, down_weight=down_weight)


eps = 1e-06
neg_big = -1e+30
gelu_scale = 0.7978845608028654

@jax.custom_vjp
def low(v):
    return lax.optimization_barrier(v.astype(jnp.bfloat16)).astype(jnp.float32)

@jax.custom_vjp
def low_back(v):
    return v

def low_keep(v):
    return (low(v), None)

def low_pass(kept, grad):
    return (grad,)

def back_keep(v):
    return (v, None)

def back_low(kept, grad):
    return (low(grad),)
low.defvjp(low_keep, low_pass)
low_back.defvjp(back_keep, back_low)

def rms_scale(hidden_rows, gain_vector):
    inverse = lax.rsqrt(lax.optimization_barrier(jnp.mean(hidden_rows * hidden_rows, axis=-1, keepdims=True)) + eps)
    return hidden_rows * inverse * gain_vector

def gelu_tanh(inputs):
    return 0.5 * inputs * (1.0 + jnp.tanh(gelu_scale * (inputs + 0.044715 * inputs * inputs * inputs)))

def matmul_high(left_side, right_side):
    return jnp.dot(left_side, right_side, precision=lax.Precision.HIGHEST, preferred_element_type=jnp.float32)

def attend_item(queries, keys_in, values_in, allowed):
    scores = jnp.einsum('qhd,khd->hqk', queries, keys_in, precision=lax.Precision.HIGHEST)
    scores = low_back(scores)
    scores = jnp.where(allowed[None], scores, neg_big)
    row_peak = lax.optimization_barrier(jnp.max(scores, axis=-1, keepdims=True))
    exp_scores = jnp.exp(scores - row_peak)
    probs_full = exp_scores / lax.optimization_barrier(jnp.sum(exp_scores, axis=-1, keepdims=True))
    mixed_heads = jnp.einsum('hqk,khd->qhd', low(probs_full), values_in, precision=lax.Precision.HIGHEST)
    return mixed_heads.reshape(queries.shape[0], queries.shape[1] * queries.shape[2])
attend_saved = jax.checkpoint(attend_item)

def reference(tokens, memory, mem_count, cotangent, gain_self, self_query, self_key, self_value, self_out, gain_cross, cross_query, cross_key, cross_value, cross_out, gain_feed, gate_weight, up_weight, down_weight):
    causal = jnp.arange(TAB)[:, None] >= jnp.arange(TAB)[None, :]
    patch_live = jnp.arange(MEM)[None, :] < mem_count[:, None]

    def split_heads(flat_rows):
        return flat_rows.reshape(ITEMS, -1, H, HD)

    def self_item(packed):
        return attend_saved(packed[0], packed[1], packed[2], causal)

    def cross_item(packed):
        return attend_saved(packed[0], packed[1], packed[2], packed[3][None, :])

    def forward(tokens, memory, gain_self, self_query, self_key, self_value, self_out, gain_cross, cross_query, cross_key, cross_value, cross_out, gain_feed, gate_weight, up_weight, down_weight):
        token_rows = tokens.reshape(-1, D)
        normed_one = low(rms_scale(token_rows, gain_self))
        query_one = low_back(low(matmul_high(normed_one, self_query)))
        key_one = low_back(low(matmul_high(normed_one, self_key)))
        value_one = low_back(low(matmul_high(normed_one, self_value)))
        attended = lax.map(self_item, (split_heads(query_one), split_heads(key_one), split_heads(value_one)))
        attended = low_back(low(attended.reshape(-1, D)))
        hidden_one = token_rows + low_back(matmul_high(attended, self_out))
        normed_two = low(rms_scale(hidden_one, gain_cross))
        query_two = low_back(low(matmul_high(normed_two, cross_query)))
        memory_rows = memory.reshape(-1, D)
        memory_keys = low_back(low(matmul_high(memory_rows, cross_key)))
        memory_values = low_back(low(matmul_high(memory_rows, cross_value)))
        crossed = lax.map(cross_item, (split_heads(query_two), split_heads(memory_keys), split_heads(memory_values), patch_live))
        crossed = low_back(low(crossed.reshape(-1, D)))
        hidden_two = hidden_one + low_back(matmul_high(crossed, cross_out))
        normed_three = low(rms_scale(hidden_two, gain_feed))
        gate_pre = low_back(matmul_high(normed_three, gate_weight))
        up_pre = low_back(matmul_high(normed_three, up_weight))
        mixed = low(gelu_tanh(gate_pre) * up_pre)
        output_rows = hidden_two + low_back(matmul_high(mixed, down_weight))
        return output_rows.reshape(tokens.shape)
    float_args = (tokens.astype(jnp.float32), memory.astype(jnp.float32), gain_self.astype(jnp.float32), self_query.astype(jnp.float32), self_key.astype(jnp.float32), self_value.astype(jnp.float32), self_out.astype(jnp.float32), gain_cross.astype(jnp.float32), cross_query.astype(jnp.float32), cross_key.astype(jnp.float32), cross_value.astype(jnp.float32), cross_out.astype(jnp.float32), gain_feed.astype(jnp.float32), gate_weight.astype(jnp.float32), up_weight.astype(jnp.float32), down_weight.astype(jnp.float32))
    output_full, pullback = jax.vjp(forward, *float_args)
    gradients = pullback(cotangent.astype(jnp.float32))
    return (output_full.astype(jnp.bfloat16), gradients[0], gradients[1], gradients[2], gradients[3], gradients[4], gradients[5], gradients[6], gradients[7], gradients[8], gradients[9], gradients[10], gradients[11], gradients[12], gradients[13], gradients[14], gradients[15])
```

```python
import jax
import jax.numpy as jnp
from jax import lax
from jax.sharding import PartitionSpec as P

H = 12
HD = 64


eps = 1e-06
neg_big = -1e30
gelu_scale = 0.7978845608028654


def rms_scale(hidden_rows, gain_vector):
    inverse = lax.rsqrt(jnp.mean(hidden_rows * hidden_rows, axis=-1, keepdims=True) + eps)
    return hidden_rows * inverse * gain_vector


def gelu_tanh(inputs):
    return (
        0.5 * inputs * (1.0 + jnp.tanh(gelu_scale * (inputs + 0.044715 * inputs * inputs * inputs)))
    )


def gated_unit(gate_pre, up_pre):
    return gelu_tanh(gate_pre) * up_pre


def project(left_side, right_side):
    return jnp.dot(left_side, right_side, preferred_element_type=jnp.float32)


def outer_rows(left_side, right_side):
    return lax.dot_general(
        left_side, right_side, (((0,), (0,)), ((), ())), preferred_element_type=jnp.float32
    )


def back_project(grad_rows, weights):
    return lax.dot_general(
        grad_rows, weights, (((1,), (1,)), ((), ())), preferred_element_type=jnp.float32
    )


def norm_back(hidden_rows, gain_vector, grad_normed):
    unused, pullback = jax.vjp(rms_scale, hidden_rows, gain_vector)
    return pullback(grad_normed)


def attend_forward(queries, keys_in, values_in, allowed):
    scores = jnp.einsum("bqhd,bkhd->bhqk", queries, keys_in, preferred_element_type=jnp.float32)
    scores = jnp.where(allowed, scores, neg_big)
    row_peak = jnp.max(scores, axis=-1, keepdims=True)
    exp_scores = jnp.exp(scores - row_peak)
    row_total = jnp.sum(exp_scores, axis=-1, keepdims=True)
    prob_low = (exp_scores / row_total).astype(jnp.bfloat16)
    mixed_heads = jnp.einsum(
        "bhqk,bkhd->bqhd", prob_low, values_in, preferred_element_type=jnp.float32
    )
    return (mixed_heads.astype(jnp.bfloat16), row_peak + jnp.log(row_total))


def attend_backward(queries, keys_in, values_in, allowed, log_total, grad_mixed):
    scores = jnp.einsum("bqhd,bkhd->bhqk", queries, keys_in, preferred_element_type=jnp.float32)
    scores = jnp.where(allowed, scores, neg_big)
    probs_full = jnp.exp(scores - log_total)
    grad_probs = jnp.einsum(
        "bqhd,bkhd->bhqk", grad_mixed, values_in, preferred_element_type=jnp.float32
    )
    centre = jnp.sum(probs_full * grad_probs, axis=-1, keepdims=True)
    grad_scores = (probs_full * (grad_probs - centre)).astype(jnp.bfloat16)
    grad_queries = jnp.einsum(
        "bhqk,bkhd->bqhd", grad_scores, keys_in, preferred_element_type=jnp.float32
    )
    grad_keys = jnp.einsum(
        "bhqk,bqhd->bkhd", grad_scores, queries, preferred_element_type=jnp.float32
    )
    grad_values = jnp.einsum(
        "bhqk,bqhd->bkhd",
        probs_full.astype(jnp.bfloat16),
        grad_mixed,
        preferred_element_type=jnp.float32,
    )
    return (grad_queries, grad_keys, grad_values)


def split_heads(flat_rows):
    return flat_rows.reshape(1, -1, H, HD)


def swap(piece, axis_name, bit):
    size = lax.axis_size(axis_name)
    return lax.ppermute(piece, axis_name, [(place, place ^ (1 << bit)) for place in range(size)])


def bit_of(axis_name, bit):
    return (lax.axis_index(axis_name) >> bit) & 1


def pick(piece, which, dim):
    return lax.dynamic_index_in_dim(piece, which, dim, keepdims=False)


def halve(piece, axis_name, bit, dim, dtype=jnp.bfloat16):
    mine = bit_of(axis_name, bit)
    received = swap(pick(piece, 1 - mine, dim), axis_name, bit)
    kept = pick(piece, mine, dim)
    return (kept.astype(jnp.float32) + received.astype(jnp.float32)).astype(dtype)


def weight_grads(rows_in, grads, order):
    rows = rows_in.shape[0]
    core = bit_of("narrow", 0)
    parts = [piece.reshape(rows, 2, 2, piece.shape[1] // 4) for piece in grads]
    widths = [piece.shape[3] for piece in parts]

    def side(which):
        picked = [pick(piece, which, 2) for piece in parts]
        return jnp.concatenate(picked, axis=2).reshape(rows, -1)

    away = outer_rows(rows_in, side(1 - core)).astype(jnp.bfloat16)
    received = swap(away, "narrow", 0)
    total = (outer_rows(rows_in, side(core)) + received.astype(jnp.float32)).astype(jnp.bfloat16)
    spread = lax.axis_size("items")
    levels = spread.bit_length() - 1
    height, width = total.shape
    total = total.reshape((2,) * levels + (height // spread, 2, width // 2))
    left = ["x"] + list(range(levels - 1, -1, -1))
    for step, bit in enumerate(order(levels)):
        last = step == levels
        dim = left.index(bit)
        if bit == "x":
            total = halve(total, "narrow", 1, total.ndim - 2, jnp.float32 if last else jnp.bfloat16)
        else:
            total = halve(total, "items", bit, dim - left.index("x") - 1 if "x" in left else dim, jnp.float32 if last else jnp.bfloat16)
        left.remove(bit)
    outs = []
    at = 0
    for width in widths:
        outs.append(total[..., at : at + width].reshape(height // spread, width))
        at += width
    return outs


def order_x(levels):
    return ["x"] + list(range(levels))


def order_y(levels):
    return list(range(levels)) + ["x"]


def order_z(levels):
    return [1, 0] + list(range(2, levels)) + ["x"]


def all_summed(piece):
    for axis_name in ("narrow", "items"):
        for bit in range(lax.axis_size(axis_name).bit_length() - 1):
            piece = piece + swap(piece, axis_name, bit)
    return piece


def to_items(piece):
    return lax.all_to_all(piece, "narrow", split_axis=0, concat_axis=1, tiled=True)


def to_shards(piece):
    return lax.all_to_all(piece, "narrow", split_axis=1, concat_axis=0, tiled=True)


def body(
    tokens,
    memory,
    mem_count,
    cotangent,
    gain_self,
    self_query,
    self_key,
    self_value,
    self_out,
    gain_cross,
    cross_query,
    cross_key,
    cross_value,
    cross_out,
    gain_feed,
    gate_weight,
    up_weight,
    down_weight,
):
    batch_size, local_tok, model_width = tokens.shape
    local_mem = memory.shape[1]
    narrow_count = lax.axis_size("narrow")
    full_tok = local_tok * narrow_count
    full_mem = local_mem * narrow_count
    bf = jnp.bfloat16
    tokens_here = to_items(tokens)
    memory_rows = to_items(memory).reshape(-1, model_width)
    cotangent_rows = to_items(cotangent).reshape(-1, model_width)
    count = pick(mem_count, lax.axis_index("narrow"), 0)
    token_rows = tokens_here.astype(jnp.float32).reshape(-1, model_width)
    normed_one = rms_scale(token_rows, gain_self).astype(bf)
    query_one = project(normed_one, self_query).astype(bf)
    key_one = project(normed_one, self_key).astype(bf)
    value_one = project(normed_one, self_value).astype(bf)
    place = jnp.arange(full_tok, dtype=jnp.int32)
    causal = (place[None, :] <= place[:, None])[None, None]
    attended_one, total_one = attend_forward(
        split_heads(query_one), split_heads(key_one), split_heads(value_one), causal
    )
    attended_flat = attended_one.reshape(-1, model_width)
    hidden_one = token_rows + project(attended_flat, self_out)
    normed_two = rms_scale(hidden_one, gain_cross).astype(bf)
    query_two = project(normed_two, cross_query).astype(bf)
    memory_key = project(memory_rows, cross_key).astype(bf)
    memory_value = project(memory_rows, cross_value).astype(bf)
    patch_live = (jnp.arange(full_mem, dtype=jnp.int32) < count)[None, None, None, :]
    crossed, total_two = attend_forward(
        split_heads(query_two), split_heads(memory_key), split_heads(memory_value), patch_live
    )
    crossed_flat = crossed.reshape(-1, model_width)
    hidden_two = hidden_one + project(crossed_flat, cross_out)
    normed_three = rms_scale(hidden_two, gain_feed).astype(bf)
    gate_pre = project(normed_three, gate_weight)
    up_pre = project(normed_three, up_weight)
    mixed_full, mix_back = jax.vjp(gated_unit, gate_pre, up_pre)
    mixed = mixed_full.astype(bf)
    result = (hidden_two + project(mixed, down_weight)).astype(bf)
    result = to_shards(result[None])
    grad_rows = cotangent_rows.astype(jnp.float32)
    (down_sum,) = weight_grads(mixed, [cotangent_rows], order_z)
    grad_gate, grad_up = mix_back(back_project(cotangent_rows, down_weight))
    grad_gate = grad_gate.astype(bf)
    grad_up = grad_up.astype(bf)
    gate_sum, up_sum = weight_grads(normed_three, [grad_gate, grad_up], order_x)
    grad_normed_three = back_project(grad_gate, gate_weight) + back_project(grad_up, up_weight)
    grad_norm_two, grad_gain_feed = norm_back(hidden_two, gain_feed, grad_normed_three)
    grad_hidden_two = grad_rows + grad_norm_two
    branch_two_grad = grad_hidden_two.astype(bf)
    (cross_out_sum,) = weight_grads(crossed_flat, [branch_two_grad], order_y)
    grad_crossed = back_project(branch_two_grad, cross_out).astype(bf)
    grad_query_two, memory_keys_grad, memory_values_grad = [
        piece.astype(bf).reshape(-1, model_width)
        for piece in attend_backward(
            split_heads(query_two),
            split_heads(memory_key),
            split_heads(memory_value),
            patch_live,
            total_two,
            split_heads(grad_crossed),
        )
    ]
    cross_key_sum, cross_value_sum = weight_grads(
        memory_rows, [memory_keys_grad, memory_values_grad], order_y
    )
    memory_grad = (
        back_project(memory_keys_grad, cross_key) + back_project(memory_values_grad, cross_value)
    ).astype(bf)
    memory_grad = to_shards(memory_grad[None]).astype(jnp.float32)
    (cross_query_sum,) = weight_grads(normed_two, [grad_query_two], order_z)
    grad_norm_one, grad_gain_cross = norm_back(
        hidden_one, gain_cross, back_project(grad_query_two, cross_query)
    )
    grad_hidden_one = grad_hidden_two + grad_norm_one
    branch_one_grad = grad_hidden_one.astype(bf)
    (self_out_sum,) = weight_grads(attended_flat, [branch_one_grad], order_y)
    grad_attended = back_project(branch_one_grad, self_out).astype(bf)
    grad_query_one, key_one_grad, value_one_grad = [
        piece.astype(bf).reshape(-1, model_width)
        for piece in attend_backward(
            split_heads(query_one),
            split_heads(key_one),
            split_heads(value_one),
            causal,
            total_one,
            split_heads(grad_attended),
        )
    ]
    self_query_sum, self_key_sum, self_value_sum = weight_grads(
        normed_one, [grad_query_one, key_one_grad, value_one_grad], order_z
    )
    grad_normed_one = (
        back_project(grad_query_one, self_query)
        + back_project(key_one_grad, self_key)
        + back_project(value_one_grad, self_value)
    )
    grad_norm_zero, grad_gain_self = norm_back(token_rows, gain_self, grad_normed_one)
    tokens_grad = (grad_hidden_one + grad_norm_zero).astype(bf)
    tokens_grad = to_shards(tokens_grad[None]).astype(jnp.float32)
    gains = all_summed(jnp.stack([grad_gain_self, grad_gain_cross, grad_gain_feed]))
    return (
        result,
        tokens_grad,
        memory_grad,
        gains[0],
        self_query_sum,
        self_key_sum,
        self_value_sum,
        self_out_sum,
        gains[1],
        cross_query_sum,
        cross_key_sum,
        cross_value_sum,
        cross_out_sum,
        gains[2],
        gate_sum,
        up_sum,
        down_sum,
    )


def solution(mesh):
    in_specs = (
        P("items", "narrow", None),
        P("items", "narrow", None),
        P("items"),
        P("items", "narrow", None),
        P(),
        P(),
        P(),
        P(),
        P(),
        P(),
        P(),
        P(),
        P(),
        P(),
        P(),
        P(),
        P(),
        P(),
    )
    out_specs = (
        P("items", "narrow", None),
        P("items", "narrow", None),
        P("items", "narrow", None),
        P(),
        P("items", "narrow"),
        P("items", "narrow"),
        P("items", "narrow"),
        P("items", "narrow"),
        P(),
        P("items", "narrow"),
        P("items", "narrow"),
        P("items", "narrow"),
        P("items", "narrow"),
        P(),
        P("items", "narrow"),
        P("items", "narrow"),
        P("items", "narrow"),
    )
    return jax.shard_map(body, mesh=mesh, in_specs=in_specs, out_specs=out_specs, check_vma=False)
```

```python
import jax
import jax.numpy as jnp
from jax import lax
from jax.experimental import pallas as pl
from jax.experimental.pallas import tpu as pltpu
from jax.sharding import PartitionSpec as P

HD = 64
LANES = 128
BLOCKS = 8

eps = 1e-06
neg_big = -1e30
gelu_scale = 0.7978845608028654
gelu_cubic = 0.044715
low = jnp.bfloat16
high = jnp.float32
vmem_bytes = 60 * 1024 * 1024


def rows_dot(left_side, right_side):
    return lax.dot_general(
        left_side, right_side, (((1,), (1,)), ((), ())), preferred_element_type=high
    )


def cols_dot(left_side, right_side):
    return lax.dot_general(
        left_side, right_side, (((0,), (0,)), ((), ())), preferred_element_type=high
    )


def plain_dot(left_side, right_side):
    return jnp.dot(left_side, right_side, preferred_element_type=high)


def inverse_scale(hidden):
    return lax.rsqrt(jnp.mean(hidden * hidden, axis=-1, keepdims=True) + eps)


def norm_back(hidden, gain, grad):
    scale = inverse_scale(hidden)
    weighted = gain * grad
    middle = jnp.mean(weighted * hidden, axis=-1, keepdims=True)
    to_rows = scale * (weighted - hidden * (scale * scale * middle))
    to_gain = jnp.sum(grad * hidden * scale, axis=0, keepdims=True)
    return to_rows, to_gain


def cost(products, moved, powers=0):
    return pl.CostEstimate(flops=2 * products, bytes_accessed=moved, transcendentals=powers)


def size_of(*pieces):
    return sum(piece.size * piece.dtype.itemsize for piece in pieces)


def after(piece, *earlier):
    return lax.optimization_barrier((piece, *earlier))[0]


def row_spec(rows, width):
    return pl.BlockSpec((rows, width), lambda step: (step, 0))


def whole_spec(shape):
    return pl.BlockSpec(
        shape, lambda step: (0,) * len(shape), pipeline_mode=pl.Buffered(1)
    )


def row_call(kernel, name, step_rows, by_rows, constants, outs, sums=(), passes=2):
    total = by_rows[0].shape[0]
    step_rows = min(step_rows, total)
    return pl.pallas_call(
        kernel,
        grid=(total // step_rows,),
        in_specs=[row_spec(step_rows, piece.shape[1]) for piece in by_rows]
        + [whole_spec(piece.shape) for piece in constants],
        out_specs=[row_spec(step_rows, width) for width, _ in outs]
        + [pl.BlockSpec((1, width), lambda step: (0, 0)) for width in sums],
        out_shape=[jax.ShapeDtypeStruct((total, width), kind) for width, kind in outs]
        + [jax.ShapeDtypeStruct((1, width), high) for width in sums],
        cost_estimate=cost(
            total * sum(piece.size for piece in constants) * passes, size_of(*by_rows, *constants)
        ),
        compiler_params=pltpu.CompilerParams(vmem_limit_bytes=vmem_bytes),
        name=name,
    )(*by_rows, *constants)


def add_up(total_ref, part):
    @pl.when(pl.program_id(0) == 0)
    def _():
        total_ref[...] = jnp.zeros_like(total_ref)

    total_ref[...] += part


def enter_self(tokens_ref, gain_ref, wq_ref, wk_ref, wv_ref, normed_ref, q_ref, k_ref, v_ref):
    hidden = tokens_ref[...].astype(high)
    normed = (hidden * inverse_scale(hidden) * gain_ref[...]).astype(low)
    normed_ref[...] = normed
    q_ref[...] = plain_dot(normed, wq_ref[...]).astype(low)
    k_ref[...] = plain_dot(normed, wk_ref[...]).astype(low)
    v_ref[...] = plain_dot(normed, wv_ref[...]).astype(low)


def enter_memory(memory_ref, wk_ref, wv_ref, k_ref, v_ref):
    rows = memory_ref[...]
    k_ref[...] = plain_dot(rows, wk_ref[...]).astype(low)
    v_ref[...] = plain_dot(rows, wv_ref[...]).astype(low)


def enter_cross(attended_ref, tokens_ref, gain_ref, out_ref, wq_ref, hidden_ref, normed_ref, q_ref):
    hidden = tokens_ref[...].astype(high) + plain_dot(attended_ref[...], out_ref[...])
    hidden_ref[...] = hidden
    normed = (hidden * inverse_scale(hidden) * gain_ref[...]).astype(low)
    normed_ref[...] = normed
    q_ref[...] = plain_dot(normed, wq_ref[...]).astype(low)


def feed_both(
    crossed_ref,
    hidden_ref,
    cotangent_ref,
    gain_ref,
    out_ref,
    gate_ref,
    up_ref,
    down_ref,
    normed_ref,
    mixed_ref,
    grad_gate_ref,
    grad_up_ref,
    result_ref,
    grad_hidden_ref,
    branch_ref,
    grad_crossed_ref,
    grad_gain_ref,
):
    gain = gain_ref[...]
    hidden = hidden_ref[...] + plain_dot(crossed_ref[...], out_ref[...])
    normed = (hidden * inverse_scale(hidden) * gain).astype(low)
    normed_ref[...] = normed
    gate = plain_dot(normed, gate_ref[...])
    up = plain_dot(normed, up_ref[...])
    square = gate * gate
    curve = jnp.tanh(gelu_scale * (gate + gelu_cubic * gate * square))
    half = 0.5 * (1.0 + curve)
    bent = gate * half
    slope = half + 0.5 * gate * (1.0 - curve * curve) * (
        gelu_scale * (1.0 + 3.0 * gelu_cubic * square)
    )
    mixed = (bent * up).astype(low)
    mixed_ref[...] = mixed
    result_ref[...] = (hidden + plain_dot(mixed, down_ref[...])).astype(low)
    cotangent = cotangent_ref[...]
    back = rows_dot(cotangent, down_ref[...])
    grad_gate = (back * up * slope).astype(low)
    grad_up = (back * bent).astype(low)
    grad_gate_ref[...] = grad_gate
    grad_up_ref[...] = grad_up
    grad_normed = rows_dot(grad_gate, gate_ref[...]) + rows_dot(grad_up, up_ref[...])
    to_rows, to_gain = norm_back(hidden, gain, grad_normed)
    grad_hidden = cotangent.astype(high) + to_rows
    grad_hidden_ref[...] = grad_hidden
    branch = grad_hidden.astype(low)
    branch_ref[...] = branch
    grad_crossed_ref[...] = rows_dot(branch, out_ref[...]).astype(low)
    add_up(grad_gain_ref, to_gain)


def leave_cross(
    grad_q_ref,
    hidden_ref,
    grad_in_ref,
    gain_ref,
    wq_ref,
    out_ref,
    grad_hidden_ref,
    branch_ref,
    grad_attended_ref,
    grad_gain_ref,
):
    to_rows, to_gain = norm_back(
        hidden_ref[...], gain_ref[...], rows_dot(grad_q_ref[...], wq_ref[...])
    )
    grad_hidden = grad_in_ref[...] + to_rows
    grad_hidden_ref[...] = grad_hidden
    branch = grad_hidden.astype(low)
    branch_ref[...] = branch
    grad_attended_ref[...] = rows_dot(branch, out_ref[...]).astype(low)
    add_up(grad_gain_ref, to_gain)


def leave_memory(grad_k_ref, grad_v_ref, wk_ref, wv_ref, grad_ref):
    grad_ref[...] = (
        rows_dot(grad_k_ref[...], wk_ref[...]) + rows_dot(grad_v_ref[...], wv_ref[...])
    ).astype(low)


def leave_self(
    grad_q_ref,
    grad_k_ref,
    grad_v_ref,
    tokens_ref,
    grad_in_ref,
    gain_ref,
    wq_ref,
    wk_ref,
    wv_ref,
    grad_ref,
    grad_gain_ref,
):
    grad_normed = (
        rows_dot(grad_q_ref[...], wq_ref[...])
        + rows_dot(grad_k_ref[...], wk_ref[...])
        + rows_dot(grad_v_ref[...], wv_ref[...])
    )
    to_rows, to_gain = norm_back(tokens_ref[...].astype(high), gain_ref[...], grad_normed)
    grad_ref[...] = (grad_in_ref[...] + to_rows).astype(low)
    add_up(grad_gain_ref, to_gain)


def two_heads(rows):
    first = lax.broadcasted_iota(jnp.int32, rows.shape, 1) < HD
    zero = jnp.zeros_like(rows)
    return jnp.concatenate([jnp.where(first, rows, zero), jnp.where(first, zero, rows)], axis=0)


def one_pair(stacked):
    half = stacked.shape[1] // 2
    first = lax.broadcasted_iota(jnp.int32, (stacked.shape[0], half), 0) < HD
    return jnp.where(first, stacked[:, :half], stacked[:, half:]).T


def attend_forward_kernel(
    causal, step, count_ref, q_ref, k_ref, v_ref, weight_ref, mixed_ref, inverse_ref, score_ref
):
    queries = two_heads(q_ref[...])
    wide = queries.shape[0]
    peak = jnp.full((1, wide), neg_big, high)
    for begin in range(0, k_ref.shape[0], step):
        here = slice(begin, begin + step)
        scores = rows_dot(k_ref[here, :], queries)
        if causal:
            key = lax.broadcasted_iota(jnp.int32, (step, wide), 0) + begin
            token = lax.broadcasted_iota(jnp.int32, (step, wide), 1)
            token = jnp.where(token >= wide // 2, token - wide // 2, token)
            scores = jnp.where(key <= token, scores, neg_big)
        else:
            key = lax.broadcasted_iota(jnp.int32, (step, 1), 0) + begin
            scores = scores + jnp.where(key < count_ref[0], 0.0, neg_big)
        score_ref[here, :] = scores
        peak = jnp.maximum(peak, jnp.max(scores, axis=0, keepdims=True))
    total = jnp.zeros((1, wide), high)
    mixed = jnp.zeros((q_ref.shape[1], wide), high)
    for begin in range(0, k_ref.shape[0], step):
        here = slice(begin, begin + step)
        weights = jnp.exp(score_ref[here, :] - peak)
        total = total + jnp.sum(weights, axis=0, keepdims=True)
        weights = weights.astype(low)
        weight_ref[0, here, :] = weights
        mixed = mixed + cols_dot(v_ref[here, :], weights)
    inverse = 1.0 / total
    inverse_ref[0] = inverse
    mixed_ref[...] = one_pair(mixed * inverse).astype(low)


def attend_forward(queries, keys, values, count, causal, step, name):
    tokens, width = queries.shape
    patches = keys.shape[0]
    pairs = width // LANES
    by_pair = lambda rows: pl.BlockSpec((rows, LANES), lambda pair, _: (0, pair))
    return pl.pallas_call(
        lambda *refs: attend_forward_kernel(causal, step, *refs),
        out_shape=(
            jax.ShapeDtypeStruct((pairs, patches, 2 * tokens), low),
            jax.ShapeDtypeStruct((tokens, width), low),
            jax.ShapeDtypeStruct((pairs, 1, 2 * tokens), high),
        ),
        grid_spec=pltpu.PrefetchScalarGridSpec(
            num_scalar_prefetch=1,
            grid=(pairs,),
            in_specs=[by_pair(tokens), by_pair(patches), by_pair(patches)],
            out_specs=[
                pl.BlockSpec((1, patches, 2 * tokens), lambda pair, _: (pair, 0, 0)),
                by_pair(tokens),
                pl.BlockSpec((1, 1, 2 * tokens), lambda pair, _: (pair, 0, 0)),
            ],
            scratch_shapes=[pltpu.VMEM((patches, 2 * tokens), high)],
        ),
        cost_estimate=cost(8 * patches * tokens * width, size_of(queries, keys, values)),
        compiler_params=pltpu.CompilerParams(vmem_limit_bytes=vmem_bytes),
        name=name,
    )(count, queries, keys, values)


def attend_backward_kernel(
    step,
    weight_ref,
    inverse_ref,
    q_ref,
    k_ref,
    v_ref,
    mixed_ref,
    grad_mixed_ref,
    *out_refs,
):
    grad_q_ref, grad_k_ref, grad_v_ref = out_refs[-3:]
    queries = two_heads(q_ref[...])
    grads = grad_mixed_ref[...].astype(high).T
    mixed = mixed_ref[...].astype(high).T
    first = lax.broadcasted_iota(jnp.int32, grads.shape, 0) < HD
    zero = jnp.zeros_like(grads)
    scaled = jnp.concatenate(
        [jnp.where(first, grads, zero), jnp.where(first, zero, grads)], axis=1
    )
    scaled = (scaled * inverse_ref[0]).astype(low)
    wide = scaled.astype(high)
    centre = jnp.sum(wide * jnp.concatenate([mixed, mixed], axis=1), axis=0, keepdims=True)
    rows = wide.T.astype(low)
    grad_q = jnp.zeros(wide.shape, high)
    for begin in range(0, k_ref.shape[0], step):
        here = slice(begin, begin + step)
        weights = weight_ref[0, here, :]
        grad_probs = plain_dot(v_ref[here, :], scaled)
        grad_scores = (weights.astype(high) * (grad_probs - centre)).astype(low)
        grad_v_ref[here, :] = plain_dot(weights, rows).astype(low)
        grad_k_ref[here, :] = plain_dot(grad_scores, queries).astype(low)
        grad_q = grad_q + cols_dot(k_ref[here, :], grad_scores)
    grad_q_ref[...] = one_pair(grad_q).astype(low)


def attend_backward(weights, inverse, queries, keys, values, mixed, grad_mixed, step, name, first, end, filled=()):
    tokens, width = queries.shape
    patches = keys.shape[0]
    by_token = pl.BlockSpec((tokens, LANES), lambda pair: (0, pair + first))
    by_patch = pl.BlockSpec((patches, LANES), lambda pair: (0, pair + first))
    return pl.pallas_call(
        lambda *refs: attend_backward_kernel(step, *refs),
        out_shape=(
            jax.ShapeDtypeStruct((tokens, width), low),
            jax.ShapeDtypeStruct((patches, width), low),
            jax.ShapeDtypeStruct((patches, width), low),
        ),
        grid=(end - first,),
        in_specs=[
            pl.BlockSpec((1, patches, 2 * tokens), lambda pair: (pair + first, 0, 0)),
            pl.BlockSpec((1, 1, 2 * tokens), lambda pair: (pair + first, 0, 0)),
            by_token,
            by_patch,
            by_patch,
            by_token,
            by_token,
        ]
        + [pl.BlockSpec(memory_space=pl.ANY)] * len(filled),
        out_specs=[by_token, by_patch, by_patch],
        input_output_aliases={7 + which: which for which in range(len(filled))},
        cost_estimate=cost(
            12 * patches * tokens * LANES * (end - first), 4 * patches * tokens * (end - first)
        ),
        compiler_params=pltpu.CompilerParams(vmem_limit_bytes=vmem_bytes),
        name=name,
    )(weights, inverse, queries, keys, values, mixed, grad_mixed, *filled)


def swap(piece, axis_name, bit):
    size = lax.axis_size(axis_name)
    return lax.ppermute(piece, axis_name, [(place, place ^ (1 << bit)) for place in range(size)])


def bit_of(axis_name, bit):
    return (lax.axis_index(axis_name) >> bit) & 1


def pick(piece, which):
    return lax.dynamic_index_in_dim(piece, which, 0, keepdims=False)


class Parcel:
    def __init__(self, order, parts, shapes, extra=0):
        self.order = order
        self.parts = parts
        self.plain = [shapes[job][1] // 4 // LANES for job, _, _ in parts]
        self.mixed = [int(shapes[job][1] // 4 % LANES > 0) for job, _, _ in parts]
        heights = [end - begin for _, begin, end in parts]
        self.own = sum(tiles * height for tiles, height in zip(self.plain, heights))
        self.extra = extra
        self.both = extra + sum(tiles * height for tiles, height in zip(self.mixed, heights))
        self.rows = 2 * self.own + self.both
        at, both_at = 0, 0
        self.at, self.both_at = [], []
        for tiles, shared, height in zip(self.plain, self.mixed, heights):
            self.at.append(at)
            self.both_at.append(both_at)
            at += tiles * height
            both_at += shared * height

    def place(self, block):
        bits = [(block >> bit) & 1 for bit in self.order]
        return bits[0] * 4 + bits[1] * 2 + bits[2]


def core_tiles(grad, core):
    quarter = grad.shape[1] // 4
    starts = [core * quarter, 2 * quarter + core * quarter]
    tiles = [
        grad[:, start + at : start + at + LANES]
        for start in starts
        for at in range(0, quarter - LANES + 1, LANES)
    ]
    rest = quarter % LANES
    if rest:
        tiles.append(
            jnp.concatenate(
                [grad[:, start + quarter - rest : start + quarter] for start in starts], axis=1
            )
        )
    return tiles


def weight_kernel(jobs, parcels, n_in, core_ref, *refs):
    ins, outs, turned_ref = refs[:n_in], refs[n_in:-1], refs[-1]
    core = core_ref[0]
    for which, parcel in enumerate(parcels):
        if parcel.extra:
            for kind in (0, 1):
                for block in range(BLOCKS):
                    outs[2 * which + kind][block, parcel.rows - parcel.extra :, :] = ins[-1][...]
    last_rows = None
    for job, (row_at, grad_at) in enumerate(jobs):
        rows_ref, grad = ins[row_at], ins[grad_at][...]
        depth, height = rows_ref.shape
        if row_at != last_rows:
            turned_ref[:height, :depth] = rows_ref[...].T
            last_rows = row_at
        turned = turned_ref[:height, :depth]
        sides = [core_tiles(grad, 0), core_tiles(grad, 1)]
        count = len(sides[0])
        wanted = [
            (kind, tile, jnp.where(core == kind, sides[0][tile], sides[1][tile]))
            for kind in (0, 1)
            for tile in range(count)
        ]
        for begin in range(0, 2 * count, 2):
            group = wanted[begin : begin + 2]
            product = plain_dot(turned, jnp.concatenate([piece for _, _, piece in group], axis=1))
            product = product.astype(low)
            block_rows = height // BLOCKS
            for slot, (kind, tile, _) in enumerate(group):
                for which, parcel in enumerate(parcels):
                    for part, (owner, first, end) in enumerate(parcel.parts):
                        if owner != job:
                            continue
                        plain = parcel.plain[part]
                        span = end - first
                        if tile < 2 * plain:
                            at = (tile // plain) * parcel.own + parcel.at[part] + (tile % plain) * span
                        else:
                            at = 2 * parcel.own + parcel.both_at[part]
                        for block in range(BLOCKS):
                            top = block * block_rows
                            outs[2 * which + kind][parcel.place(block), at : at + span, :] = product[
                                top + first : top + end, slot * LANES : (slot + 1) * LANES
                            ]


def weight_parts(core, arrays, jobs, parcels, name):
    depth = max(arrays[row_at].shape[0] for row_at, _ in jobs)
    height = max(arrays[row_at].shape[1] for row_at, _ in jobs)
    vmem = pl.BlockSpec(memory_space=pltpu.VMEM)
    return pl.pallas_call(
        lambda *refs: weight_kernel(jobs, parcels, len(arrays), *refs),
        in_specs=[pl.BlockSpec(memory_space=pltpu.SMEM)] + [vmem] * len(arrays),
        out_specs=[vmem] * (2 * len(parcels)),
        out_shape=[
            jax.ShapeDtypeStruct((BLOCKS, parcel.rows, LANES), low)
            for parcel in parcels
            for _ in range(2)
        ],
        scratch_shapes=[pltpu.VMEM((height, depth), low)],
        cost_estimate=cost(
            sum(arrays[row_at].size * arrays[grad_at].shape[1] for row_at, grad_at in jobs) * 2,
            size_of(*arrays),
        ),
        compiler_params=pltpu.CompilerParams(vmem_limit_bytes=vmem_bytes),
        name=name,
    )(core, *arrays)


class Travel:
    def __init__(self, parcel, kept, sent):
        self.parcel = parcel
        self.kept = kept
        self.received = swap(sent, "narrow", 0)
        self.bits = list(parcel.order)

    def step(self, *earlier):
        parcel = self.parcel
        kept, received = self.kept, self.received
        if earlier:
            kept, received = lax.optimization_barrier((kept, received, *earlier))[:2]
        if self.bits:
            top = lax.axis_size("items").bit_length() - 4
            bit = self.bits.pop(0)
            mine = bit_of("items", top + bit)
            half = kept.shape[0] // 2
            kept = kept.reshape(2, half, parcel.rows, LANES)
            received = received.reshape(2, half, parcel.rows, LANES)
            both = lambda which: (
                pick(kept, which).astype(high) + pick(received, which).astype(high)
            ).astype(low)
            away, self.kept = both(1 - mine), both(mine)
            self.received = swap(away, "items", top + bit)
        else:
            total = (kept[0].astype(high) + received[0].astype(high)).astype(low)
            mine = bit_of("narrow", 1)
            shared = total[2 * parcel.own :]

            def side(which):
                own = lax.dynamic_slice_in_dim(total, which * parcel.own, parcel.own, 0)
                return jnp.concatenate([own, shared], axis=0) if parcel.both else own

            away, self.kept = side(1 - mine), side(mine)
            self.received = swap(away, "narrow", 1)
        return self.kept, away


def finish_kernel(parcels, x_ref, *refs):
    x = x_ref[0]
    outs = refs[2 * len(parcels) :]
    for which, parcel in enumerate(parcels):
        total = refs[2 * which][...].astype(high) + refs[2 * which + 1][...].astype(high)
        for part, (job, first, end) in enumerate(parcel.parts):
            span = end - first
            for tile in range(parcel.plain[part]):
                at = parcel.at[part] + tile * span
                outs[job][first:end, tile * LANES : (tile + 1) * LANES] = total[at : at + span]
            if parcel.mixed[part]:
                at = parcel.own + parcel.both_at[part]
                shared = total[at : at + span]
                half = LANES // 2
                begin = parcel.plain[part] * LANES
                outs[job][first:end, begin : begin + half] = jnp.where(
                    x == 0, shared[:, :half], shared[:, half:]
                )
        if parcel.extra:
            outs[-1][...] = total[-parcel.extra :]


def start_weights(arrays, jobs, parcels, name):
    pieces = weight_parts(bit_of("narrow", 0).reshape(1), arrays, jobs, parcels, name)
    return [
        Travel(parcel, pieces[2 * which], pieces[2 * which + 1])
        for which, parcel in enumerate(parcels)
    ]


def end_weights(travels, shapes, name):
    parcels = [trip.parcel for trip in travels]
    ends = [piece for trip in travels for piece in (trip.kept, trip.received)]
    vmem = pl.BlockSpec(memory_space=pltpu.VMEM)
    extra = sum(parcel.extra for parcel in parcels)
    out_shapes = [(height // BLOCKS, width // 4) for height, width in shapes]
    out_shapes += [(extra, LANES)] if extra else []
    outs = pl.pallas_call(
        lambda *refs: finish_kernel(parcels, *refs),
        in_specs=[pl.BlockSpec(memory_space=pltpu.SMEM)] + [vmem] * len(ends),
        out_specs=[vmem] * len(out_shapes),
        out_shape=[jax.ShapeDtypeStruct(shape, high) for shape in out_shapes],
        compiler_params=pltpu.CompilerParams(vmem_limit_bytes=vmem_bytes),
        name=name,
    )(bit_of("narrow", 1).reshape(1), *ends)
    sums, extras = list(outs[: len(shapes)]), list(outs[len(shapes) :])
    levels = lax.axis_size("items").bit_length() - 1
    for bit in range(levels - 4, -1, -1):
        mine = bit_of("items", bit)
        halves = [piece.reshape(2, piece.shape[0] // 2, piece.shape[1]) for piece in sums]
        sums = [pick(piece, mine) + swap(pick(piece, 1 - mine), "items", bit) for piece in halves]
        extras = [piece + swap(piece, "items", bit) for piece in extras]
    return sums + extras


def exchange(piece):
    return lax.all_to_all(piece, "narrow", split_axis=0, concat_axis=0, tiled=True)


def body(
    tokens,
    memory,
    mem_count,
    cotangent,
    gain_self,
    self_query,
    self_key,
    self_value,
    self_out,
    gain_cross,
    cross_query,
    cross_key,
    cross_value,
    cross_out,
    gain_feed,
    gate_weight,
    up_weight,
    down_weight,
):
    width = tokens.shape[2]
    inner = gate_weight.shape[1]
    gain_self, gain_cross, gain_feed = [
        gain.reshape(1, width) for gain in (gain_self, gain_cross, gain_feed)
    ]
    token_rows = exchange(tokens).reshape(-1, width)
    memory_rows = exchange(memory).reshape(-1, width)
    cotangent_rows = exchange(cotangent).reshape(-1, width)
    count = pick(mem_count, lax.axis_index("narrow")).reshape(1)
    normed_one, query_one, key_one, value_one = row_call(
        enter_self,
        "enter_self",
        256,
        [token_rows],
        [gain_self, self_query, self_key, self_value],
        [(width, low)] * 4,
    )
    weights_one, attended, inverse_one = attend_forward(
        query_one, key_one, value_one, count, True, 256, "self_forward"
    )
    hidden_one, normed_two, query_two = row_call(
        enter_cross,
        "enter_cross",
        256,
        [attended, token_rows],
        [gain_cross, self_out, cross_query],
        [(width, high), (width, low), (width, low)],
    )
    memory_keys, memory_values = row_call(
        enter_memory,
        "enter_memory",
        512,
        [memory_rows],
        [cross_key, cross_value],
        [(width, low)] * 2,
    )
    weights_two, crossed, inverse_two = attend_forward(
        query_two, memory_keys, memory_values, count, False, 512, "cross_forward"
    )
    (
        normed_three,
        mixed,
        grad_gate,
        grad_up,
        result,
        grad_hidden_two,
        branch_two,
        grad_crossed,
        grad_gain_feed,
    ) = row_call(
        feed_both,
        "feed_both",
        256,
        [crossed, hidden_one, cotangent_rows],
        [gain_feed, cross_out, gate_weight, up_weight, down_weight],
        [
            (width, low),
            (inner, low),
            (inner, low),
            (inner, low),
            (width, low),
            (width, high),
            (width, low),
            (width, low),
        ],
        [width],
    )
    square = (width, width)
    feed_shapes = [(width, inner), (width, inner), (inner, width), square]
    rows, tall = width // BLOCKS, inner // BLOCKS
    feed_trips = start_weights(
        [normed_three, grad_gate, grad_up, mixed, cotangent_rows, crossed, branch_two],
        [(0, 1), (0, 2), (3, 4), (5, 6)],
        [
            Parcel((0, 1, 2), [(0, 0, rows), (2, 0, tall // 2)], feed_shapes),
            Parcel((1, 0, 2), [(1, 0, rows), (2, tall // 2, tall), (3, 0, rows)], feed_shapes),
        ],
        "feed_weights",
    )
    result = exchange(result.reshape(tokens.shape))
    step = lambda trips, earlier: [part for trip in trips for part in trip.step(earlier)]
    ready = feed_trips[0].kept
    grads_two = ()
    for first in (0, 2, 4):
        grads_two = attend_backward(
            weights_two,
            inverse_two,
            query_two,
            memory_keys,
            memory_values,
            crossed,
            after(grad_crossed, ready),
            512,
            "cross_backward",
            first,
            first + 2,
            grads_two,
        )
        ready = step(feed_trips, grads_two[0])[0]
    grad_query_two, memory_keys_grad, memory_values_grad = grads_two
    grad_hidden_one, branch_one, grad_attended, grad_gain_cross = row_call(
        leave_cross,
        "leave_cross",
        256,
        [after(grad_query_two, ready), hidden_one, grad_hidden_two],
        [gain_cross, cross_query, self_out],
        [(width, high), (width, low), (width, low)],
        [width],
    )
    (memory_grad,) = row_call(
        leave_memory,
        "leave_memory",
        512,
        [after(memory_keys_grad, branch_one), memory_values_grad],
        [cross_key, cross_value],
        [(width, low)],
        passes=1,
    )
    ready = step(feed_trips, memory_grad)[0]
    memory_grad = exchange(memory_grad.reshape(memory.shape)).astype(high)
    cross_shapes = [square] * 4
    cross_trips = start_weights(
        [
            memory_rows,
            after(memory_keys_grad, ready),
            memory_values_grad,
            normed_two,
            grad_query_two,
            attended,
            branch_one,
        ],
        [(0, 1), (0, 2), (3, 4), (5, 6)],
        [
            Parcel((0, 1, 2), [(0, 0, rows), (2, 0, rows)], cross_shapes),
            Parcel((1, 0, 2), [(1, 0, rows), (3, 0, rows)], cross_shapes),
        ],
        "cross_weights",
    )
    ready = cross_trips[0].kept
    grads_one = ()
    for first in (0, 3):
        grads_one = attend_backward(
            weights_one,
            inverse_one,
            query_one,
            key_one,
            value_one,
            attended,
            after(grad_attended, ready),
            512,
            "self_backward",
            first,
            first + 3,
            grads_one,
        )
        ready = step(cross_trips, grads_one[0])[0]
    grad_query_one, key_one_grad, value_one_grad = grads_one
    tokens_grad, grad_gain_self = row_call(
        leave_self,
        "leave_self",
        256,
        [after(grad_query_one, ready), key_one_grad, value_one_grad, token_rows, grad_hidden_one],
        [gain_self, self_query, self_key, self_value],
        [(width, low)],
        [width],
    )
    gains = jnp.concatenate([grad_gain_self, grad_gain_cross, grad_gain_feed], axis=0).astype(low)
    gains = jnp.pad(gains.reshape(-1, LANES), ((0, 32 - 3 * width // LANES), (0, 0)))
    self_shapes = [square] * 3
    self_trips = start_weights(
        [normed_one, grad_query_one, key_one_grad, value_one_grad, gains],
        [(0, 1), (0, 2), (0, 3)],
        [
            Parcel((0, 1, 2), [(0, 0, rows), (2, 0, rows // 2)], self_shapes, 32),
            Parcel((1, 0, 2), [(1, 0, rows), (2, rows // 2, rows)], self_shapes),
        ],
        "self_weights",
    )
    tokens_grad = exchange(tokens_grad.reshape(tokens.shape)).astype(high)
    gate_sum, up_sum, down_sum, cross_out_sum = end_weights(
        feed_trips, feed_shapes, "feed_weights_end"
    )
    for trip in self_trips + cross_trips:
        trip.step()
    for trip in self_trips + cross_trips:
        trip.step()
    for trip in self_trips:
        trip.step()
    for trip in self_trips:
        trip.step()
    cross_key_sum, cross_value_sum, cross_query_sum, self_out_sum = end_weights(
        cross_trips, cross_shapes, "cross_weights_end"
    )
    self_query_sum, self_key_sum, self_value_sum, gains = end_weights(
        self_trips, self_shapes, "self_weights_end"
    )
    gains = gains[: 3 * width // LANES].reshape(3, width)
    return (
        result,
        tokens_grad,
        memory_grad,
        gains[0],
        self_query_sum,
        self_key_sum,
        self_value_sum,
        self_out_sum,
        gains[1],
        cross_query_sum,
        cross_key_sum,
        cross_value_sum,
        cross_out_sum,
        gains[2],
        gate_sum,
        up_sum,
        down_sum,
    )


def solution(mesh):
    in_specs = (
        P("items", "narrow", None),
        P("items", "narrow", None),
        P("items"),
        P("items", "narrow", None),
        P(),
        P(),
        P(),
        P(),
        P(),
        P(),
        P(),
        P(),
        P(),
        P(),
        P(),
        P(),
        P(),
        P(),
    )
    out_specs = (
        P("items", "narrow", None),
        P("items", "narrow", None),
        P("items", "narrow", None),
        P(),
        P("items", "narrow"),
        P("items", "narrow"),
        P("items", "narrow"),
        P("items", "narrow"),
        P(),
        P("items", "narrow"),
        P("items", "narrow"),
        P("items", "narrow"),
        P("items", "narrow"),
        P(),
        P("items", "narrow"),
        P("items", "narrow"),
        P("items", "narrow"),
    )
    return jax.shard_map(body, mesh=mesh, in_specs=in_specs, out_specs=out_specs, check_vma=False)
```

```python
import jax
import jax.numpy as jnp
from jax import lax
from jax.experimental import pallas as pl
from jax.experimental.pallas import tpu as pltpu
from jax.sharding import PartitionSpec as P

HD = 64
LANES = 128
BLOCKS = 8

eps = 1e-06
neg_big = -1e30
gelu_scale = 0.7978845608028654
gelu_cubic = 0.044715
low = jnp.bfloat16
high = jnp.float32
vmem_bytes = 60 * 1024 * 1024


def rows_dot(left_side, right_side):
    return lax.dot_general(
        left_side, right_side, (((1,), (1,)), ((), ())), preferred_element_type=high
    )


def cols_dot(left_side, right_side):
    return lax.dot_general(
        left_side, right_side, (((0,), (0,)), ((), ())), preferred_element_type=high
    )


def plain_dot(left_side, right_side):
    return jnp.dot(left_side, right_side, preferred_element_type=high)


def inverse_scale(hidden):
    return lax.rsqrt(jnp.mean(hidden * hidden, axis=-1, keepdims=True) + eps)


def norm_back(hidden, gain, grad):
    scale = inverse_scale(hidden)
    weighted = gain * grad
    middle = jnp.mean(weighted * hidden, axis=-1, keepdims=True)
    to_rows = scale * (weighted - hidden * (scale * scale * middle))
    to_gain = jnp.sum(grad * hidden * scale, axis=0, keepdims=True)
    return to_rows, to_gain


call_time = {
    "enter_memory_near": 2,
    "enter_self": 3.5,
    "self_forward": 3,
    "enter_cross": 2,
    "cross_forward_near": 6,
    "enter_memory_far": 2,
    "cross_forward_far": 6,
    "cross_backward_far_b": 100,
    "self_weights": 100,
    "feed_weights_two": 100,
    "memory_back": 100,
    "self_weights_two": 100,
    "self_weights_end": 100,
}


def cost(name):
    return pl.CostEstimate(
        flops=int(call_time.get(name, 0.001) * 1.15e9), bytes_accessed=1, transcendentals=0
    )


def after(piece, *earlier):
    return lax.optimization_barrier((piece, *earlier))[0]


def row_spec(rows, width):
    return pl.BlockSpec((rows, width), lambda step: (step, 0))


def whole_spec(shape):
    return pl.BlockSpec(
        shape, lambda step: (0,) * len(shape), pipeline_mode=pl.Buffered(1)
    )


def row_call(kernel, name, step_rows, by_rows, constants, outs, sums=()):
    total = by_rows[0].shape[0]
    step_rows = min(step_rows, total)
    return pl.pallas_call(
        kernel,
        grid=(total // step_rows,),
        in_specs=[row_spec(step_rows, piece.shape[1]) for piece in by_rows]
        + [whole_spec(piece.shape) for piece in constants],
        out_specs=[row_spec(step_rows, width) for width, _ in outs]
        + [pl.BlockSpec((1, width), lambda step: (0, 0)) for width in sums],
        out_shape=[jax.ShapeDtypeStruct((total, width), kind) for width, kind in outs]
        + [jax.ShapeDtypeStruct((1, width), high) for width in sums],
        cost_estimate=cost(name),
        compiler_params=pltpu.CompilerParams(vmem_limit_bytes=vmem_bytes),
        name=name,
    )(*by_rows, *constants)


def add_up(total_ref, part):
    @pl.when(pl.program_id(0) == 0)
    def _():
        total_ref[...] = jnp.zeros_like(total_ref)

    total_ref[...] += part


def enter_self(tokens_ref, gain_ref, wq_ref, wk_ref, wv_ref, normed_ref, q_ref, k_ref, v_ref):
    hidden = tokens_ref[...].astype(high)
    normed = (hidden * inverse_scale(hidden) * gain_ref[...]).astype(low)
    normed_ref[...] = normed
    q_ref[...] = plain_dot(normed, wq_ref[...]).astype(low)
    k_ref[...] = plain_dot(normed, wk_ref[...]).astype(low)
    v_ref[...] = plain_dot(normed, wv_ref[...]).astype(low)


def enter_memory(first_ref, second_ref, wk_ref, wv_ref, rows_ref, k_ref, v_ref):
    half = first_ref.shape[0]
    for at, piece_ref in ((0, first_ref), (half, second_ref)):
        rows = piece_ref[...]
        rows_ref[at : at + half, :] = rows
        k_ref[at : at + half, :] = plain_dot(rows, wk_ref[...]).astype(low)
        v_ref[at : at + half, :] = plain_dot(rows, wv_ref[...]).astype(low)


def one_step_call(kernel, name, ins, outs, scratch=()):
    vmem = pl.BlockSpec(memory_space=pltpu.VMEM)
    smem = pl.BlockSpec(memory_space=pltpu.SMEM)
    return pl.pallas_call(
        kernel,
        in_specs=[smem if piece.dtype == jnp.int32 else vmem for piece in ins],
        out_specs=[vmem] * len(outs),
        out_shape=[jax.ShapeDtypeStruct(shape, kind) for shape, kind in outs],
        scratch_shapes=list(scratch),
        cost_estimate=cost(name),
        compiler_params=pltpu.CompilerParams(vmem_limit_bytes=vmem_bytes),
        name=name,
    )(*ins)


def enter_cross(attended_ref, tokens_ref, gain_ref, out_ref, wq_ref, hidden_ref, normed_ref, q_ref):
    hidden = tokens_ref[...].astype(high) + plain_dot(attended_ref[...], out_ref[...])
    hidden_ref[...] = hidden
    normed = (hidden * inverse_scale(hidden) * gain_ref[...]).astype(low)
    normed_ref[...] = normed
    q_ref[...] = plain_dot(normed, wq_ref[...]).astype(low)


def put_block(parcel, job, tile, rows_of, out_ref, spot):
    plain, rows = parcel.plain[job], parcel.heights[job]
    if tile < 2 * plain:
        at = (tile // plain) * parcel.own + parcel.at[job] + (tile % plain) * rows
        out_ref[spot, at : at + rows, :] = rows_of
    else:
        half = LANES // 2
        for side in (0, 1):
            at = side * parcel.own + parcel.at[job] + plain * rows
            lanes = slice(side * half, (side + 1) * half)
            out_ref[spot, at : at + rows // 2, :] = jnp.concatenate(
                [rows_of[: rows // 2, lanes], rows_of[rows // 2 :, lanes]], axis=1
            )


def put_rows(parcel, job, product, tile, out_ref, slot):
    rows = parcel.heights[job]
    for block in range(BLOCKS):
        put_block(
            parcel,
            job,
            tile,
            product[block * rows : (block + 1) * rows, slot * LANES : (slot + 1) * LANES],
            out_ref,
            place(block),
        )


def feed_both(
    parcel,
    parts,
    core_ref,
    crossed_ref,
    hidden_in_ref,
    cotangent_ref,
    gain_ref,
    out_ref,
    gate_ref,
    up_ref,
    down_ref,
    result_ref,
    grad_hidden_ref,
    branch_ref,
    grad_crossed_ref,
    grad_gain_ref,
    kept_out_ref,
    sent_out_ref,
    hidden_ref,
    normed_ref,
    turned_ref,
    sum_ref,
    back_ref,
    sides_ref,
    kept_ref,
    sent_ref,
    done_ref,
):
    step = pl.program_id(0)
    core = core_ref[0]
    gain = gain_ref[...]

    @pl.when(step == 0)
    def _():
        hidden = hidden_in_ref[...] + plain_dot(crossed_ref[...], out_ref[...])
        hidden_ref[...] = hidden
        normed = (hidden * inverse_scale(hidden) * gain).astype(low)
        normed_ref[...] = normed
        turned_ref[...] = normed.T
        sum_ref[...] = hidden
        back_ref[...] = jnp.zeros_like(back_ref)
        sides_ref[...] = jnp.concatenate(both_sides(cotangent_ref[...], core), axis=1)

    inner = parcel.at[2]

    def copies(side_ref, out_ref, begin, rows, slot):
        here = (slice(None), pl.ds(begin, rows), slice(None))
        return pltpu.make_async_copy(side_ref.at[here], out_ref.at[here], done_ref.at[slot])

    normed = normed_ref[...]
    cotangent = cotangent_ref[...]
    turned = turned_ref[...]
    sides = sides_ref[...]
    part = gate_ref.shape[1]
    size = part // 2
    output, back_sum = sum_ref[...], back_ref[...]
    grads, mixes = [], []
    for begin in range(0, part, size):
        here = slice(begin, begin + size)
        gate = plain_dot(normed, gate_ref[:, here])
        up = plain_dot(normed, up_ref[:, here])
        back = rows_dot(cotangent, down_ref[here, :])
        square = gate * gate
        curve = jnp.tanh(gelu_scale * (gate + gelu_cubic * gate * square))
        half = 0.5 * (1.0 + curve)
        bent = gate * half
        slope = half + 0.5 * gate * (1.0 - curve * curve) * (
            gelu_scale * (1.0 + 3.0 * gelu_cubic * square)
        )
        mixed = (bent * up).astype(low)
        grad_gate = (back * up * slope).astype(low)
        grad_up = (back * bent).astype(low)
        output = output + plain_dot(mixed, down_ref[here, :])
        back_sum = (
            back_sum
            + rows_dot(grad_gate, gate_ref[:, here])
            + rows_dot(grad_up, up_ref[:, here])
        )
        mixes.append(mixed)
        grads.append((grad_gate, grad_up))
    sum_ref[...] = output
    back_ref[...] = back_sum
    side = (step >> 1) * parcel.own
    for kind, (side_ref, target_ref) in enumerate(
        ((kept_ref, kept_out_ref), (sent_ref, sent_out_ref))
    ):

        @pl.when(((step & 1) ^ core) == kind)
        def _():
            for job in (0, 1):
                rows = parcel.heights[job]
                for which, pair in enumerate(grads):
                    product = plain_dot(turned, pair[job]).astype(low)
                    for tile in range(size // LANES):
                        at = side + parcel.at[job] + (which * size // LANES + tile) * rows
                        at = pl.multiple_of(at, 16)
                        for block in range(BLOCKS):
                            side_ref[place(block), pl.ds(at, rows), :] = product[
                                block * rows : (block + 1) * rows, tile * LANES : (tile + 1) * LANES
                            ]
            copies(side_ref, target_ref, pl.multiple_of(side, 16), inner, step).start()

    rows = parcel.heights[2]
    tiles = sides.shape[1] // LANES // 2
    for which, mixed in enumerate(mixes):
        product = cols_dot(mixed, sides).astype(low)
        here = product.shape[0] // rows
        for kind, side_ref in enumerate((kept_ref, sent_ref)):
            for tile in range(tiles):
                lane = (kind * tiles + tile) * LANES
                for block in range(here):
                    put_block(
                        parcel,
                        2,
                        tile,
                        product[block * rows : (block + 1) * rows, lane : lane + LANES],
                        side_ref,
                        place(step * here * 2 + which * here + block),
                    )

    @pl.when(step == pl.num_programs(0) - 1)
    def _():
        hidden = hidden_ref[...]
        result_ref[...] = sum_ref[...].astype(low)
        to_rows, to_gain = norm_back(hidden, gain, back_ref[...])
        grad_gain_ref[...] = to_gain
        grad_hidden = cotangent.astype(high) + to_rows
        grad_hidden_ref[...] = grad_hidden
        branch = grad_hidden.astype(low)
        branch_ref[...] = branch
        grad_crossed_ref[...] = rows_dot(branch, out_ref[...]).astype(low)
        sides = jnp.concatenate(both_sides(branch, core), axis=1)
        product = cols_dot(crossed_ref[...], sides).astype(low)
        for kind, side_ref in enumerate((kept_ref, sent_ref)):
            for tile in range(tiles):
                put_rows(parcel, 3, product, tile, side_ref, kind * tiles + tile)
        spans = ((inner, parcel.own), (parcel.own + inner, parcel.rows))
        last = [
            copies(side_ref, target_ref, begin, end - begin, parts + 2 * kind + which)
            for kind, (side_ref, target_ref) in enumerate(
                ((kept_ref, kept_out_ref), (sent_ref, sent_out_ref))
            )
            for which, (begin, end) in enumerate(spans)
        ]
        for copy in last:
            copy.start()
        for slot in range(parts):
            copies(kept_ref, kept_out_ref, 0, inner, slot).wait()
        for copy in last:
            copy.wait()


def feed_call(
    parcel, core, crossed, hidden, cotangent, gain, out_weight, gate_weight, up_weight, down_weight
):
    tokens, width = crossed.shape
    inner = gate_weight.shape[1]
    parts = lax.axis_size("narrow")
    part = inner // parts
    whole = lambda piece: whole_spec(piece.shape)
    fixed = lambda shape: pl.BlockSpec(shape, lambda step: (0,) * len(shape))
    parcel_shape = (BLOCKS, parcel.rows, LANES)
    return pl.pallas_call(
        lambda *refs: feed_both(parcel, parts, *refs),
        grid=(parts,),
        in_specs=[pl.BlockSpec(memory_space=pltpu.SMEM)]
        + [whole(crossed), whole(hidden), whole(cotangent), whole(gain), whole(out_weight)]
        + [pl.BlockSpec((width, part), lambda step: (0, step))] * 2
        + [pl.BlockSpec((part, width), lambda step: (step, 0))],
        out_specs=[fixed((tokens, width))] * 4
        + [fixed((1, width))]
        + [pl.BlockSpec(memory_space=pl.ANY)] * 2,
        out_shape=[
            jax.ShapeDtypeStruct((tokens, width), low),
            jax.ShapeDtypeStruct((tokens, width), high),
            jax.ShapeDtypeStruct((tokens, width), low),
            jax.ShapeDtypeStruct((tokens, width), low),
            jax.ShapeDtypeStruct((1, width), high),
            jax.ShapeDtypeStruct(parcel_shape, low),
            jax.ShapeDtypeStruct(parcel_shape, low),
        ],
        scratch_shapes=[
            pltpu.VMEM((tokens, width), high),
            pltpu.VMEM((tokens, width), low),
            pltpu.VMEM((width, tokens), low),
            pltpu.VMEM((tokens, width), high),
            pltpu.VMEM((tokens, width), high),
            pltpu.VMEM((tokens, width), low),
            pltpu.VMEM(parcel_shape, low),
            pltpu.VMEM(parcel_shape, low),
            pltpu.SemaphoreType.DMA((parts + 4,)),
        ],
        cost_estimate=cost("feed_both"),
        compiler_params=pltpu.CompilerParams(vmem_limit_bytes=vmem_bytes),
        name="feed_both",
    )(core, crossed, hidden, cotangent, gain, out_weight, gate_weight, up_weight, down_weight)


def lower_bits(sums):
    levels = lax.axis_size("items").bit_length() - 1
    for bit in range(levels - 4, -1, -1):
        mine = bit_of("items", bit)
        halves = [piece.reshape(2, piece.shape[0] // 2, piece.shape[1]) for piece in sums]
        sums = [pick(piece, mine) + swap(pick(piece, 1 - mine), "items", 1 << bit) for piece in halves]
    return sums


def memory_back(parcel, core_ref, *refs):
    wk_ref, wv_ref, away_ref, near_ref, kept_ref, sent_ref, total_ref = refs[6:]
    step = pl.program_id(0)
    steps = pl.num_programs(0)

    def block(rows_ref, grad_k_ref, grad_v_ref, grad_ref, first):
        grad_k, grad_v = grad_k_ref[...], grad_v_ref[...]
        grad_ref[...] = (rows_dot(grad_k, wk_ref[...]) + rows_dot(grad_v, wv_ref[...])).astype(low)
        width = grad_k.shape[1]
        rows = rows_ref[...].T
        parts = plain_dot(rows, grad_k), plain_dot(rows, grad_v)
        for job, part in enumerate(parts):
            columns = slice(job * width, (job + 1) * width)

            if first:

                @pl.when(step == 0)
                def _():
                    total_ref[:, columns] = part

                @pl.when(step > 0)
                def _():
                    total_ref[:, columns] += part

            else:
                total_ref[:, columns] += part

    @pl.when(step < steps // 2)
    def _():
        block(*refs[:3], away_ref, True)

    @pl.when(step >= steps // 2)
    def _():
        block(*refs[3:6], near_ref, False)

    @pl.when(step == steps - 1)
    def _():
        core = core_ref[0]
        for job, (_, width) in enumerate(parcel.shapes):
            total = total_ref[:, job * width : (job + 1) * width].astype(low)
            tiles = both_sides(total, core)
            count = len(tiles) // 2
            for at, product in enumerate(tiles):
                kind, tile = divmod(at, count)
                put_rows(parcel, job, product, tile, (kept_ref, sent_ref)[kind], 0)


def memory_back_call(parcel, core, far, near, wk, wv):
    total, width = far[0].shape
    half = total // 2
    name = "memory_back"
    first = lambda: pl.BlockSpec((half, width), lambda step: (jnp.minimum(step, 1), 0))
    second = lambda: pl.BlockSpec((half, width), lambda step: (jnp.maximum(step - 2, 0), 0))
    parcel_shape = (BLOCKS, parcel.rows, LANES)
    fixed = pl.BlockSpec(parcel_shape, lambda step: (0, 0, 0))
    return pl.pallas_call(
        lambda *refs: memory_back(parcel, *refs),
        grid=(4,),
        in_specs=[pl.BlockSpec(memory_space=pltpu.SMEM)]
        + [first() for _ in far]
        + [second() for _ in near]
        + [whole_spec(piece.shape) for piece in (wk, wv)],
        out_specs=[first(), second(), fixed, fixed],
        out_shape=[jax.ShapeDtypeStruct((total, width), low)] * 2
        + [jax.ShapeDtypeStruct(parcel_shape, low)] * 2,
        scratch_shapes=[pltpu.VMEM((width, 2 * width), high)],
        cost_estimate=cost(name),
        compiler_params=pltpu.CompilerParams(vmem_limit_bytes=vmem_bytes),
        name=name,
    )(core, *far, *near, wk, wv)


def land_memory(place_ref, *refs):
    for which in range(len(refs) - 1):

        @pl.when(pl.program_id(0) == which)
        def _():
            refs[-1][0] = refs[which][...].astype(high)


def land_call(place, pieces):
    rows, width = pieces[1].shape
    return pl.pallas_call(
        land_memory,
        out_shape=jax.ShapeDtypeStruct((len(pieces), rows, width), high),
        grid_spec=pltpu.PrefetchScalarGridSpec(
            num_scalar_prefetch=1,
            grid=(len(pieces),),
            in_specs=[
                pl.BlockSpec((rows, width), lambda step, _: (0, 0), pipeline_mode=pl.Buffered(1))
                for _ in pieces
            ],
            out_specs=pl.BlockSpec((1, rows, width), lambda step, place: (place[0] ^ step, 0, 0)),
        ),
        cost_estimate=cost("land_memory"),
        compiler_params=pltpu.CompilerParams(vmem_limit_bytes=vmem_bytes),
        name="land_memory",
    )(place, *pieces)


def leave_cross(
    grad_q_ref,
    hidden_ref,
    grad_in_ref,
    gain_ref,
    wq_ref,
    out_ref,
    grad_hidden_ref,
    branch_ref,
    grad_attended_ref,
    grad_gain_ref,
):
    to_rows, to_gain = norm_back(
        hidden_ref[...], gain_ref[...], rows_dot(grad_q_ref[...], wq_ref[...])
    )
    grad_hidden = grad_in_ref[...] + to_rows
    grad_hidden_ref[...] = grad_hidden
    branch = grad_hidden.astype(low)
    branch_ref[...] = branch
    grad_attended_ref[...] = rows_dot(branch, out_ref[...]).astype(low)
    add_up(grad_gain_ref, to_gain)


def leave_self(
    grad_q_ref,
    grad_k_ref,
    grad_v_ref,
    tokens_ref,
    grad_in_ref,
    gain_ref,
    wq_ref,
    wk_ref,
    wv_ref,
    grad_ref,
    grad_gain_ref,
):
    grad_normed = (
        rows_dot(grad_q_ref[...], wq_ref[...])
        + rows_dot(grad_k_ref[...], wk_ref[...])
        + rows_dot(grad_v_ref[...], wv_ref[...])
    )
    to_rows, to_gain = norm_back(tokens_ref[...].astype(high), gain_ref[...], grad_normed)
    grad_ref[...] = (grad_in_ref[...] + to_rows).astype(low)
    add_up(grad_gain_ref, to_gain)


def two_heads(rows):
    first = lax.broadcasted_iota(jnp.int32, rows.shape, 1) < HD
    zero = jnp.zeros_like(rows)
    return jnp.concatenate([jnp.where(first, rows, zero), jnp.where(first, zero, rows)], axis=0)


def one_pair(stacked):
    half = stacked.shape[1] // 2
    first = lax.broadcasted_iota(jnp.int32, (stacked.shape[0], half), 0) < HD
    return jnp.where(first, stacked[:, :half], stacked[:, half:]).T


def attend_forward_kernel(causal, chunks, carried, last, live_ref, q_ref, k_ref, v_ref, *refs):
    before, refs = refs[:carried], refs[carried:]
    queries = two_heads(q_ref[...])
    wide = queries.shape[0]
    size = k_ref.shape[0] // chunks
    if not causal:
        lane = lax.broadcasted_iota(jnp.int32, queries.shape, 1)
        queries = jnp.concatenate([queries, jnp.where(lane == 0, 1.0, 0.0).astype(low)], axis=1)
    peaks, totals, mixes = [], [], []
    for chunk in range(chunks):
        here = slice(chunk * size, (chunk + 1) * size)
        keys = k_ref[here, :]
        if causal:
            scores = rows_dot(keys, queries)
            key = lax.broadcasted_iota(jnp.int32, (size, wide), 0) + chunk * size
            token = lax.broadcasted_iota(jnp.int32, (size, wide), 1)
            token = jnp.where(token >= wide // 2, token - wide // 2, token)
            scores = jnp.where(key <= token, scores, neg_big)
        else:
            key = lax.broadcasted_iota(jnp.int32, keys.shape, 0)
            lane = lax.broadcasted_iota(jnp.int32, keys.shape, 1)
            dead = jnp.where((lane == 0) & (key >= live_ref[chunk]), neg_big, 0.0).astype(low)
            scores = rows_dot(jnp.concatenate([keys, dead], axis=1), queries)
        peak = jnp.max(scores, axis=0, keepdims=True)
        weights = jnp.exp(scores - peak)
        total = jnp.sum(weights, axis=0, keepdims=True)
        weights = weights.astype(low)
        refs[0][0, here, :] = weights
        peaks.append(peak)
        totals.append(total)
        mixes.append(cols_dot(v_ref[here, :], weights))
    if carried:
        stats_in = before[1][0]
        count = chunks
        peaks = [stats_in[at : at + 1] for at in range(count)] + peaks
        totals = [stats_in[count + at : count + at + 1] for at in range(count)] + totals
    top = peaks[0]
    for peak in peaks[1:]:
        top = jnp.maximum(top, peak)
    scales = [jnp.exp(peak - top) for peak in peaks]
    mixed = sum(mix * scale for mix, scale in zip(mixes, scales[-chunks:]))
    if carried:
        earlier = peaks[0]
        for peak in peaks[1:chunks]:
            earlier = jnp.maximum(earlier, peak)
        mixed = mixed + before[0][0] * jnp.exp(earlier - top)
    if last:
        inverse = 1.0 / sum(total * scale for total, scale in zip(totals, scales))
        refs[1][...] = one_pair(mixed * inverse).astype(low)
        for at, scale in enumerate(scales):
            refs[2][0, at : at + 1, :] = scale * inverse
    else:
        refs[1][0] = mixed
        for at in range(chunks):
            refs[2][0, at : at + 1, :] = peaks[at]
            refs[2][0, chunks + at : chunks + at + 1, :] = totals[at]


def attend_forward(queries, keys, values, live, causal, chunks, name, last=True, before=()):
    tokens, width = queries.shape
    patches = keys.shape[0]
    pairs = width // LANES
    by_pair = lambda rows: pl.BlockSpec((rows, LANES), lambda pair, _: (0, pair))
    stack = lambda rows: pl.BlockSpec((1, rows, 2 * tokens), lambda pair, _: (pair, 0, 0))
    return pl.pallas_call(
        lambda *refs: attend_forward_kernel(causal, chunks, len(before), last, *refs),
        out_shape=(
            jax.ShapeDtypeStruct((pairs, patches, 2 * tokens), low),
            jax.ShapeDtypeStruct((tokens, width), low)
            if last
            else jax.ShapeDtypeStruct((pairs, LANES, 2 * tokens), high),
            jax.ShapeDtypeStruct((pairs, 8, 2 * tokens), high),
        ),
        grid_spec=pltpu.PrefetchScalarGridSpec(
            num_scalar_prefetch=1,
            grid=(pairs,),
            in_specs=[by_pair(tokens), by_pair(patches), by_pair(patches)]
            + [stack(piece.shape[1]) for piece in before],
            out_specs=[stack(patches), by_pair(tokens) if last else stack(LANES), stack(8)],
        ),
        cost_estimate=cost(name),
        compiler_params=pltpu.CompilerParams(vmem_limit_bytes=vmem_bytes),
        name=name,
    )(live, queries, keys, values, *before)


def attend_backward_kernel(
    chunks,
    offset,
    carried,
    last,
    weight_ref,
    inverse_ref,
    q_ref,
    k_ref,
    v_ref,
    mixed_ref,
    grad_mixed_ref,
    *refs,
):
    before, (grad_q_ref, grad_k_ref, grad_v_ref) = refs[:carried], refs[-3:]
    queries = two_heads(q_ref[...])
    grads = grad_mixed_ref[...].astype(high).T
    mixed = mixed_ref[...].astype(high).T
    first = lax.broadcasted_iota(jnp.int32, grads.shape, 0) < HD
    zero = jnp.zeros_like(grads)
    grads = jnp.concatenate([jnp.where(first, grads, zero), jnp.where(first, zero, grads)], axis=1)
    mixed = jnp.concatenate([mixed, mixed], axis=1)
    size = k_ref.shape[0] // chunks
    grad_q = jnp.zeros(grads.shape, high)
    for chunk in range(chunks):
        here = slice(chunk * size, (chunk + 1) * size)
        at = offset + chunk
        scaled = (grads * inverse_ref[0, at : at + 1, :]).astype(low)
        wide = scaled.astype(high)
        centre = jnp.sum(wide * mixed, axis=0, keepdims=True)
        rows = wide.T.astype(low)
        weights = weight_ref[0, here, :]
        grad_probs = plain_dot(v_ref[here, :], scaled)
        grad_scores = (weights.astype(high) * (grad_probs - centre)).astype(low)
        grad_v_ref[here, :] = plain_dot(weights, rows).astype(low)
        grad_k_ref[here, :] = plain_dot(grad_scores, queries).astype(low)
        grad_q = grad_q + cols_dot(k_ref[here, :], grad_scores)
    grad_q = one_pair(grad_q)
    if carried:
        grad_q = grad_q + before[0][...]
    grad_q_ref[...] = grad_q.astype(grad_q_ref.dtype)


def attend_backward(
    weights,
    inverse,
    queries,
    keys,
    values,
    mixed,
    grad_mixed,
    chunks,
    offset,
    name,
    last=True,
    before=(),
    pairs=None,
    filled=(),
):
    tokens, width = queries.shape
    patches = keys.shape[0]
    begin, end = pairs or (0, width // LANES)
    by_token = pl.BlockSpec((tokens, LANES), lambda pair: (0, pair + begin))
    by_patch = pl.BlockSpec((patches, LANES), lambda pair: (0, pair + begin))
    return pl.pallas_call(
        lambda *refs: attend_backward_kernel(chunks, offset, len(before), last, *refs),
        out_shape=(
            jax.ShapeDtypeStruct((tokens, width), low if last else high),
            jax.ShapeDtypeStruct((patches, width), low),
            jax.ShapeDtypeStruct((patches, width), low),
        ),
        grid=(end - begin,),
        in_specs=[
            pl.BlockSpec((1, patches, 2 * tokens), lambda pair: (pair + begin, 0, 0)),
            pl.BlockSpec((1, 8, 2 * tokens), lambda pair: (pair + begin, 0, 0)),
            by_token,
            by_patch,
            by_patch,
            by_token,
            by_token,
        ]
        + [by_token] * len(before)
        + [pl.BlockSpec(memory_space=pl.ANY)] * len(filled),
        out_specs=[by_token, by_patch, by_patch],
        input_output_aliases={7 + len(before) + which: which for which in range(len(filled))},
        cost_estimate=cost(name),
        compiler_params=pltpu.CompilerParams(vmem_limit_bytes=vmem_bytes),
        name=name,
    )(weights, inverse, queries, keys, values, mixed, grad_mixed, *before, *filled)


def swap(piece, axis_name, mask):
    size = lax.axis_size(axis_name)
    return lax.ppermute(piece, axis_name, [(place, place ^ mask) for place in range(size)])


def bit_of(axis_name, bit):
    return (lax.axis_index(axis_name) >> bit) & 1


def pick(piece, which):
    return lax.dynamic_index_in_dim(piece, which, 0, keepdims=False)


class Parcel:
    def __init__(self, shapes, extra=0):
        self.shapes = shapes
        self.heights = [height // BLOCKS for height, _ in shapes]
        self.plain = [width // 4 // LANES for _, width in shapes]
        self.at = []
        at = 0
        for (_, width), tiles, height in zip(shapes, self.plain, self.heights):
            self.at.append(at)
            at += tiles * height + (height // 2 if width // 4 % LANES else 0)
        self.extra = extra
        self.own = at + extra
        self.rows = 2 * self.own


def place(block):
    return (block & 1) * 4 + (block & 2) + (block >> 2)


def core_tiles(grad, core):
    quarter = grad.shape[1] // 4
    starts = [core * quarter, 2 * quarter + core * quarter]
    tiles = [
        grad[:, start + at : start + at + LANES]
        for start in starts
        for at in range(0, quarter - LANES + 1, LANES)
    ]
    rest = quarter % LANES
    if rest:
        tiles.append(
            jnp.concatenate(
                [grad[:, start + quarter - rest : start + quarter] for start in starts], axis=1
            )
        )
    return tiles


def both_sides(grad, core):
    first, second = core_tiles(grad, 0), core_tiles(grad, 1)
    own = [jnp.where(core == 0, one, other) for one, other in zip(first, second)]
    return own + [jnp.where(core == 0, other, one) for one, other in zip(first, second)]


def weight_kernel(jobs, parcel, n_in, core_ref, *refs):
    ins, (kept_ref, sent_ref), turned_ref = refs[:n_in], refs[n_in:-1], refs[-1]
    core = core_ref[0]
    if parcel.extra:
        for out_ref in (kept_ref, sent_ref):
            for block in range(BLOCKS):
                for end in (parcel.own, parcel.rows):
                    out_ref[block, end - parcel.extra : end, :] = ins[-1][...]
    last_rows = None
    for job, (row_at, grad_at, from_lane) in enumerate(jobs):
        width = parcel.shapes[job][1]
        grad = ins[grad_at][:, from_lane : from_lane + width]
        if row_at is not None and row_at != last_rows:
            turned_ref[...] = ins[row_at][...].T
            last_rows = row_at
        tiles = both_sides(grad, core)
        count = len(tiles) // 2
        for begin in range(0, 2 * count, 2):
            product = jnp.concatenate(tiles[begin : begin + 2], axis=1)
            if row_at is not None:
                product = plain_dot(turned_ref[...], product)
            product = product.astype(low)
            for slot in (0, 1):
                kind, tile = divmod(begin + slot, count)
                put_rows(parcel, job, product, tile, (kept_ref, sent_ref)[kind], slot)


def fold_one(parcel, with_x, mine_ref, kept_ref, received_ref, *out_refs):
    for which, out_ref in enumerate(out_refs):
        part = mine_ref[0] ^ which
        if with_x:
            begin = pl.multiple_of((part & 1) * parcel.own, 16)
            here = (part >> 1, slice(None), pl.ds(begin, parcel.own), slice(None))
        else:
            here = part
        out_ref[...] = (kept_ref[here].astype(high) + received_ref[here].astype(high)).astype(low)


def sum_of(refs):
    first, second, third, fourth = [ref[...].astype(high) for ref in refs]
    return (first + second) + (third + fourth)


def fold_two(parcel, with_x, first_ref, second_ref, third_ref, fourth_ref, out_ref):
    total = sum_of((first_ref, second_ref, third_ref, fourth_ref)).astype(low)
    if with_x:
        out_ref[...] = total
    else:
        for which in range(4):
            begin = (which & 1) * parcel.own
            out_ref[which] = total[which >> 1, begin : begin + parcel.own, :]


def fold_end(parcel, parts_ref, *outs):
    total = sum_of([parts_ref.at[which] for which in range(4)])
    for job, rows in enumerate(parcel.heights):
        at = parcel.at[job]
        for tile in range(parcel.plain[job]):
            outs[job][:, tile * LANES : (tile + 1) * LANES] = total[at : at + rows]
            at += rows
        begin = parcel.plain[job] * LANES
        rest = outs[job].shape[1] - begin
        if rest:
            outs[job][: rows // 2, begin:] = total[at : at + rows // 2, :rest]
            outs[job][rows // 2 :, begin:] = total[at : at + rows // 2, rest:]
    if parcel.extra:
        outs[-1][...] = total[-parcel.extra :]


def weight_parts(arrays, jobs, parcel, name):
    turned = [arrays[job[0]].shape for job in jobs if job[0] is not None]
    depth, height = turned[0] if turned else (16, LANES)
    return one_step_call(
        lambda *refs: weight_kernel(jobs, parcel, len(arrays), *refs),
        name,
        [bit_of("narrow", 0).reshape(1), *arrays],
        [((BLOCKS, parcel.rows, LANES), low)] * 2,
        [pltpu.VMEM((height, depth), low)],
    )


class Travel:
    def __init__(self, parcel, kept, sent, name, with_x):
        self.parcel = parcel
        self.name = name
        self.kept = kept
        self.received = swap(sent, "narrow", 1)
        self.top = lax.axis_size("items").bit_length() - 4
        self.with_x = with_x

    def joint(self, up, side):
        narrow = lax.axis_size("narrow")
        return [
            (place, ((place // narrow) ^ up) * narrow + ((place % narrow) ^ side))
            for place in range(lax.axis_size("items") * narrow)
        ]

    def fold_one(self, *earlier):
        kept, received = lax.optimization_barrier((self.kept, self.received, *earlier))[:2]
        rows, top = self.parcel.rows, self.top
        if self.with_x:
            mine = bit_of("items", top) * 2 + bit_of("narrow", 1)
            view, shape = (2, 4, rows, LANES), (4, self.parcel.own, LANES)
            partners = [(0, 2), (1 << top, 0), (1 << top, 2)]
        else:
            mine = bit_of("items", top) * 2 + bit_of("items", top + 1)
            view, shape = (4, 2, rows, LANES), (2, rows, LANES)
            partners = [(2 << top, 0), (1 << top, 0), (3 << top, 0)]
        parts = one_step_call(
            lambda *refs: fold_one(self.parcel, self.with_x, *refs),
            self.name + "_one",
            [mine.reshape(1), kept.reshape(view), received.reshape(view)],
            [(shape, low)] * 4,
        )
        self.parts = [parts[0]] + [
            lax.ppermute(part, ("items", "narrow"), self.joint(*partner))
            for part, partner in zip(parts[1:], partners)
        ]
        return parts[0]

    def fold_two(self, *earlier):
        parts = lax.optimization_barrier((*self.parts, *earlier))[:4]
        parcel = self.parcel
        (parts,) = one_step_call(
            lambda *refs: fold_two(parcel, self.with_x, *refs),
            self.name + "_two",
            list(parts),
            [((4, parcel.own, LANES), low)],
        )
        far = 4 << self.top
        first, second = ((2 << self.top, 0), (far, 0)) if self.with_x else ((far, 0), (0, 2))
        narrow = lax.axis_size("narrow")
        clear = first[0] | second[0]
        side = first[1] | second[1]
        groups = [
            [
                (item | one[0] | two[0]) * narrow + (other | one[1] | two[1])
                for one in ((0, 0), first)
                for two in ((0, 0), second)
            ]
            for item in range(lax.axis_size("items"))
            for other in range(narrow)
            if not item & clear and not other & side
        ]
        self.parts = lax.all_to_all(
            parts, ("items", "narrow"), 0, 0, axis_index_groups=groups, tiled=True
        )
        return parts

    def end(self, *earlier):
        parts = lax.optimization_barrier((self.parts, *earlier))[0]
        parcel = self.parcel
        outs = [((height // BLOCKS, width // 4), high) for height, width in parcel.shapes]
        outs += [((parcel.extra, LANES), high)] if parcel.extra else []
        outs = list(
            one_step_call(
                lambda *refs: fold_end(parcel, *refs),
                self.name + "_end",
                [parts],
                outs,
            )
        )
        count = len(parcel.shapes)
        extras = outs[count:]
        for bit in range(self.top, 0, -1):
            extras = [piece + swap(piece, "items", 1 << (bit - 1)) for piece in extras]
        return list(lower_bits(outs[:count])) + extras


def exchange(piece):
    return lax.all_to_all(piece, "narrow", split_axis=0, concat_axis=0, tiled=True)


def body(
    tokens,
    memory,
    mem_count,
    cotangent,
    gain_self,
    self_query,
    self_key,
    self_value,
    self_out,
    gain_cross,
    cross_query,
    cross_key,
    cross_value,
    cross_out,
    gain_feed,
    gate_weight,
    up_weight,
    down_weight,
):
    width = tokens.shape[2]
    inner = gate_weight.shape[1]
    gain_self, gain_cross, gain_feed = [
        gain.reshape(1, width) for gain in (gain_self, gain_cross, gain_feed)
    ]
    parts = lax.axis_size("narrow")
    mine = lax.axis_index("narrow")
    token_rows = exchange(tokens).reshape(-1, width)
    own_memory, *away_memory = [pick(memory, mine ^ which) for which in range(parts)]
    pieces = [own_memory] + [
        swap(piece, "narrow", which + 1) for which, piece in enumerate(away_memory)
    ]
    cotangent_rows = exchange(cotangent).reshape(-1, width)
    count = pick(mem_count, mine)
    local_mem = memory.shape[1]
    live = jnp.stack([count - local_mem * (mine ^ which) for which in range(parts)]).astype(jnp.int32)
    kinds = [((2 * local_mem, width), low)] * 3
    near_rows, near_keys, near_values = one_step_call(
        enter_memory,
        "enter_memory_near",
        [pieces[0], pieces[1], cross_key, cross_value],
        kinds,
    )
    normed_one, query_one, key_one, value_one = row_call(
        enter_self,
        "enter_self",
        256,
        [after(token_rows, near_keys)],
        [gain_self, self_query, self_key, self_value],
        [(width, low)] * 4,
    )
    weights_one, attended, inverse_one = attend_forward(
        query_one, key_one, value_one, live, True, 1, "self_forward"
    )
    hidden_one, normed_two, query_two = row_call(
        enter_cross,
        "enter_cross",
        256,
        [attended, token_rows],
        [gain_cross, self_out, cross_query],
        [(width, high), (width, low), (width, low)],
    )
    near_weights, near_mixed, near_stats = attend_forward(
        query_two, near_keys, near_values, live[:2], False, 2, "cross_forward_near", False
    )
    far_rows, far_keys, far_values = one_step_call(
        enter_memory,
        "enter_memory_far",
        [after(pieces[2], near_stats), pieces[3], cross_key, cross_value],
        kinds,
    )
    far_weights, crossed, inverse_two = attend_forward(
        query_two,
        far_keys,
        far_values,
        live[2:],
        False,
        2,
        "cross_forward_far",
        True,
        (near_mixed, near_stats),
    )
    square = (width, width)
    feed_parcel = Parcel([(width, inner), (width, inner), (inner, width), square])
    result, grad_hidden_two, branch_two, grad_crossed, grad_gain_feed, *feed_parts = feed_call(
        feed_parcel,
        bit_of("narrow", 0).reshape(1),
        crossed,
        hidden_one,
        cotangent_rows,
        gain_feed,
        cross_out,
        gate_weight,
        up_weight,
        down_weight,
    )
    feed_trip = Travel(feed_parcel, *feed_parts, "feed_weights", True)
    result = exchange(result.reshape(tokens.shape))
    far = ()
    ready = feed_trip.kept
    for pairs in ((0, 3), (3, 6)):
        far = attend_backward(
            far_weights,
            inverse_two,
            query_two,
            far_keys,
            far_values,
            crossed,
            after(grad_crossed, ready),
            2,
            2,
            "cross_backward_far_a" if pairs[0] == 0 else "cross_backward_far_b",
            False,
            pairs=pairs,
            filled=far,
        )
        ready = feed_trip.fold_one(far[0]) if pairs[0] == 0 else far[0]
    far_grad_q, far_grad_k, far_grad_v = far
    grad_query_two, near_grad_k, near_grad_v = attend_backward(
        near_weights,
        inverse_two,
        query_two,
        near_keys,
        near_values,
        crossed,
        after(grad_crossed, result),
        2,
        0,
        "cross_backward_near",
        True,
        (far_grad_q,),
    )
    grad_hidden_one, branch_one, grad_attended, grad_gain_cross = row_call(
        leave_cross,
        "leave_cross",
        256,
        [grad_query_two, hidden_one, grad_hidden_two],
        [gain_cross, cross_query, self_out],
        [(width, high), (width, low), (width, low)],
        [width],
    )
    grad_query_one, key_one_grad, value_one_grad = attend_backward(
        weights_one,
        inverse_one,
        query_one,
        key_one,
        value_one,
        attended,
        grad_attended,
        1,
        0,
        "self_backward",
    )
    tokens_grad, grad_gain_self = row_call(
        leave_self,
        "leave_self",
        256,
        [grad_query_one, key_one_grad, value_one_grad, token_rows, grad_hidden_one],
        [gain_self, self_query, self_key, self_value],
        [(width, low)],
        [width],
    )
    gains = jnp.concatenate([grad_gain_self, grad_gain_cross, grad_gain_feed], axis=0).astype(low)
    gains = jnp.pad(gains.reshape(-1, LANES), ((0, 32 - 3 * width // LANES), (0, 0)))
    self_parcel = Parcel([square] * 5, 32)
    self_parts = weight_parts(
        [
            after(normed_one, tokens_grad, *feed_trip.parts[1:]),
            grad_query_one,
            key_one_grad,
            value_one_grad,
            normed_two,
            grad_query_two,
            attended,
            branch_one,
            gains,
        ],
        [(0, 1, 0), (0, 2, 0), (0, 3, 0), (4, 5, 0), (6, 7, 0)],
        self_parcel,
        "self_weights",
    )
    self_trip = Travel(self_parcel, *self_parts, "self_weights", True)
    tokens_grad = exchange(tokens_grad.reshape(tokens.shape))
    ready = feed_trip.fold_two(self_parts[0], tokens_grad)
    ready = self_trip.fold_one(ready)
    cross_parcel = Parcel([square] * 2)
    grad_away, grad_near, *cross_parts = memory_back_call(
        cross_parcel,
        bit_of("narrow", 0).reshape(1),
        [after(far_rows, ready), far_grad_k, far_grad_v],
        [near_rows, near_grad_k, near_grad_v],
        cross_key,
        cross_value,
    )
    landed_away = swap(grad_away, "narrow", 2)
    cross_trip = Travel(cross_parcel, *cross_parts, "cross_weights", False)
    tokens_grad = tokens_grad.astype(high)
    ready = self_trip.fold_two(grad_away)
    ready = cross_trip.fold_one(ready)
    gate_sum, up_sum, down_sum, cross_out_sum = feed_trip.end(ready)
    ready = gate_sum
    ready = cross_trip.fold_two(ready)
    grad_near, landed_away = lax.optimization_barrier((grad_near, landed_away, ready))[:2]
    landed_core = swap(grad_near[local_mem:], "narrow", 1)
    landed_far = swap(landed_away[local_mem:], "narrow", 1)
    self_query_sum, self_key_sum, self_value_sum, cross_query_sum, self_out_sum, gains = (
        self_trip.end(ready)
    )
    memory_grad = land_call(
        mine.reshape(1),
        [after(grad_near, self_query_sum), landed_core, landed_away, landed_far],
    )
    cross_key_sum, cross_value_sum = cross_trip.end(memory_grad)
    gains = gains[: 3 * width // LANES].reshape(3, width)
    return (
        result,
        tokens_grad,
        memory_grad,
        gains[0],
        self_query_sum,
        self_key_sum,
        self_value_sum,
        self_out_sum,
        gains[1],
        cross_query_sum,
        cross_key_sum,
        cross_value_sum,
        cross_out_sum,
        gains[2],
        gate_sum,
        up_sum,
        down_sum,
    )


def solution(mesh):
    in_specs = (
        P("items", "narrow", None),
        P("items", "narrow", None),
        P("items"),
        P("items", "narrow", None),
        P(),
        P(),
        P(),
        P(),
        P(),
        P(),
        P(),
        P(),
        P(),
        P(),
        P(),
        P(),
        P(),
        P(),
    )
    out_specs = (
        P("items", "narrow", None),
        P("items", "narrow", None),
        P("items", "narrow", None),
        P(),
        P("items", "narrow"),
        P("items", "narrow"),
        P("items", "narrow"),
        P("items", "narrow"),
        P(),
        P("items", "narrow"),
        P("items", "narrow"),
        P("items", "narrow"),
        P("items", "narrow"),
        P(),
        P("items", "narrow"),
        P("items", "narrow"),
        P("items", "narrow"),
    )
    return jax.shard_map(body, mesh=mesh, in_specs=in_specs, out_specs=out_specs, check_vma=False)
```

```python
import jax
import jax.numpy as jnp
from jax import lax
from jax.experimental import pallas as pl
from jax.experimental.pallas import tpu as pltpu
from jax.sharding import PartitionSpec as P

HD = 64
LANES = 128
BLOCKS = 8

eps = 1e-06
neg_big = -1e30
gelu_scale = 0.7978845608028654
gelu_cubic = 0.044715
low = jnp.bfloat16
high = jnp.float32
vmem_bytes = 60 * 1024 * 1024


def rows_dot(left_side, right_side):
    return lax.dot_general(
        left_side, right_side, (((1,), (1,)), ((), ())), preferred_element_type=high
    )


def cols_dot(left_side, right_side):
    return lax.dot_general(
        left_side, right_side, (((0,), (0,)), ((), ())), preferred_element_type=high
    )


def plain_dot(left_side, right_side):
    return jnp.dot(left_side, right_side, preferred_element_type=high)


def inverse_scale(hidden):
    return lax.rsqrt(jnp.mean(hidden * hidden, axis=-1, keepdims=True) + eps)


def norm_back(hidden, gain, grad):
    scale = inverse_scale(hidden)
    weighted = gain * grad
    middle = jnp.mean(weighted * hidden, axis=-1, keepdims=True)
    to_rows = scale * (weighted - hidden * (scale * scale * middle))
    to_gain = jnp.sum(grad * hidden * scale, axis=0, keepdims=True)
    return to_rows, to_gain


call_time = {
    "enter_memory_near": 2,
    "self_forward": 8,
    "cross_forward_near": 6,
    "enter_memory_far": 2,
    "cross_forward_far": 6,
    "cross_backward_far_b": 100,
    "feed_weights_two": 100,
    "memory_back": 100,
    "self_weights_two": 100,
    "self_weights_end": 100,
}


def cost(name):
    return pl.CostEstimate(
        flops=int(call_time.get(name, 0.001) * 1.15e9), bytes_accessed=1, transcendentals=0
    )


def after(piece, *earlier):
    return lax.optimization_barrier((piece, *earlier))[0]


def row_spec(rows, width):
    return pl.BlockSpec((rows, width), lambda step: (step, 0))


def whole_spec(shape):
    return pl.BlockSpec(
        shape, lambda step: (0,) * len(shape), pipeline_mode=pl.Buffered(1)
    )


def self_forward(
    tokens_ref,
    gains_ref,
    next_query_ref,
    wq_ref,
    wk_ref,
    wv_ref,
    out_ref,
    normed_ref,
    q_ref,
    k_ref,
    v_ref,
    weight_ref,
    mixed_ref,
    inverse_ref,
    hidden_ref,
    next_normed_ref,
    next_q_ref,
):
    pair = pl.program_id(0)

    @pl.when(pair == 0)
    def _():
        hidden = tokens_ref[...].astype(high)
        normed_ref[...] = (hidden * inverse_scale(hidden) * gains_ref[0:1, :]).astype(low)
        hidden_ref[...] = hidden

    weights = jnp.concatenate([wq_ref[...], wk_ref[...], wv_ref[...]], axis=1)
    projected = plain_dot(normed_ref[...], weights).astype(low)
    for at, part_ref in enumerate((q_ref, k_ref, v_ref)):
        part_ref[...] = projected[:, at * LANES : (at + 1) * LANES]
    attend_forward_kernel(
        True, 1, 0, True, None, q_ref, k_ref, v_ref, weight_ref, mixed_ref, inverse_ref
    )
    hidden_ref[...] += plain_dot(mixed_ref[...], out_ref[...])

    @pl.when(pair == pl.num_programs(0) - 1)
    def _():
        hidden = hidden_ref[...]
        normed = (hidden * inverse_scale(hidden) * gains_ref[1:2, :]).astype(low)
        next_normed_ref[...] = normed
        next_q_ref[...] = plain_dot(normed, next_query_ref[...]).astype(low)


def self_forward_call(tokens, gains, next_query, wq, wk, wv, out_weight):
    rows, width = tokens.shape
    pairs = width // LANES
    whole = pl.BlockSpec((rows, width), lambda pair: (0, 0))
    columns = pl.BlockSpec((rows, LANES), lambda pair: (0, pair))
    stack = lambda height: pl.BlockSpec((1, height, 2 * rows), lambda pair: (pair, 0, 0))
    plain = jax.ShapeDtypeStruct((rows, width), low)
    return pl.pallas_call(
        self_forward,
        grid=(pairs,),
        in_specs=[whole_spec(piece.shape) for piece in (tokens, gains, next_query)]
        + [pl.BlockSpec((width, LANES), lambda pair: (0, pair))] * 3
        + [pl.BlockSpec((LANES, width), lambda pair: (pair, 0))],
        out_specs=[whole, columns, columns, columns, stack(rows), columns, stack(8)] + [whole] * 3,
        out_shape=[
            plain,
            plain,
            plain,
            plain,
            jax.ShapeDtypeStruct((pairs, rows, 2 * rows), low),
            plain,
            jax.ShapeDtypeStruct((pairs, 8, 2 * rows), high),
            jax.ShapeDtypeStruct((rows, width), high),
            plain,
            plain,
        ],
        cost_estimate=cost("self_forward"),
        compiler_params=pltpu.CompilerParams(vmem_limit_bytes=vmem_bytes),
        name="self_forward",
    )(tokens, gains, next_query, wq, wk, wv, out_weight)


def enter_memory(first_ref, second_ref, wk_ref, wv_ref, rows_ref, k_ref, v_ref):
    half = first_ref.shape[0]
    for at, piece_ref in ((0, first_ref), (half, second_ref)):
        rows = piece_ref[...]
        rows_ref[at : at + half, :] = rows
        k_ref[at : at + half, :] = plain_dot(rows, wk_ref[...]).astype(low)
        v_ref[at : at + half, :] = plain_dot(rows, wv_ref[...]).astype(low)


def one_step_call(kernel, name, ins, outs, scratch=()):
    vmem = pl.BlockSpec(memory_space=pltpu.VMEM)
    smem = pl.BlockSpec(memory_space=pltpu.SMEM)
    return pl.pallas_call(
        kernel,
        in_specs=[smem if piece.dtype == jnp.int32 else vmem for piece in ins],
        out_specs=[vmem] * len(outs),
        out_shape=[jax.ShapeDtypeStruct(shape, kind) for shape, kind in outs],
        scratch_shapes=list(scratch),
        cost_estimate=cost(name),
        compiler_params=pltpu.CompilerParams(vmem_limit_bytes=vmem_bytes),
        name=name,
    )(*ins)


def put_block(parcel, job, tile, rows_of, out_ref, spot):
    plain, rows = parcel.plain[job], parcel.heights[job]
    if tile < 2 * plain:
        at = (tile // plain) * parcel.own + parcel.at[job] + (tile % plain) * rows
        out_ref[spot, at : at + rows, :] = rows_of
    else:
        half = LANES // 2
        for side in (0, 1):
            at = side * parcel.own + parcel.at[job] + plain * rows
            lanes = slice(side * half, (side + 1) * half)
            out_ref[spot, at : at + rows // 2, :] = jnp.concatenate(
                [rows_of[: rows // 2, lanes], rows_of[rows // 2 :, lanes]], axis=1
            )


def put_rows(parcel, job, product, tile, out_ref, slot):
    rows = parcel.heights[job]
    for block in range(BLOCKS):
        put_block(
            parcel,
            job,
            tile,
            product[block * rows : (block + 1) * rows, slot * LANES : (slot + 1) * LANES],
            out_ref,
            place(block),
        )


def feed_both(
    parcel,
    parts,
    core_ref,
    crossed_ref,
    hidden_in_ref,
    cotangent_ref,
    gain_ref,
    out_ref,
    gate_ref,
    up_ref,
    down_ref,
    result_ref,
    grad_hidden_ref,
    branch_ref,
    grad_crossed_ref,
    grad_gain_ref,
    kept_out_ref,
    sent_out_ref,
    hidden_ref,
    normed_ref,
    turned_ref,
    sum_ref,
    back_ref,
    sides_ref,
    kept_ref,
    sent_ref,
    done_ref,
):
    step = pl.program_id(0)
    core = core_ref[0]
    gain = gain_ref[2:3, :]

    @pl.when(step == 0)
    def _():
        hidden = hidden_in_ref[...] + plain_dot(crossed_ref[...], out_ref[...])
        hidden_ref[...] = hidden
        normed = (hidden * inverse_scale(hidden) * gain).astype(low)
        normed_ref[...] = normed
        turned_ref[...] = normed.T
        sum_ref[...] = hidden
        back_ref[...] = jnp.zeros_like(back_ref)
        sides_ref[...] = jnp.concatenate(both_sides(cotangent_ref[...], core), axis=1)

    inner = parcel.at[2]

    def copies(side_ref, out_ref, begin, rows, slot):
        here = (slice(None), pl.ds(begin, rows), slice(None))
        return pltpu.make_async_copy(side_ref.at[here], out_ref.at[here], done_ref.at[slot])

    normed = normed_ref[...]
    cotangent = cotangent_ref[...]
    turned = turned_ref[...]
    sides = sides_ref[...]
    part = gate_ref.shape[1]
    size = part
    output, back_sum = sum_ref[...], back_ref[...]
    grads, mixes = [], []
    for begin in range(0, part, size):
        here = slice(begin, begin + size)
        gate = plain_dot(normed, gate_ref[:, here])
        up = plain_dot(normed, up_ref[:, here])
        back = rows_dot(cotangent, down_ref[here, :])
        square = gate * gate
        curve = jnp.tanh(gelu_scale * (gate + gelu_cubic * gate * square))
        half = 0.5 * (1.0 + curve)
        bent = gate * half
        slope = half + 0.5 * gate * (1.0 - curve * curve) * (
            gelu_scale * (1.0 + 3.0 * gelu_cubic * square)
        )
        mixed = (bent * up).astype(low)
        grad_gate = (back * up * slope).astype(low)
        grad_up = (back * bent).astype(low)
        output = output + plain_dot(mixed, down_ref[here, :])
        back_sum = (
            back_sum
            + rows_dot(grad_gate, gate_ref[:, here])
            + rows_dot(grad_up, up_ref[:, here])
        )
        mixes.append(mixed)
        grads.append((grad_gate, grad_up))
    sum_ref[...] = output
    back_ref[...] = back_sum
    side = (step >> 1) * parcel.own
    for kind, (side_ref, target_ref) in enumerate(
        ((kept_ref, kept_out_ref), (sent_ref, sent_out_ref))
    ):

        @pl.when(((step & 1) ^ core) == kind)
        def _():
            for job in (0, 1):
                rows = parcel.heights[job]
                for which, pair in enumerate(grads):
                    product = plain_dot(turned, pair[job]).astype(low)
                    for tile in range(size // LANES):
                        at = side + parcel.at[job] + (which * size // LANES + tile) * rows
                        at = pl.multiple_of(at, 16)
                        for block in range(BLOCKS):
                            side_ref[place(block), pl.ds(at, rows), :] = product[
                                block * rows : (block + 1) * rows, tile * LANES : (tile + 1) * LANES
                            ]
            copies(side_ref, target_ref, pl.multiple_of(side, 16), inner, step).start()

    rows = parcel.heights[2]
    tiles = sides.shape[1] // LANES // 2
    for which, mixed in enumerate(mixes):
        product = cols_dot(mixed, sides).astype(low)
        here = product.shape[0] // rows
        for kind, side_ref in enumerate((kept_ref, sent_ref)):
            for tile in range(tiles):
                lane = (kind * tiles + tile) * LANES
                for block in range(here):
                    put_block(
                        parcel,
                        2,
                        tile,
                        product[block * rows : (block + 1) * rows, lane : lane + LANES],
                        side_ref,
                        place(step * here + block),
                    )

    @pl.when(step == pl.num_programs(0) - 1)
    def _():
        hidden = hidden_ref[...]
        result_ref[...] = sum_ref[...].astype(low)
        to_rows, to_gain = norm_back(hidden, gain, back_ref[...])
        grad_gain_ref[...] = to_gain
        grad_hidden = cotangent.astype(high) + to_rows
        grad_hidden_ref[...] = grad_hidden
        branch = grad_hidden.astype(low)
        branch_ref[...] = branch
        grad_crossed_ref[...] = rows_dot(branch, out_ref[...]).astype(low)
        sides = jnp.concatenate(both_sides(branch, core), axis=1)
        product = cols_dot(crossed_ref[...], sides).astype(low)
        for kind, side_ref in enumerate((kept_ref, sent_ref)):
            for tile in range(tiles):
                put_rows(parcel, 3, product, tile, side_ref, kind * tiles + tile)
        spans = ((inner, parcel.own), (parcel.own + inner, parcel.rows))
        last = [
            copies(side_ref, target_ref, begin, end - begin, parts + 2 * kind + which)
            for kind, (side_ref, target_ref) in enumerate(
                ((kept_ref, kept_out_ref), (sent_ref, sent_out_ref))
            )
            for which, (begin, end) in enumerate(spans)
        ]
        for copy in last:
            copy.start()
        for slot in range(parts):
            copies(kept_ref, kept_out_ref, 0, inner, slot).wait()
        for copy in last:
            copy.wait()


def feed_call(
    parcel, core, crossed, hidden, cotangent, gain, out_weight, gate_weight, up_weight, down_weight
):
    tokens, width = crossed.shape
    inner = gate_weight.shape[1]
    parts = lax.axis_size("narrow")
    part = inner // parts
    whole = lambda piece: whole_spec(piece.shape)
    fixed = lambda shape: pl.BlockSpec(shape, lambda step: (0,) * len(shape))
    parcel_shape = (BLOCKS, parcel.rows, LANES)
    return pl.pallas_call(
        lambda *refs: feed_both(parcel, parts, *refs),
        grid=(parts,),
        in_specs=[pl.BlockSpec(memory_space=pltpu.SMEM)]
        + [whole(crossed), whole(hidden), whole(cotangent), whole(gain), whole(out_weight)]
        + [pl.BlockSpec((width, part), lambda step: (0, step))] * 2
        + [pl.BlockSpec((part, width), lambda step: (step, 0))],
        out_specs=[fixed((tokens, width))] * 4
        + [fixed((1, width))]
        + [pl.BlockSpec(memory_space=pl.ANY)] * 2,
        out_shape=[
            jax.ShapeDtypeStruct((tokens, width), low),
            jax.ShapeDtypeStruct((tokens, width), high),
            jax.ShapeDtypeStruct((tokens, width), low),
            jax.ShapeDtypeStruct((tokens, width), low),
            jax.ShapeDtypeStruct((1, width), high),
            jax.ShapeDtypeStruct(parcel_shape, low),
            jax.ShapeDtypeStruct(parcel_shape, low),
        ],
        scratch_shapes=[
            pltpu.VMEM((tokens, width), high),
            pltpu.VMEM((tokens, width), low),
            pltpu.VMEM((width, tokens), low),
            pltpu.VMEM((tokens, width), high),
            pltpu.VMEM((tokens, width), high),
            pltpu.VMEM((tokens, width), low),
            pltpu.VMEM(parcel_shape, low),
            pltpu.VMEM(parcel_shape, low),
            pltpu.SemaphoreType.DMA((parts + 4,)),
        ],
        cost_estimate=cost("feed_both"),
        compiler_params=pltpu.CompilerParams(vmem_limit_bytes=vmem_bytes),
        name="feed_both",
    )(core, crossed, hidden, cotangent, gain, out_weight, gate_weight, up_weight, down_weight)


def lower_bits(sums):
    levels = lax.axis_size("items").bit_length() - 1
    for bit in range(levels - 4, -1, -1):
        mine = bit_of("items", bit)
        halves = [piece.reshape(2, piece.shape[0] // 2, piece.shape[1]) for piece in sums]
        sums = [pick(piece, mine) + swap(pick(piece, 1 - mine), "items", 1 << bit) for piece in halves]
    return sums


def memory_back(parcel, core_ref, *refs):
    wk_ref, wv_ref, away_ref, near_ref, kept_ref, sent_ref, total_ref = refs[6:]
    step = pl.program_id(0)
    steps = pl.num_programs(0)

    def block(rows_ref, grad_k_ref, grad_v_ref, grad_ref, first):
        grad_k, grad_v = grad_k_ref[...], grad_v_ref[...]
        grad_ref[...] = (rows_dot(grad_k, wk_ref[...]) + rows_dot(grad_v, wv_ref[...])).astype(low)
        width = grad_k.shape[1]
        rows = rows_ref[...].T
        parts = plain_dot(rows, grad_k), plain_dot(rows, grad_v)
        for job, part in enumerate(parts):
            columns = slice(job * width, (job + 1) * width)

            if first:

                @pl.when(step == 0)
                def _():
                    total_ref[:, columns] = part

                @pl.when(step > 0)
                def _():
                    total_ref[:, columns] += part

            else:
                total_ref[:, columns] += part

    @pl.when(step < steps // 2)
    def _():
        block(*refs[:3], away_ref, True)

    @pl.when(step >= steps // 2)
    def _():
        block(*refs[3:6], near_ref, False)

    @pl.when(step == steps - 1)
    def _():
        core = core_ref[0]
        for job, (_, width) in enumerate(parcel.shapes):
            total = total_ref[:, job * width : (job + 1) * width].astype(low)
            tiles = both_sides(total, core)
            count = len(tiles) // 2
            for at, product in enumerate(tiles):
                kind, tile = divmod(at, count)
                put_rows(parcel, job, product, tile, (kept_ref, sent_ref)[kind], 0)


def memory_back_call(parcel, core, far, near, wk, wv):
    total, width = far[0].shape
    half = total // 2
    name = "memory_back"
    first = lambda: pl.BlockSpec((half, width), lambda step: (jnp.minimum(step, 1), 0))
    second = lambda: pl.BlockSpec((half, width), lambda step: (jnp.maximum(step - 2, 0), 0))
    parcel_shape = (BLOCKS, parcel.rows, LANES)
    fixed = pl.BlockSpec(parcel_shape, lambda step: (0, 0, 0))
    return pl.pallas_call(
        lambda *refs: memory_back(parcel, *refs),
        grid=(4,),
        in_specs=[pl.BlockSpec(memory_space=pltpu.SMEM)]
        + [first() for _ in far]
        + [second() for _ in near]
        + [whole_spec(piece.shape) for piece in (wk, wv)],
        out_specs=[first(), second(), fixed, fixed],
        out_shape=[jax.ShapeDtypeStruct((total, width), low)] * 2
        + [jax.ShapeDtypeStruct(parcel_shape, low)] * 2,
        scratch_shapes=[pltpu.VMEM((width, 2 * width), high)],
        cost_estimate=cost(name),
        compiler_params=pltpu.CompilerParams(vmem_limit_bytes=vmem_bytes),
        name=name,
    )(core, *far, *near, wk, wv)


def land_memory(place_ref, *refs):
    for which in range(len(refs) - 1):

        @pl.when(pl.program_id(0) == which)
        def _():
            refs[-1][0] = refs[which][...].astype(high)


def land_call(place, pieces):
    rows, width = pieces[1].shape
    return pl.pallas_call(
        land_memory,
        out_shape=jax.ShapeDtypeStruct((len(pieces), rows, width), high),
        grid_spec=pltpu.PrefetchScalarGridSpec(
            num_scalar_prefetch=1,
            grid=(len(pieces),),
            in_specs=[
                pl.BlockSpec((rows, width), lambda step, _: (0, 0), pipeline_mode=pl.Buffered(1))
                for _ in pieces
            ],
            out_specs=pl.BlockSpec((1, rows, width), lambda step, place: (place[0] ^ step, 0, 0)),
        ),
        cost_estimate=cost("land_memory"),
        compiler_params=pltpu.CompilerParams(vmem_limit_bytes=vmem_bytes),
        name="land_memory",
    )(place, *pieces)


def two_heads(rows):
    first = lax.broadcasted_iota(jnp.int32, rows.shape, 1) < HD
    zero = jnp.zeros_like(rows)
    return jnp.concatenate([jnp.where(first, rows, zero), jnp.where(first, zero, rows)], axis=0)


def one_pair(stacked):
    half = stacked.shape[1] // 2
    first = lax.broadcasted_iota(jnp.int32, (stacked.shape[0], half), 0) < HD
    return jnp.where(first, stacked[:, :half], stacked[:, half:]).T


def attend_forward_kernel(causal, chunks, carried, last, live_ref, q_ref, k_ref, v_ref, *refs):
    before, refs = refs[:carried], refs[carried:]
    queries = two_heads(q_ref[...])
    wide = queries.shape[0]
    size = k_ref.shape[0] // chunks
    if not causal:
        lane = lax.broadcasted_iota(jnp.int32, queries.shape, 1)
        queries = jnp.concatenate([queries, jnp.where(lane == 0, 1.0, 0.0).astype(low)], axis=1)
    peaks, totals, mixes = [], [], []
    for chunk in range(chunks):
        here = slice(chunk * size, (chunk + 1) * size)
        keys = k_ref[here, :]
        if causal:
            scores = rows_dot(keys, queries)
            key = lax.broadcasted_iota(jnp.int32, (size, wide), 0) + chunk * size
            token = lax.broadcasted_iota(jnp.int32, (size, wide), 1)
            token = jnp.where(token >= wide // 2, token - wide // 2, token)
            scores = jnp.where(key <= token, scores, neg_big)
        else:
            key = lax.broadcasted_iota(jnp.int32, keys.shape, 0)
            lane = lax.broadcasted_iota(jnp.int32, keys.shape, 1)
            dead = jnp.where((lane == 0) & (key >= live_ref[chunk + (chunks if carried else 0)]), neg_big, 0.0).astype(low)
            scores = rows_dot(jnp.concatenate([keys, dead], axis=1), queries)
        peak = jnp.max(scores, axis=0, keepdims=True)
        weights = jnp.exp(scores - peak)
        total = jnp.sum(weights, axis=0, keepdims=True)
        weights = weights.astype(low)
        refs[0][0, here, :] = weights
        peaks.append(peak)
        totals.append(total)
        mixes.append(cols_dot(v_ref[here, :], weights))
    if carried:
        stats_in = before[1][0]
        count = chunks
        peaks = [stats_in[at : at + 1] for at in range(count)] + peaks
        totals = [stats_in[count + at : count + at + 1] for at in range(count)] + totals
    top = peaks[0]
    for peak in peaks[1:]:
        top = jnp.maximum(top, peak)
    scales = [jnp.exp(peak - top) for peak in peaks]
    mixed = sum(mix * scale for mix, scale in zip(mixes, scales[-chunks:]))
    if carried:
        earlier = peaks[0]
        for peak in peaks[1:chunks]:
            earlier = jnp.maximum(earlier, peak)
        mixed = mixed + before[0][0] * jnp.exp(earlier - top)
    if last:
        inverse = 1.0 / sum(total * scale for total, scale in zip(totals, scales))
        refs[1][...] = one_pair(mixed * inverse).astype(low)
        for at, scale in enumerate(scales):
            refs[2][0, at : at + 1, :] = scale * inverse
    else:
        refs[1][0] = mixed
        for at in range(chunks):
            refs[2][0, at : at + 1, :] = peaks[at]
            refs[2][0, chunks + at : chunks + at + 1, :] = totals[at]


def attend_forward(queries, keys, values, live, causal, chunks, name, last=True, before=()):
    tokens, width = queries.shape
    patches = keys.shape[0]
    pairs = width // LANES
    by_pair = lambda rows: pl.BlockSpec((rows, LANES), lambda pair, _: (0, pair))
    stack = lambda rows: pl.BlockSpec((1, rows, 2 * tokens), lambda pair, _: (pair, 0, 0))
    return pl.pallas_call(
        lambda *refs: attend_forward_kernel(causal, chunks, len(before), last, *refs),
        out_shape=(
            jax.ShapeDtypeStruct((pairs, patches, 2 * tokens), low),
            jax.ShapeDtypeStruct((tokens, width), low)
            if last
            else jax.ShapeDtypeStruct((pairs, LANES, 2 * tokens), high),
            jax.ShapeDtypeStruct((pairs, 8, 2 * tokens), high),
        ),
        grid_spec=pltpu.PrefetchScalarGridSpec(
            num_scalar_prefetch=1,
            grid=(pairs,),
            in_specs=[by_pair(tokens), by_pair(patches), by_pair(patches)]
            + [stack(piece.shape[1]) for piece in before],
            out_specs=[stack(patches), by_pair(tokens) if last else stack(LANES), stack(8)],
        ),
        cost_estimate=cost(name),
        compiler_params=pltpu.CompilerParams(vmem_limit_bytes=vmem_bytes),
        name=name,
    )(live, queries, keys, values, *before)


def attend_backward_kernel(
    chunks,
    offset,
    carried,
    last,
    weight_ref,
    inverse_ref,
    q_ref,
    k_ref,
    v_ref,
    mixed_ref,
    grad_mixed_ref,
    *refs,
):
    before, (grad_q_ref, grad_k_ref, grad_v_ref) = refs[:carried], refs[-3:]
    queries = two_heads(q_ref[...])
    grads = grad_mixed_ref[...].astype(high).T
    mixed = mixed_ref[...].astype(high).T
    first = lax.broadcasted_iota(jnp.int32, grads.shape, 0) < HD
    zero = jnp.zeros_like(grads)
    grads = jnp.concatenate([jnp.where(first, grads, zero), jnp.where(first, zero, grads)], axis=1)
    mixed = jnp.concatenate([mixed, mixed], axis=1)
    size = k_ref.shape[0] // chunks
    grad_q = jnp.zeros(grads.shape, high)
    for chunk in range(chunks):
        here = slice(chunk * size, (chunk + 1) * size)
        at = offset + chunk
        scaled = (grads * inverse_ref[0, at : at + 1, :]).astype(low)
        wide = scaled.astype(high)
        centre = jnp.sum(wide * mixed, axis=0, keepdims=True)
        rows = wide.T.astype(low)
        weights = weight_ref[0, here, :]
        grad_probs = plain_dot(v_ref[here, :], scaled)
        grad_scores = (weights.astype(high) * (grad_probs - centre)).astype(low)
        grad_v_ref[here, :] = plain_dot(weights, rows).astype(low)
        grad_k_ref[here, :] = plain_dot(grad_scores, queries).astype(low)
        grad_q = grad_q + cols_dot(k_ref[here, :], grad_scores)
    grad_q = one_pair(grad_q)
    if carried:
        grad_q = grad_q + before[0][...]
    grad_q_ref[...] = grad_q.astype(grad_q_ref.dtype)


def attend_backward(
    weights,
    inverse,
    queries,
    keys,
    values,
    mixed,
    grad_mixed,
    chunks,
    offset,
    name,
    last=True,
    before=(),
    pairs=None,
    filled=(),
):
    tokens, width = queries.shape
    patches = keys.shape[0]
    begin, end = pairs or (0, width // LANES)
    by_token = pl.BlockSpec((tokens, LANES), lambda pair: (0, pair + begin))
    by_patch = pl.BlockSpec((patches, LANES), lambda pair: (0, pair + begin))
    return pl.pallas_call(
        lambda *refs: attend_backward_kernel(chunks, offset, len(before), last, *refs),
        out_shape=(
            jax.ShapeDtypeStruct((tokens, width), low if last else high),
            jax.ShapeDtypeStruct((patches, width), low),
            jax.ShapeDtypeStruct((patches, width), low),
        ),
        grid=(end - begin,),
        in_specs=[
            pl.BlockSpec((1, patches, 2 * tokens), lambda pair: (pair + begin, 0, 0)),
            pl.BlockSpec((1, 8, 2 * tokens), lambda pair: (pair + begin, 0, 0)),
            by_token,
            by_patch,
            by_patch,
            by_token,
            by_token,
        ]
        + [by_token] * len(before)
        + [pl.BlockSpec(memory_space=pl.ANY)] * len(filled),
        out_specs=[by_token, by_patch, by_patch],
        input_output_aliases={7 + len(before) + which: which for which in range(len(filled))},
        cost_estimate=cost(name),
        compiler_params=pltpu.CompilerParams(vmem_limit_bytes=vmem_bytes),
        name=name,
    )(weights, inverse, queries, keys, values, mixed, grad_mixed, *before, *filled)


def swap(piece, axis_name, mask):
    size = lax.axis_size(axis_name)
    return lax.ppermute(piece, axis_name, [(place, place ^ mask) for place in range(size)])


def bit_of(axis_name, bit):
    return (lax.axis_index(axis_name) >> bit) & 1


def pick(piece, which):
    return lax.dynamic_index_in_dim(piece, which, 0, keepdims=False)


class Parcel:
    def __init__(self, shapes, extra=0):
        self.shapes = shapes
        self.heights = [height // BLOCKS for height, _ in shapes]
        self.plain = [width // 4 // LANES for _, width in shapes]
        self.at = []
        at = 0
        for (_, width), tiles, height in zip(shapes, self.plain, self.heights):
            self.at.append(at)
            at += tiles * height + (height // 2 if width // 4 % LANES else 0)
        self.extra = extra
        self.own = at + extra
        self.rows = 2 * self.own


def place(block):
    return (block & 1) * 4 + (block & 2) + (block >> 2)


def core_tiles(grad, core):
    quarter = grad.shape[1] // 4
    starts = [core * quarter, 2 * quarter + core * quarter]
    tiles = [
        grad[:, start + at : start + at + LANES]
        for start in starts
        for at in range(0, quarter - LANES + 1, LANES)
    ]
    rest = quarter % LANES
    if rest:
        tiles.append(
            jnp.concatenate(
                [grad[:, start + quarter - rest : start + quarter] for start in starts], axis=1
            )
        )
    return tiles


def both_sides(grad, core):
    first, second = core_tiles(grad, 0), core_tiles(grad, 1)
    own = [jnp.where(core == 0, one, other) for one, other in zip(first, second)]
    return own + [jnp.where(core == 0, other, one) for one, other in zip(first, second)]


def self_backward(
    parcel,
    core_ref,
    grad_q_two_ref,
    hidden_ref,
    grad_in_ref,
    gain_ref,
    cross_query_ref,
    out_weight_ref,
    feed_gain_ref,
    attended_ref,
    weight_ref,
    inverse_ref,
    q_ref,
    k_ref,
    v_ref,
    mixed_ref,
    wq_ref,
    wk_ref,
    wv_ref,
    normed_hbm_ref,
    next_normed_hbm_ref,
    tokens_hbm_ref,
    tokens_grad_ref,
    kept_ref,
    sent_ref,
    grad_hidden_ref,
    branch_ref,
    grad_mixed_ref,
    gains_ref,
    grads_ref,
    back_ref,
    late_ref,
    turned_ref,
    packed_ref,
    done_ref,
):
    pair = pl.program_id(0)
    pairs = pl.num_programs(0)
    late = [
        pltpu.make_async_copy(far_ref, late_ref.at[at], done_ref.at[at])
        for at, far_ref in enumerate((normed_hbm_ref, next_normed_hbm_ref, tokens_hbm_ref))
    ]

    @pl.when(pair == 0)
    def _():
        for copy in late:
            copy.start()
        to_rows, to_gain = norm_back(
            hidden_ref[...], gain_ref[1:2, :], rows_dot(grad_q_two_ref[...], cross_query_ref[...])
        )
        grad_hidden = grad_in_ref[...] + to_rows
        grad_hidden_ref[...] = grad_hidden
        branch = grad_hidden.astype(low)
        branch_ref[...] = branch
        grad_mixed_ref[...] = rows_dot(branch, out_weight_ref[...]).astype(low)
        gains_ref[1:2, :] = to_gain
        gains_ref[2:3, :] = feed_gain_ref[...]
        back_ref[...] = jnp.zeros_like(back_ref)

    here = pl.ds(pl.multiple_of(pair * LANES, LANES), LANES)
    views = [grads_ref.at[at, :, here] for at in range(3)]
    attend_backward_kernel(
        1,
        0,
        0,
        True,
        weight_ref,
        inverse_ref,
        q_ref,
        k_ref,
        v_ref,
        mixed_ref,
        grad_mixed_ref.at[:, here],
        *views,
    )
    grads = jnp.concatenate([view[...] for view in views], axis=1)
    weights = jnp.concatenate([wq_ref[...], wk_ref[...], wv_ref[...]], axis=1)
    back_ref[...] += rows_dot(grads, weights)

    @pl.when(pair == pairs - 1)
    def _():
        for copy in late:
            copy.wait()
        to_rows, to_gain = norm_back(late_ref[2].astype(high), gain_ref[0:1, :], back_ref[...])
        tokens_grad_ref[...] = (grad_hidden_ref[...] + to_rows).astype(low)
        gains_ref[0:1, :] = to_gain
        width = to_gain.shape[1]
        tiles = width // LANES
        packed_ref[...] = jnp.zeros_like(packed_ref)
        for gain in range(3):
            for tile in range(tiles):
                packed_ref[gain * tiles + tile : gain * tiles + tile + 1, :] = gains_ref[
                    gain : gain + 1, tile * LANES : (tile + 1) * LANES
                ]
        packed = packed_ref[...].astype(low)
        for out_ref in (kept_ref, sent_ref):
            for block in range(BLOCKS):
                for end in (parcel.own, parcel.rows):
                    out_ref[block, end - parcel.extra : end, :] = packed
        core = core_ref[0]
        jobs = (
            [(late_ref.at[0], grads_ref[at]) for at in range(3)]
            + [(late_ref.at[1], grad_q_two_ref[...])]
            + [(attended_ref, branch_ref[...])]
        )
        for job, (rows_ref, grad) in enumerate(jobs):
            if job in (0, 3, 4):
                turned_ref[...] = rows_ref[...].T
            tiles = both_sides(grad, core)
            count = len(tiles) // 2
            for begin in range(0, 2 * count, 2):
                product = plain_dot(
                    turned_ref[...], jnp.concatenate(tiles[begin : begin + 2], axis=1)
                ).astype(low)
                for slot in (0, 1):
                    kind, tile = divmod(begin + slot, count)
                    put_rows(parcel, job, product, tile, (kept_ref, sent_ref)[kind], slot)


def self_backward_call(
    parcel,
    core,
    grad_q_two,
    hidden,
    grad_in,
    gain,
    cross_query,
    out_weight,
    feed_gain,
    attended,
    weights,
    inverse,
    queries,
    keys,
    values,
    projections,
    late,
):
    rows, width = hidden.shape
    pairs = width // LANES
    columns = pl.BlockSpec((rows, LANES), lambda pair: (0, pair))
    stack = lambda height: pl.BlockSpec((1, height, 2 * rows), lambda pair: (pair, 0, 0))
    whole = (grad_q_two, hidden, grad_in, gain, cross_query, out_weight, feed_gain, attended)
    fixed = lambda shape: pl.BlockSpec(shape, lambda pair: (0,) * len(shape))
    parcel_shape = (BLOCKS, parcel.rows, LANES)
    return pl.pallas_call(
        lambda *refs: self_backward(parcel, *refs),
        grid=(pairs,),
        in_specs=[pl.BlockSpec(memory_space=pltpu.SMEM)]
        + [whole_spec(piece.shape) for piece in whole]
        + [stack(rows), stack(8), columns, columns, columns, columns]
        + [pl.BlockSpec((width, LANES), lambda pair: (0, pair))] * 3
        + [pl.BlockSpec(memory_space=pl.ANY)] * 3,
        out_specs=[fixed((rows, width)), whole_spec(parcel_shape), whole_spec(parcel_shape)],
        out_shape=[
            jax.ShapeDtypeStruct((rows, width), low),
            jax.ShapeDtypeStruct(parcel_shape, low),
            jax.ShapeDtypeStruct(parcel_shape, low),
        ],
        scratch_shapes=[
            pltpu.VMEM((rows, width), high),
            pltpu.VMEM((rows, width), low),
            pltpu.VMEM((rows, width), low),
            pltpu.VMEM((8, width), high),
            pltpu.VMEM((3, rows, width), low),
            pltpu.VMEM((rows, width), high),
            pltpu.VMEM((3, rows, width), low),
            pltpu.VMEM((width, rows), low),
            pltpu.VMEM((parcel.extra, LANES), high),
            pltpu.SemaphoreType.DMA((3,)),
        ],
        cost_estimate=cost("self_backward"),
        compiler_params=pltpu.CompilerParams(vmem_limit_bytes=vmem_bytes),
        name="self_backward",
    )(
        core,
        *whole,
        weights,
        inverse,
        queries,
        keys,
        values,
        attended,
        *projections,
        *late,
    )


def fold_one(mine_ref, kept_ref, received_ref, *out_refs):
    for which, out_ref in enumerate(out_refs):

        @pl.when(pl.program_id(0) == which)
        def _():
            total = kept_ref[0].astype(high) + received_ref[0].astype(high)
            out_ref[...] = total.astype(low)


def fold_one_call(name, mine, kept, received, view, shape, index):
    block = pl.BlockSpec((1, *shape), lambda step, mine: index(mine[0] ^ step))
    return pl.pallas_call(
        fold_one,
        grid_spec=pltpu.PrefetchScalarGridSpec(
            num_scalar_prefetch=1,
            grid=(4,),
            in_specs=[block, block],
            out_specs=[
                pl.BlockSpec(shape, lambda step, _: (0, 0, 0), pipeline_mode=pl.Buffered(1))
            ]
            * 4,
        ),
        out_shape=[jax.ShapeDtypeStruct(shape, low)] * 4,
        cost_estimate=cost(name),
        compiler_params=pltpu.CompilerParams(vmem_limit_bytes=vmem_bytes),
        name=name,
    )(mine, kept.reshape(view), received.reshape(view))


def sum_of(refs):
    first, second, third, fourth = [ref[...].astype(high) for ref in refs]
    return (first + second) + (third + fourth)


def fold_two(parcel, with_x, first_ref, second_ref, third_ref, fourth_ref, out_ref):
    total = sum_of((first_ref, second_ref, third_ref, fourth_ref)).astype(low)
    if with_x:
        out_ref[...] = total
    else:
        for which in range(4):
            begin = (which & 1) * parcel.own
            out_ref[which] = total[which >> 1, begin : begin + parcel.own, :]


def fold_end(parcel, parts_ref, *outs):
    total = sum_of([parts_ref.at[which] for which in range(4)])
    for job, rows in enumerate(parcel.heights):
        at = parcel.at[job]
        for tile in range(parcel.plain[job]):
            outs[job][:, tile * LANES : (tile + 1) * LANES] = total[at : at + rows]
            at += rows
        begin = parcel.plain[job] * LANES
        rest = outs[job].shape[1] - begin
        if rest:
            outs[job][: rows // 2, begin:] = total[at : at + rows // 2, :rest]
            outs[job][rows // 2 :, begin:] = total[at : at + rows // 2, rest:]
    if parcel.extra:
        outs[-1][...] = total[-parcel.extra :]


class Travel:
    def __init__(self, parcel, kept, sent, name, with_x):
        self.parcel = parcel
        self.name = name
        self.kept = kept
        self.received = swap(sent, "narrow", 1)
        self.top = lax.axis_size("items").bit_length() - 4
        self.with_x = with_x

    def joint(self, up, side):
        narrow = lax.axis_size("narrow")
        return [
            (place, ((place // narrow) ^ up) * narrow + ((place % narrow) ^ side))
            for place in range(lax.axis_size("items") * narrow)
        ]

    def fold_one(self, *earlier):
        kept, received = lax.optimization_barrier((self.kept, self.received, *earlier))[:2]
        rows, top = self.parcel.rows, self.top
        if self.with_x:
            mine = bit_of("items", top) * 2 + bit_of("narrow", 1)
            view, shape = (2, 4, rows, LANES), (4, self.parcel.own, LANES)
            partners = [(0, 2), (1 << top, 0), (1 << top, 2)]
            index = lambda part: (part >> 1, 0, part & 1, 0)
        else:
            mine = bit_of("items", top) * 2 + bit_of("items", top + 1)
            view, shape = (4, 2, rows, LANES), (2, rows, LANES)
            partners = [(2 << top, 0), (1 << top, 0), (3 << top, 0)]
            index = lambda part: (part, 0, 0, 0)
        parts = fold_one_call(
            self.name + "_one", mine.reshape(1), kept, received, view, shape, index
        )
        self.parts = [parts[0]] + [
            lax.ppermute(part, ("items", "narrow"), self.joint(*partner))
            for part, partner in zip(parts[1:], partners)
        ]
        return parts[0]

    def fold_two(self, *earlier):
        parts = lax.optimization_barrier((*self.parts, *earlier))[:4]
        parcel = self.parcel
        (parts,) = one_step_call(
            lambda *refs: fold_two(parcel, self.with_x, *refs),
            self.name + "_two",
            list(parts),
            [((4, parcel.own, LANES), low)],
        )
        far = 4 << self.top
        first, second = ((2 << self.top, 0), (far, 0)) if self.with_x else ((far, 0), (0, 2))
        narrow = lax.axis_size("narrow")
        clear = first[0] | second[0]
        side = first[1] | second[1]
        groups = [
            [
                (item | one[0] | two[0]) * narrow + (other | one[1] | two[1])
                for one in ((0, 0), first)
                for two in ((0, 0), second)
            ]
            for item in range(lax.axis_size("items"))
            for other in range(narrow)
            if not item & clear and not other & side
        ]
        self.parts = parts
        self.groups = groups
        return parts

    def send(self, *earlier):
        parts = lax.optimization_barrier((self.parts, *earlier))[0]
        self.parts = lax.all_to_all(
            parts, ("items", "narrow"), 0, 0, axis_index_groups=self.groups, tiled=True
        )

    def end(self, *earlier):
        parts = lax.optimization_barrier((self.parts, *earlier))[0]
        parcel = self.parcel
        outs = [((height // BLOCKS, width // 4), high) for height, width in parcel.shapes]
        outs += [((parcel.extra, LANES), high)] if parcel.extra else []
        outs = list(
            one_step_call(
                lambda *refs: fold_end(parcel, *refs),
                self.name + "_end",
                [parts],
                outs,
            )
        )
        count = len(parcel.shapes)
        extras = outs[count:]
        for bit in range(self.top, 0, -1):
            extras = [piece + swap(piece, "items", 1 << (bit - 1)) for piece in extras]
        return list(lower_bits(outs[:count])) + extras


def exchange(piece):
    return lax.all_to_all(piece, "narrow", split_axis=0, concat_axis=0, tiled=True)


def body(
    tokens,
    memory,
    mem_count,
    cotangent,
    gain_self,
    self_query,
    self_key,
    self_value,
    self_out,
    gain_cross,
    cross_query,
    cross_key,
    cross_value,
    cross_out,
    gain_feed,
    gate_weight,
    up_weight,
    down_weight,
):
    width = tokens.shape[2]
    inner = gate_weight.shape[1]
    gains_in = jnp.stack([gain_self, gain_cross, gain_feed])
    parts = lax.axis_size("narrow")
    mine = lax.axis_index("narrow")
    token_rows = exchange(tokens).reshape(-1, width)
    own_memory, *away_memory = [pick(memory, mine ^ which) for which in range(parts)]
    pieces = [own_memory] + [
        swap(piece, "narrow", which + 1) for which, piece in enumerate(away_memory)
    ]
    cotangent_rows = exchange(cotangent).reshape(-1, width)
    count = pick(mem_count, mine)
    local_mem = memory.shape[1]
    live = count - local_mem * (mine ^ jnp.arange(parts, dtype=jnp.int32))
    kinds = [((2 * local_mem, width), low)] * 3
    near_rows, near_keys, near_values = one_step_call(
        enter_memory,
        "enter_memory_near",
        [pieces[0], pieces[1], cross_key, cross_value],
        kinds,
    )
    (
        normed_one,
        query_one,
        key_one,
        value_one,
        weights_one,
        attended,
        inverse_one,
        hidden_one,
        normed_two,
        query_two,
    ) = self_forward_call(
        after(token_rows, near_keys),
        gains_in,
        cross_query,
        self_query,
        self_key,
        self_value,
        self_out,
    )
    near_weights, near_mixed, near_stats = attend_forward(
        query_two, near_keys, near_values, live, False, 2, "cross_forward_near", False
    )
    far_rows, far_keys, far_values = one_step_call(
        enter_memory,
        "enter_memory_far",
        [after(pieces[2], near_stats), pieces[3], cross_key, cross_value],
        kinds,
    )
    far_weights, crossed, inverse_two = attend_forward(
        query_two,
        far_keys,
        far_values,
        live,
        False,
        2,
        "cross_forward_far",
        True,
        (near_mixed, near_stats),
    )
    square = (width, width)
    feed_parcel = Parcel([(width, inner), (width, inner), (inner, width), square])
    result, grad_hidden_two, branch_two, grad_crossed, grad_gain_feed, *feed_parts = feed_call(
        feed_parcel,
        bit_of("narrow", 0).reshape(1),
        crossed,
        hidden_one,
        cotangent_rows,
        gains_in,
        cross_out,
        gate_weight,
        up_weight,
        down_weight,
    )
    feed_trip = Travel(feed_parcel, *feed_parts, "feed_weights", True)
    result = exchange(result.reshape(tokens.shape))
    far = ()
    ready = feed_trip.kept
    for pairs in ((0, 3), (3, 6)):
        far = attend_backward(
            far_weights,
            inverse_two,
            query_two,
            far_keys,
            far_values,
            crossed,
            after(grad_crossed, ready),
            2,
            2,
            "cross_backward_far_a" if pairs[0] == 0 else "cross_backward_far_b",
            False,
            pairs=pairs,
            filled=far,
        )
        ready = feed_trip.fold_one(far[0]) if pairs[0] == 0 else far[0]
    far_grad_q, far_grad_k, far_grad_v = far
    grad_query_two, near_grad_k, near_grad_v = attend_backward(
        near_weights,
        inverse_two,
        query_two,
        near_keys,
        near_values,
        crossed,
        after(grad_crossed, result),
        2,
        0,
        "cross_backward_near",
        True,
        (far_grad_q,),
    )
    extra = -(-3 * width // LANES // 16) * 16
    self_parcel = Parcel([square] * 5, extra)
    tokens_grad, *self_parts = self_backward_call(
        self_parcel,
        bit_of("narrow", 0).reshape(1),
        grad_query_two,
        hidden_one,
        grad_hidden_two,
        gains_in,
        cross_query,
        self_out,
        grad_gain_feed,
        attended,
        weights_one,
        inverse_one,
        query_one,
        key_one,
        value_one,
        [self_query, self_key, self_value],
        [normed_one, normed_two, token_rows],
    )
    self_trip = Travel(self_parcel, *self_parts, "self_weights", True)
    tokens_grad = exchange(tokens_grad.reshape(tokens.shape))
    ready = feed_trip.fold_two(self_parts[0])
    feed_trip.send()
    ready = self_trip.fold_one(ready)
    cross_parcel = Parcel([square] * 2)
    grad_away, grad_near, *cross_parts = memory_back_call(
        cross_parcel,
        bit_of("narrow", 0).reshape(1),
        [after(far_rows, ready, tokens_grad), far_grad_k, far_grad_v],
        [near_rows, near_grad_k, near_grad_v],
        cross_key,
        cross_value,
    )
    landed_away = swap(grad_away, "narrow", 2)
    cross_trip = Travel(cross_parcel, *cross_parts, "cross_weights", False)
    tokens_grad = tokens_grad.astype(high)
    ready = self_trip.fold_two(grad_away)
    self_trip.send()
    ready = cross_trip.fold_one(ready)
    gate_sum, up_sum, down_sum, cross_out_sum = feed_trip.end(ready)
    ready = gate_sum
    ready = cross_trip.fold_two(ready)
    cross_trip.send()
    grad_near, landed_away = lax.optimization_barrier((grad_near, landed_away, ready))[:2]
    landed_core = swap(grad_near[local_mem:], "narrow", 1)
    landed_far = swap(landed_away[local_mem:], "narrow", 1)
    self_query_sum, self_key_sum, self_value_sum, cross_query_sum, self_out_sum, gains = (
        self_trip.end(ready)
    )
    memory_grad = land_call(
        mine.reshape(1),
        [after(grad_near, self_query_sum), landed_core, landed_away, landed_far],
    )
    cross_key_sum, cross_value_sum = cross_trip.end(memory_grad)
    gains = gains[: 3 * width // LANES].reshape(3, width)
    return (
        result,
        tokens_grad,
        memory_grad,
        gains[0],
        self_query_sum,
        self_key_sum,
        self_value_sum,
        self_out_sum,
        gains[1],
        cross_query_sum,
        cross_key_sum,
        cross_value_sum,
        cross_out_sum,
        gains[2],
        gate_sum,
        up_sum,
        down_sum,
    )


def solution(mesh):
    in_specs = (
        P("items", "narrow", None),
        P("items", "narrow", None),
        P("items"),
        P("items", "narrow", None),
        P(),
        P(),
        P(),
        P(),
        P(),
        P(),
        P(),
        P(),
        P(),
        P(),
        P(),
        P(),
        P(),
        P(),
    )
    out_specs = (
        P("items", "narrow", None),
        P("items", "narrow", None),
        P("items", "narrow", None),
        P(),
        P("items", "narrow"),
        P("items", "narrow"),
        P("items", "narrow"),
        P("items", "narrow"),
        P(),
        P("items", "narrow"),
        P("items", "narrow"),
        P("items", "narrow"),
        P("items", "narrow"),
        P(),
        P("items", "narrow"),
        P("items", "narrow"),
        P("items", "narrow"),
    )
    return jax.shard_map(body, mesh=mesh, in_specs=in_specs, out_specs=out_specs, check_vma=False)
```

```python
import jax
import jax.numpy as jnp
from jax import lax
from jax.experimental import pallas as pl
from jax.experimental.pallas import tpu as pltpu
from jax.sharding import PartitionSpec as P

HD = 64
LANES = 128
BLOCKS = 8

eps = 1e-06
neg_big = -1e30
smallest_total = 1e-25
gelu_scale = 0.7978845608028654
gelu_cubic = 0.044715
low = jnp.bfloat16
high = jnp.float32
vmem_bytes = 60 * 1024 * 1024


def rows_dot(left_side, right_side):
    return lax.dot_general(
        left_side, right_side, (((1,), (1,)), ((), ())), preferred_element_type=high
    )


def cols_dot(left_side, right_side):
    return lax.dot_general(
        left_side, right_side, (((0,), (0,)), ((), ())), preferred_element_type=high
    )


def plain_dot(left_side, right_side):
    return jnp.dot(left_side, right_side, preferred_element_type=high)


def inverse_scale(hidden):
    return lax.rsqrt(jnp.mean(hidden * hidden, axis=-1, keepdims=True) + eps)


def norm_back(hidden, gain, grad):
    scale = inverse_scale(hidden)
    weighted = gain * grad
    middle = jnp.mean(weighted * hidden, axis=-1, keepdims=True)
    to_rows = scale * (weighted - hidden * (scale * scale * middle))
    to_gain = jnp.sum(grad * hidden * scale, axis=0, keepdims=True)
    return to_rows, to_gain


call_time = {
    "enter_memory_near": 2,
    "self_forward": 8,
    "cross_forward_near": 6,
    "enter_memory_far": 2,
    "cross_forward_far": 6,
    "cross_backward_far_b": 100,
    "feed_weights_two": 100,
    "memory_back": 100,
    "self_weights_two": 100,
    "self_weights_end": 100,
}


def cost(name):
    return pl.CostEstimate(
        flops=int(call_time.get(name, 0.001) * 1.15e9), bytes_accessed=1, transcendentals=0
    )


def after(piece, *earlier):
    return lax.optimization_barrier((piece, *earlier))[0]


def row_spec(rows, width):
    return pl.BlockSpec((rows, width), lambda step: (step, 0))


def whole_spec(shape):
    return pl.BlockSpec(
        shape, lambda step: (0,) * len(shape), pipeline_mode=pl.Buffered(1)
    )


def self_forward(
    tokens_ref,
    gains_ref,
    next_query_ref,
    wq_ref,
    wk_ref,
    wv_ref,
    out_ref,
    normed_ref,
    q_ref,
    k_ref,
    v_ref,
    weight_ref,
    mixed_ref,
    inverse_ref,
    hidden_ref,
    next_normed_ref,
    next_q_ref,
    stats_ref,
    part_ref,
):
    pair = pl.program_id(0)

    @pl.when(pair == 0)
    def _():
        hidden = tokens_ref[...].astype(high)
        normed_ref[...] = (hidden * inverse_scale(hidden) * gains_ref[0:1, :]).astype(low)
        hidden_ref[...] = hidden

    weights = jnp.concatenate([wq_ref[...], wk_ref[...], wv_ref[...]], axis=1)
    projected = plain_dot(normed_ref[...], weights).astype(low)
    for at, head_ref in enumerate((q_ref, k_ref, v_ref)):
        head_ref[...] = projected[:, at * LANES : (at + 1) * LANES]
    attend_forward_kernel(
        True,
        1,
        0,
        True,
        None,
        q_ref,
        k_ref,
        v_ref,
        weight_ref,
        mixed_ref,
        inverse_ref,
        stats_ref,
        part_ref,
    )
    hidden_ref[...] += plain_dot(mixed_ref[...], out_ref[...])

    @pl.when(pair == pl.num_programs(0) - 1)
    def _():
        hidden = hidden_ref[...]
        normed = (hidden * inverse_scale(hidden) * gains_ref[1:2, :]).astype(low)
        next_normed_ref[...] = normed
        next_q_ref[...] = plain_dot(normed, next_query_ref[...]).astype(low)


def self_forward_call(tokens, gains, next_query, wq, wk, wv, out_weight):
    rows, width = tokens.shape
    pairs = width // LANES
    whole = pl.BlockSpec((rows, width), lambda pair: (0, 0))
    columns = pl.BlockSpec((rows, LANES), lambda pair: (0, pair))
    stack = lambda height: pl.BlockSpec((1, height, 2 * rows), lambda pair: (pair, 0, 0))
    plain = jax.ShapeDtypeStruct((rows, width), low)
    return pl.pallas_call(
        self_forward,
        grid=(pairs,),
        in_specs=[whole_spec(piece.shape) for piece in (tokens, gains, next_query)]
        + [pl.BlockSpec((width, LANES), lambda pair: (0, pair))] * 3
        + [pl.BlockSpec((LANES, width), lambda pair: (pair, 0))],
        out_specs=[whole, columns, columns, columns, stack(rows), columns, stack(8)] + [whole] * 3,
        out_shape=[
            plain,
            plain,
            plain,
            plain,
            jax.ShapeDtypeStruct((pairs, rows, 2 * rows), low),
            plain,
            jax.ShapeDtypeStruct((pairs, 8, 2 * rows), high),
            jax.ShapeDtypeStruct((rows, width), high),
            plain,
            plain,
        ],
        scratch_shapes=[
            pltpu.VMEM((2, 2 * rows), high),
            pltpu.VMEM((1, LANES, 2 * rows), high),
        ],
        cost_estimate=cost("self_forward"),
        compiler_params=pltpu.CompilerParams(vmem_limit_bytes=vmem_bytes),
        name="self_forward",
    )(tokens, gains, next_query, wq, wk, wv, out_weight)


def enter_memory(first_ref, second_ref, wk_ref, wv_ref, rows_ref, k_ref, v_ref):
    half = first_ref.shape[0]
    for at, piece_ref in ((0, first_ref), (half, second_ref)):
        rows = piece_ref[...]
        rows_ref[at : at + half, :] = rows
        k_ref[at : at + half, :] = plain_dot(rows, wk_ref[...]).astype(low)
        v_ref[at : at + half, :] = plain_dot(rows, wv_ref[...]).astype(low)


def one_step_call(kernel, name, ins, outs, scratch=()):
    vmem = pl.BlockSpec(memory_space=pltpu.VMEM)
    smem = pl.BlockSpec(memory_space=pltpu.SMEM)
    return pl.pallas_call(
        kernel,
        in_specs=[smem if piece.dtype == jnp.int32 else vmem for piece in ins],
        out_specs=[vmem] * len(outs),
        out_shape=[jax.ShapeDtypeStruct(shape, kind) for shape, kind in outs],
        scratch_shapes=list(scratch),
        cost_estimate=cost(name),
        compiler_params=pltpu.CompilerParams(vmem_limit_bytes=vmem_bytes),
        name=name,
    )(*ins)


def put_block(parcel, job, tile, rows_of, out_ref, spot):
    plain, rows = parcel.plain[job], parcel.heights[job]
    if tile < 2 * plain:
        at = (tile // plain) * parcel.own + parcel.at[job] + (tile % plain) * rows
        out_ref[spot, at : at + rows, :] = rows_of
    else:
        half = LANES // 2
        for side in (0, 1):
            at = side * parcel.own + parcel.at[job] + plain * rows
            lanes = slice(side * half, (side + 1) * half)
            out_ref[spot, at : at + rows // 2, :] = jnp.concatenate(
                [rows_of[: rows // 2, lanes], rows_of[rows // 2 :, lanes]], axis=1
            )


def put_rows(parcel, job, product, tile, out_ref, slot):
    rows = parcel.heights[job]
    for block in range(BLOCKS):
        put_block(
            parcel,
            job,
            tile,
            product[block * rows : (block + 1) * rows, slot * LANES : (slot + 1) * LANES],
            out_ref,
            place(block),
        )


def feed_both(
    parcel,
    parts,
    core_ref,
    crossed_ref,
    hidden_in_ref,
    cotangent_ref,
    gain_ref,
    out_ref,
    gate_ref,
    up_ref,
    down_ref,
    result_ref,
    grad_hidden_ref,
    branch_ref,
    grad_crossed_ref,
    grad_gain_ref,
    kept_out_ref,
    sent_out_ref,
    hidden_ref,
    normed_ref,
    turned_ref,
    sum_ref,
    back_ref,
    sides_ref,
    kept_ref,
    sent_ref,
    done_ref,
):
    step = pl.program_id(0)
    core = core_ref[0]
    gain = gain_ref[2:3, :]

    @pl.when(step == 0)
    def _():
        hidden = hidden_in_ref[...] + plain_dot(crossed_ref[...], out_ref[...])
        hidden_ref[...] = hidden
        normed = (hidden * inverse_scale(hidden) * gain).astype(low)
        normed_ref[...] = normed
        turned_ref[...] = normed.T
        sum_ref[...] = hidden
        back_ref[...] = jnp.zeros_like(back_ref)
        sides_ref[...] = jnp.concatenate(both_sides(cotangent_ref[...], core), axis=1)

    inner = parcel.at[2]

    def copies(side_ref, out_ref, begin, rows, slot):
        here = (slice(None), pl.ds(begin, rows), slice(None))
        return pltpu.make_async_copy(side_ref.at[here], out_ref.at[here], done_ref.at[slot])

    normed = normed_ref[...]
    cotangent = cotangent_ref[...]
    turned = turned_ref[...]
    sides = sides_ref[...]
    part = gate_ref.shape[1]
    size = part
    output, back_sum = sum_ref[...], back_ref[...]
    grads, mixes = [], []
    for begin in range(0, part, size):
        here = slice(begin, begin + size)
        gate = plain_dot(normed, gate_ref[:, here])
        up = plain_dot(normed, up_ref[:, here])
        back = rows_dot(cotangent, down_ref[here, :])
        square = gate * gate
        curve = jnp.tanh(gelu_scale * (gate + gelu_cubic * gate * square))
        half = 0.5 * (1.0 + curve)
        bent = gate * half
        slope = half + 0.5 * gate * (1.0 - curve * curve) * (
            gelu_scale * (1.0 + 3.0 * gelu_cubic * square)
        )
        mixed = (bent * up).astype(low)
        grad_gate = (back * up * slope).astype(low)
        grad_up = (back * bent).astype(low)
        output = output + plain_dot(mixed, down_ref[here, :])
        back_sum = (
            back_sum
            + rows_dot(grad_gate, gate_ref[:, here])
            + rows_dot(grad_up, up_ref[:, here])
        )
        mixes.append(mixed)
        grads.append((grad_gate, grad_up))
    sum_ref[...] = output
    back_ref[...] = back_sum
    side = (step >> 1) * parcel.own
    for kind, (side_ref, target_ref) in enumerate(
        ((kept_ref, kept_out_ref), (sent_ref, sent_out_ref))
    ):

        @pl.when(((step & 1) ^ core) == kind)
        def _():
            for job in (0, 1):
                rows = parcel.heights[job]
                for which, pair in enumerate(grads):
                    product = plain_dot(turned, pair[job]).astype(low)
                    for tile in range(size // LANES):
                        at = side + parcel.at[job] + (which * size // LANES + tile) * rows
                        at = pl.multiple_of(at, 16)
                        for block in range(BLOCKS):
                            side_ref[place(block), pl.ds(at, rows), :] = product[
                                block * rows : (block + 1) * rows, tile * LANES : (tile + 1) * LANES
                            ]
            copies(side_ref, target_ref, pl.multiple_of(side, 16), inner, step).start()

    rows = parcel.heights[2]
    tiles = sides.shape[1] // LANES // 2
    for which, mixed in enumerate(mixes):
        product = cols_dot(mixed, sides).astype(low)
        here = product.shape[0] // rows
        for kind, side_ref in enumerate((kept_ref, sent_ref)):
            for tile in range(tiles):
                lane = (kind * tiles + tile) * LANES
                for block in range(here):
                    put_block(
                        parcel,
                        2,
                        tile,
                        product[block * rows : (block + 1) * rows, lane : lane + LANES],
                        side_ref,
                        place(step * here + block),
                    )

    @pl.when(step == pl.num_programs(0) - 1)
    def _():
        hidden = hidden_ref[...]
        result_ref[...] = sum_ref[...].astype(low)
        to_rows, to_gain = norm_back(hidden, gain, back_ref[...])
        grad_gain_ref[...] = to_gain
        grad_hidden = cotangent.astype(high) + to_rows
        grad_hidden_ref[...] = grad_hidden
        branch = grad_hidden.astype(low)
        branch_ref[...] = branch
        grad_crossed_ref[...] = rows_dot(branch, out_ref[...]).astype(low)
        sides = jnp.concatenate(both_sides(branch, core), axis=1)
        product = cols_dot(crossed_ref[...], sides).astype(low)
        for kind, side_ref in enumerate((kept_ref, sent_ref)):
            for tile in range(tiles):
                put_rows(parcel, 3, product, tile, side_ref, kind * tiles + tile)
        spans = ((inner, parcel.own), (parcel.own + inner, parcel.rows))
        last = [
            copies(side_ref, target_ref, begin, end - begin, parts + 2 * kind + which)
            for kind, (side_ref, target_ref) in enumerate(
                ((kept_ref, kept_out_ref), (sent_ref, sent_out_ref))
            )
            for which, (begin, end) in enumerate(spans)
        ]
        for copy in last:
            copy.start()
        for slot in range(parts):
            copies(kept_ref, kept_out_ref, 0, inner, slot).wait()
        for copy in last:
            copy.wait()


def feed_call(
    parcel, core, crossed, hidden, cotangent, gain, out_weight, gate_weight, up_weight, down_weight
):
    tokens, width = crossed.shape
    inner = gate_weight.shape[1]
    parts = lax.axis_size("narrow")
    part = inner // parts
    whole = lambda piece: whole_spec(piece.shape)
    fixed = lambda shape: pl.BlockSpec(shape, lambda step: (0,) * len(shape))
    parcel_shape = (BLOCKS, parcel.rows, LANES)
    return pl.pallas_call(
        lambda *refs: feed_both(parcel, parts, *refs),
        grid=(parts,),
        in_specs=[pl.BlockSpec(memory_space=pltpu.SMEM)]
        + [whole(crossed), whole(hidden), whole(cotangent), whole(gain), whole(out_weight)]
        + [pl.BlockSpec((width, part), lambda step: (0, step))] * 2
        + [pl.BlockSpec((part, width), lambda step: (step, 0))],
        out_specs=[fixed((tokens, width))] * 4
        + [fixed((1, width))]
        + [pl.BlockSpec(memory_space=pl.ANY)] * 2,
        out_shape=[
            jax.ShapeDtypeStruct((tokens, width), low),
            jax.ShapeDtypeStruct((tokens, width), high),
            jax.ShapeDtypeStruct((tokens, width), low),
            jax.ShapeDtypeStruct((tokens, width), low),
            jax.ShapeDtypeStruct((1, width), high),
            jax.ShapeDtypeStruct(parcel_shape, low),
            jax.ShapeDtypeStruct(parcel_shape, low),
        ],
        scratch_shapes=[
            pltpu.VMEM((tokens, width), high),
            pltpu.VMEM((tokens, width), low),
            pltpu.VMEM((width, tokens), low),
            pltpu.VMEM((tokens, width), high),
            pltpu.VMEM((tokens, width), high),
            pltpu.VMEM((tokens, width), low),
            pltpu.VMEM(parcel_shape, low),
            pltpu.VMEM(parcel_shape, low),
            pltpu.SemaphoreType.DMA((parts + 4,)),
        ],
        cost_estimate=cost("feed_both"),
        compiler_params=pltpu.CompilerParams(vmem_limit_bytes=vmem_bytes),
        name="feed_both",
    )(core, crossed, hidden, cotangent, gain, out_weight, gate_weight, up_weight, down_weight)


def lower_bits(sums):
    levels = lax.axis_size("items").bit_length() - 1
    for bit in range(levels - 4, -1, -1):
        mine = bit_of("items", bit)
        halves = [piece.reshape(2, piece.shape[0] // 2, piece.shape[1]) for piece in sums]
        sums = [pick(piece, mine) + swap(pick(piece, 1 - mine), "items", 1 << bit) for piece in halves]
    return sums


def memory_back(parcel, core_ref, *refs):
    wk_ref, wv_ref, away_ref, near_ref, kept_ref, sent_ref, total_ref = refs[6:]
    step = pl.program_id(0)
    steps = pl.num_programs(0)

    def block(rows_ref, grad_k_ref, grad_v_ref, grad_ref, first):
        grad_k, grad_v = grad_k_ref[...], grad_v_ref[...]
        grad_ref[...] = (rows_dot(grad_k, wk_ref[...]) + rows_dot(grad_v, wv_ref[...])).astype(low)
        width = grad_k.shape[1]
        rows = rows_ref[...].T
        parts = plain_dot(rows, grad_k), plain_dot(rows, grad_v)
        for job, part in enumerate(parts):
            columns = slice(job * width, (job + 1) * width)

            if first:

                @pl.when(step == 0)
                def _():
                    total_ref[:, columns] = part

                @pl.when(step > 0)
                def _():
                    total_ref[:, columns] += part

            else:
                total_ref[:, columns] += part

    @pl.when(step < steps // 2)
    def _():
        block(*refs[:3], away_ref, True)

    @pl.when(step >= steps // 2)
    def _():
        block(*refs[3:6], near_ref, False)

    @pl.when(step == steps - 1)
    def _():
        core = core_ref[0]
        for job, (_, width) in enumerate(parcel.shapes):
            total = total_ref[:, job * width : (job + 1) * width].astype(low)
            tiles = both_sides(total, core)
            count = len(tiles) // 2
            for at, product in enumerate(tiles):
                kind, tile = divmod(at, count)
                put_rows(parcel, job, product, tile, (kept_ref, sent_ref)[kind], 0)


def memory_back_call(parcel, core, far, near, wk, wv):
    total, width = far[0].shape
    half = total // 2
    name = "memory_back"
    first = lambda: pl.BlockSpec((half, width), lambda step: (jnp.minimum(step, 1), 0))
    second = lambda: pl.BlockSpec((half, width), lambda step: (jnp.maximum(step - 2, 0), 0))
    parcel_shape = (BLOCKS, parcel.rows, LANES)
    fixed = pl.BlockSpec(parcel_shape, lambda step: (0, 0, 0))
    return pl.pallas_call(
        lambda *refs: memory_back(parcel, *refs),
        grid=(4,),
        in_specs=[pl.BlockSpec(memory_space=pltpu.SMEM)]
        + [first() for _ in far]
        + [second() for _ in near]
        + [whole_spec(piece.shape) for piece in (wk, wv)],
        out_specs=[first(), second(), fixed, fixed],
        out_shape=[jax.ShapeDtypeStruct((total, width), low)] * 2
        + [jax.ShapeDtypeStruct(parcel_shape, low)] * 2,
        scratch_shapes=[pltpu.VMEM((width, 2 * width), high)],
        cost_estimate=cost(name),
        compiler_params=pltpu.CompilerParams(vmem_limit_bytes=vmem_bytes),
        name=name,
    )(core, *far, *near, wk, wv)


def land_memory(place_ref, *refs):
    for which in range(len(refs) - 1):

        @pl.when(pl.program_id(0) == which)
        def _():
            refs[-1][0] = refs[which][...].astype(high)


def land_call(place, pieces):
    rows, width = pieces[1].shape
    return pl.pallas_call(
        land_memory,
        out_shape=jax.ShapeDtypeStruct((len(pieces), rows, width), high),
        grid_spec=pltpu.PrefetchScalarGridSpec(
            num_scalar_prefetch=1,
            grid=(len(pieces),),
            in_specs=[
                pl.BlockSpec((rows, width), lambda step, _: (0, 0), pipeline_mode=pl.Buffered(1))
                for _ in pieces
            ],
            out_specs=pl.BlockSpec((1, rows, width), lambda step, place: (place[0] ^ step, 0, 0)),
        ),
        cost_estimate=cost("land_memory"),
        compiler_params=pltpu.CompilerParams(vmem_limit_bytes=vmem_bytes),
        name="land_memory",
    )(place, *pieces)


def two_heads(rows):
    first = lax.broadcasted_iota(jnp.int32, rows.shape, 1) < HD
    zero = jnp.zeros_like(rows)
    return jnp.concatenate([jnp.where(first, rows, zero), jnp.where(first, zero, rows)], axis=0)


def one_pair(stacked):
    half = stacked.shape[1] // 2
    first = lax.broadcasted_iota(jnp.int32, (stacked.shape[0], half), 0) < HD
    return jnp.where(first, stacked[:, :half], stacked[:, half:]).T


def attend_forward_kernel(causal, chunks, carried, last, live_ref, q_ref, k_ref, v_ref, *refs):
    before, refs = refs[:carried], refs[carried:]
    queries = two_heads(q_ref[...])
    wide = queries.shape[0]
    size = k_ref.shape[0] // chunks

    def weigh(here, scores, peak):
        weights = jnp.exp(scores - peak)
        total = jnp.sum(weights, axis=0, keepdims=True)
        weights = weights.astype(low)
        refs[0][0, here, :] = weights
        return total, cols_dot(v_ref[here, :], weights)

    stats_ref, mixed_ref = refs[-2:]
    squares = queries.astype(high)
    squares = (squares * squares).astype(low)
    lengths = rows_dot(jnp.ones((8, LANES), low), squares)[:1]
    if not causal:
        lane = lax.broadcasted_iota(jnp.int32, queries.shape, 1)
        queries = jnp.concatenate([queries, jnp.where(lane == 0, 1.0, 0.0).astype(low)], axis=1)
    for chunk in range(chunks):
        here = slice(chunk * size, (chunk + 1) * size)
        live = size if causal else live_ref[chunk + (chunks if carried else 0)]

        def scored():
            keys = k_ref[here, :]
            if causal:
                key = lax.broadcasted_iota(jnp.int32, (size, wide), 0) + chunk * size
                token = lax.broadcasted_iota(jnp.int32, (size, wide), 1)
                token = jnp.where(token >= wide // 2, token - wide // 2, token)
                return jnp.where(key <= token, rows_dot(keys, queries), neg_big)
            key = lax.broadcasted_iota(jnp.int32, keys.shape, 0)
            lane = lax.broadcasted_iota(jnp.int32, keys.shape, 1)
            dead = jnp.where((lane == 0) & (key >= live), neg_big, 0.0).astype(low)
            return rows_dot(jnp.concatenate([keys, dead], axis=1), queries)

        def keep(scores, peak):
            total, mix = weigh(here, scores, peak)
            stats_ref[chunk : chunk + 1, :] = peak if causal else jnp.where(live > 0, peak, neg_big)
            stats_ref[chunks + chunk : chunks + chunk + 1, :] = total
            mixed_ref[chunk] = mix
            return total

        squares = k_ref[here, :].astype(high)
        squares = squares * squares
        first = lax.broadcasted_iota(jnp.int32, squares.shape, 1) < HD
        sides = [
            jnp.max(jnp.sum(jnp.where(side, squares, 0.0), axis=1, keepdims=True), axis=0, keepdims=True)
            for side in (first, ~first)
        ]
        column = lax.broadcasted_iota(jnp.int32, (1, wide), 1)
        longest = jnp.where(column < wide // 2, sides[0], sides[1])
        total = keep(scored(), 1.01 * jnp.sqrt(lengths * longest))

        @pl.when((live > 0) & (jnp.min(total) < smallest_total))
        def _():
            scores = scored()
            keep(scores, jnp.max(scores, axis=0, keepdims=True))

    peaks = [stats_ref[at : at + 1] for at in range(chunks)]
    totals = [stats_ref[chunks + at : chunks + at + 1] for at in range(chunks)]
    mixes = [mixed_ref[at] for at in range(chunks)]
    if carried:
        stats_in = before[1][0]
        count = chunks
        peaks = [stats_in[at : at + 1] for at in range(count)] + peaks
        totals = [stats_in[count + at : count + at + 1] for at in range(count)] + totals
    top = peaks[0]
    for peak in peaks[1:]:
        top = jnp.maximum(top, peak)
    scales = [jnp.exp(peak - top) for peak in peaks]
    mixed = sum(mix * scale for mix, scale in zip(mixes, scales[-chunks:]))
    if carried:
        earlier = peaks[0]
        for peak in peaks[1:chunks]:
            earlier = jnp.maximum(earlier, peak)
        mixed = mixed + before[0][0] * jnp.exp(earlier - top)
    if last:
        inverse = 1.0 / sum(total * scale for total, scale in zip(totals, scales))
        refs[1][...] = one_pair(mixed * inverse).astype(low)
        for at, scale in enumerate(scales):
            refs[2][0, at : at + 1, :] = scale * inverse
    else:
        refs[1][0] = mixed
        for at in range(chunks):
            refs[2][0, at : at + 1, :] = peaks[at]
            refs[2][0, chunks + at : chunks + at + 1, :] = totals[at]


def attend_forward(queries, keys, values, live, causal, chunks, name, last=True, before=()):
    tokens, width = queries.shape
    patches = keys.shape[0]
    pairs = width // LANES
    by_pair = lambda rows: pl.BlockSpec((rows, LANES), lambda pair, _: (0, pair))
    stack = lambda rows: pl.BlockSpec((1, rows, 2 * tokens), lambda pair, _: (pair, 0, 0))
    return pl.pallas_call(
        lambda *refs: attend_forward_kernel(causal, chunks, len(before), last, *refs),
        out_shape=(
            jax.ShapeDtypeStruct((pairs, patches, 2 * tokens), low),
            jax.ShapeDtypeStruct((tokens, width), low)
            if last
            else jax.ShapeDtypeStruct((pairs, LANES, 2 * tokens), high),
            jax.ShapeDtypeStruct((pairs, 8, 2 * tokens), high),
        ),
        grid_spec=pltpu.PrefetchScalarGridSpec(
            num_scalar_prefetch=1,
            grid=(pairs,),
            in_specs=[by_pair(tokens), by_pair(patches), by_pair(patches)]
            + [stack(piece.shape[1]) for piece in before],
            out_specs=[stack(patches), by_pair(tokens) if last else stack(LANES), stack(8)],
            scratch_shapes=[
                pltpu.VMEM((2 * chunks, 2 * tokens), high),
                pltpu.VMEM((chunks, LANES, 2 * tokens), high),
            ],
        ),
        cost_estimate=cost(name),
        compiler_params=pltpu.CompilerParams(vmem_limit_bytes=vmem_bytes),
        name=name,
    )(live, queries, keys, values, *before)


def attend_backward_kernel(
    chunks,
    offset,
    carried,
    last,
    weight_ref,
    inverse_ref,
    q_ref,
    k_ref,
    v_ref,
    mixed_ref,
    grad_mixed_ref,
    *refs,
):
    before, (grad_q_ref, grad_k_ref, grad_v_ref) = refs[:carried], refs[-3:]
    queries = two_heads(q_ref[...])
    grads = grad_mixed_ref[...].astype(high).T
    mixed = mixed_ref[...].astype(high).T
    first = lax.broadcasted_iota(jnp.int32, grads.shape, 0) < HD
    zero = jnp.zeros_like(grads)
    grads = jnp.concatenate([jnp.where(first, grads, zero), jnp.where(first, zero, grads)], axis=1)
    mixed = jnp.concatenate([mixed, mixed], axis=1)
    size = k_ref.shape[0] // chunks
    grad_q = jnp.zeros(grads.shape, high)
    for chunk in range(chunks):
        here = slice(chunk * size, (chunk + 1) * size)
        at = offset + chunk
        scaled = (grads * inverse_ref[0, at : at + 1, :]).astype(low)
        wide = scaled.astype(high)
        centre = jnp.sum(wide * mixed, axis=0, keepdims=True)
        rows = wide.T.astype(low)
        weights = weight_ref[0, here, :]
        grad_probs = plain_dot(v_ref[here, :], scaled)
        grad_scores = (weights.astype(high) * (grad_probs - centre)).astype(low)
        grad_v_ref[here, :] = plain_dot(weights, rows).astype(low)
        grad_k_ref[here, :] = plain_dot(grad_scores, queries).astype(low)
        grad_q = grad_q + cols_dot(k_ref[here, :], grad_scores)
    grad_q = one_pair(grad_q)
    if carried:
        grad_q = grad_q + before[0][...]
    grad_q_ref[...] = grad_q.astype(grad_q_ref.dtype)


def attend_backward(
    weights,
    inverse,
    queries,
    keys,
    values,
    mixed,
    grad_mixed,
    chunks,
    offset,
    name,
    last=True,
    before=(),
    pairs=None,
    filled=(),
):
    tokens, width = queries.shape
    patches = keys.shape[0]
    begin, end = pairs or (0, width // LANES)
    by_token = pl.BlockSpec((tokens, LANES), lambda pair: (0, pair + begin))
    by_patch = pl.BlockSpec((patches, LANES), lambda pair: (0, pair + begin))
    return pl.pallas_call(
        lambda *refs: attend_backward_kernel(chunks, offset, len(before), last, *refs),
        out_shape=(
            jax.ShapeDtypeStruct((tokens, width), low if last else high),
            jax.ShapeDtypeStruct((patches, width), low),
            jax.ShapeDtypeStruct((patches, width), low),
        ),
        grid=(end - begin,),
        in_specs=[
            pl.BlockSpec((1, patches, 2 * tokens), lambda pair: (pair + begin, 0, 0)),
            pl.BlockSpec((1, 8, 2 * tokens), lambda pair: (pair + begin, 0, 0)),
            by_token,
            by_patch,
            by_patch,
            by_token,
            by_token,
        ]
        + [by_token] * len(before)
        + [pl.BlockSpec(memory_space=pl.ANY)] * len(filled),
        out_specs=[by_token, by_patch, by_patch],
        input_output_aliases={7 + len(before) + which: which for which in range(len(filled))},
        cost_estimate=cost(name),
        compiler_params=pltpu.CompilerParams(vmem_limit_bytes=vmem_bytes),
        name=name,
    )(weights, inverse, queries, keys, values, mixed, grad_mixed, *before, *filled)


def swap(piece, axis_name, mask):
    size = lax.axis_size(axis_name)
    return lax.ppermute(piece, axis_name, [(place, place ^ mask) for place in range(size)])


def bit_of(axis_name, bit):
    return (lax.axis_index(axis_name) >> bit) & 1


def pick(piece, which):
    return lax.dynamic_index_in_dim(piece, which, 0, keepdims=False)


class Parcel:
    def __init__(self, shapes, extra=0):
        self.shapes = shapes
        self.heights = [height // BLOCKS for height, _ in shapes]
        self.plain = [width // 4 // LANES for _, width in shapes]
        self.at = []
        at = 0
        for (_, width), tiles, height in zip(shapes, self.plain, self.heights):
            self.at.append(at)
            at += tiles * height + (height // 2 if width // 4 % LANES else 0)
        self.extra = extra
        self.own = at + extra
        self.rows = 2 * self.own


def place(block):
    return (block & 1) * 4 + (block & 2) + (block >> 2)


def core_tiles(grad, core):
    quarter = grad.shape[1] // 4
    starts = [core * quarter, 2 * quarter + core * quarter]
    tiles = [
        grad[:, start + at : start + at + LANES]
        for start in starts
        for at in range(0, quarter - LANES + 1, LANES)
    ]
    rest = quarter % LANES
    if rest:
        tiles.append(
            jnp.concatenate(
                [grad[:, start + quarter - rest : start + quarter] for start in starts], axis=1
            )
        )
    return tiles


def both_sides(grad, core):
    first, second = core_tiles(grad, 0), core_tiles(grad, 1)
    own = [jnp.where(core == 0, one, other) for one, other in zip(first, second)]
    return own + [jnp.where(core == 0, other, one) for one, other in zip(first, second)]


def self_backward(
    parcel,
    core_ref,
    grad_q_two_ref,
    hidden_ref,
    grad_in_ref,
    gain_ref,
    cross_query_ref,
    out_weight_ref,
    feed_gain_ref,
    attended_ref,
    weight_ref,
    inverse_ref,
    q_ref,
    k_ref,
    v_ref,
    mixed_ref,
    wq_ref,
    wk_ref,
    wv_ref,
    normed_hbm_ref,
    next_normed_hbm_ref,
    tokens_hbm_ref,
    tokens_grad_ref,
    kept_ref,
    sent_ref,
    grad_hidden_ref,
    branch_ref,
    grad_mixed_ref,
    gains_ref,
    grads_ref,
    back_ref,
    late_ref,
    turned_ref,
    packed_ref,
    done_ref,
):
    pair = pl.program_id(0)
    pairs = pl.num_programs(0)
    late = [
        pltpu.make_async_copy(far_ref, late_ref.at[at], done_ref.at[at])
        for at, far_ref in enumerate((normed_hbm_ref, next_normed_hbm_ref, tokens_hbm_ref))
    ]

    @pl.when(pair == 0)
    def _():
        for copy in late:
            copy.start()
        to_rows, to_gain = norm_back(
            hidden_ref[...], gain_ref[1:2, :], rows_dot(grad_q_two_ref[...], cross_query_ref[...])
        )
        grad_hidden = grad_in_ref[...] + to_rows
        grad_hidden_ref[...] = grad_hidden
        branch = grad_hidden.astype(low)
        branch_ref[...] = branch
        grad_mixed_ref[...] = rows_dot(branch, out_weight_ref[...]).astype(low)
        gains_ref[1:2, :] = to_gain
        gains_ref[2:3, :] = feed_gain_ref[...]
        back_ref[...] = jnp.zeros_like(back_ref)

    here = pl.ds(pl.multiple_of(pair * LANES, LANES), LANES)
    views = [grads_ref.at[at, :, here] for at in range(3)]
    attend_backward_kernel(
        1,
        0,
        0,
        True,
        weight_ref,
        inverse_ref,
        q_ref,
        k_ref,
        v_ref,
        mixed_ref,
        grad_mixed_ref.at[:, here],
        *views,
    )
    grads = jnp.concatenate([view[...] for view in views], axis=1)
    weights = jnp.concatenate([wq_ref[...], wk_ref[...], wv_ref[...]], axis=1)
    back_ref[...] += rows_dot(grads, weights)

    @pl.when(pair == pairs - 1)
    def _():
        for copy in late:
            copy.wait()
        to_rows, to_gain = norm_back(late_ref[2].astype(high), gain_ref[0:1, :], back_ref[...])
        tokens_grad_ref[...] = (grad_hidden_ref[...] + to_rows).astype(low)
        gains_ref[0:1, :] = to_gain
        width = to_gain.shape[1]
        tiles = width // LANES
        packed_ref[...] = jnp.zeros_like(packed_ref)
        for gain in range(3):
            for tile in range(tiles):
                packed_ref[gain * tiles + tile : gain * tiles + tile + 1, :] = gains_ref[
                    gain : gain + 1, tile * LANES : (tile + 1) * LANES
                ]
        packed = packed_ref[...].astype(low)
        for out_ref in (kept_ref, sent_ref):
            for block in range(BLOCKS):
                for end in (parcel.own, parcel.rows):
                    out_ref[block, end - parcel.extra : end, :] = packed
        core = core_ref[0]
        jobs = (
            [(late_ref.at[0], grads_ref[at]) for at in range(3)]
            + [(late_ref.at[1], grad_q_two_ref[...])]
            + [(attended_ref, branch_ref[...])]
        )
        for job, (rows_ref, grad) in enumerate(jobs):
            if job in (0, 3, 4):
                turned_ref[...] = rows_ref[...].T
            tiles = both_sides(grad, core)
            count = len(tiles) // 2
            for begin in range(0, 2 * count, 2):
                product = plain_dot(
                    turned_ref[...], jnp.concatenate(tiles[begin : begin + 2], axis=1)
                ).astype(low)
                for slot in (0, 1):
                    kind, tile = divmod(begin + slot, count)
                    put_rows(parcel, job, product, tile, (kept_ref, sent_ref)[kind], slot)


def self_backward_call(
    parcel,
    core,
    grad_q_two,
    hidden,
    grad_in,
    gain,
    cross_query,
    out_weight,
    feed_gain,
    attended,
    weights,
    inverse,
    queries,
    keys,
    values,
    projections,
    late,
):
    rows, width = hidden.shape
    pairs = width // LANES
    columns = pl.BlockSpec((rows, LANES), lambda pair: (0, pair))
    stack = lambda height: pl.BlockSpec((1, height, 2 * rows), lambda pair: (pair, 0, 0))
    whole = (grad_q_two, hidden, grad_in, gain, cross_query, out_weight, feed_gain, attended)
    fixed = lambda shape: pl.BlockSpec(shape, lambda pair: (0,) * len(shape))
    parcel_shape = (BLOCKS, parcel.rows, LANES)
    return pl.pallas_call(
        lambda *refs: self_backward(parcel, *refs),
        grid=(pairs,),
        in_specs=[pl.BlockSpec(memory_space=pltpu.SMEM)]
        + [whole_spec(piece.shape) for piece in whole]
        + [stack(rows), stack(8), columns, columns, columns, columns]
        + [pl.BlockSpec((width, LANES), lambda pair: (0, pair))] * 3
        + [pl.BlockSpec(memory_space=pl.ANY)] * 3,
        out_specs=[fixed((rows, width)), whole_spec(parcel_shape), whole_spec(parcel_shape)],
        out_shape=[
            jax.ShapeDtypeStruct((rows, width), low),
            jax.ShapeDtypeStruct(parcel_shape, low),
            jax.ShapeDtypeStruct(parcel_shape, low),
        ],
        scratch_shapes=[
            pltpu.VMEM((rows, width), high),
            pltpu.VMEM((rows, width), low),
            pltpu.VMEM((rows, width), low),
            pltpu.VMEM((8, width), high),
            pltpu.VMEM((3, rows, width), low),
            pltpu.VMEM((rows, width), high),
            pltpu.VMEM((3, rows, width), low),
            pltpu.VMEM((width, rows), low),
            pltpu.VMEM((parcel.extra, LANES), high),
            pltpu.SemaphoreType.DMA((3,)),
        ],
        cost_estimate=cost("self_backward"),
        compiler_params=pltpu.CompilerParams(vmem_limit_bytes=vmem_bytes),
        name="self_backward",
    )(
        core,
        *whole,
        weights,
        inverse,
        queries,
        keys,
        values,
        attended,
        *projections,
        *late,
    )


def fold_one(mine_ref, kept_ref, received_ref, *out_refs):
    for which, out_ref in enumerate(out_refs):

        @pl.when(pl.program_id(0) == which)
        def _():
            total = kept_ref[0].astype(high) + received_ref[0].astype(high)
            out_ref[...] = total.astype(low)


def fold_one_call(name, mine, kept, received, view, shape, index):
    block = pl.BlockSpec((1, *shape), lambda step, mine: index(mine[0] ^ step))
    return pl.pallas_call(
        fold_one,
        grid_spec=pltpu.PrefetchScalarGridSpec(
            num_scalar_prefetch=1,
            grid=(4,),
            in_specs=[block, block],
            out_specs=[
                pl.BlockSpec(shape, lambda step, _: (0, 0, 0), pipeline_mode=pl.Buffered(1))
            ]
            * 4,
        ),
        out_shape=[jax.ShapeDtypeStruct(shape, low)] * 4,
        cost_estimate=cost(name),
        compiler_params=pltpu.CompilerParams(vmem_limit_bytes=vmem_bytes),
        name=name,
    )(mine, kept.reshape(view), received.reshape(view))


def sum_of(refs):
    first, second, third, fourth = [ref[...].astype(high) for ref in refs]
    return (first + second) + (third + fourth)


def fold_two(parcel, with_x, first_ref, second_ref, third_ref, fourth_ref, out_ref):
    total = sum_of((first_ref, second_ref, third_ref, fourth_ref)).astype(low)
    if with_x:
        out_ref[...] = total
    else:
        for which in range(4):
            begin = (which & 1) * parcel.own
            out_ref[which] = total[which >> 1, begin : begin + parcel.own, :]


def fold_end(parcel, parts_ref, *outs):
    total = sum_of([parts_ref.at[which] for which in range(4)])
    for job, rows in enumerate(parcel.heights):
        at = parcel.at[job]
        for tile in range(parcel.plain[job]):
            outs[job][:, tile * LANES : (tile + 1) * LANES] = total[at : at + rows]
            at += rows
        begin = parcel.plain[job] * LANES
        rest = outs[job].shape[1] - begin
        if rest:
            outs[job][: rows // 2, begin:] = total[at : at + rows // 2, :rest]
            outs[job][rows // 2 :, begin:] = total[at : at + rows // 2, rest:]
    if parcel.extra:
        outs[-1][...] = total[-parcel.extra :]


class Travel:
    def __init__(self, parcel, kept, sent, name, with_x):
        self.parcel = parcel
        self.name = name
        self.kept = kept
        self.received = swap(sent, "narrow", 1)
        self.top = lax.axis_size("items").bit_length() - 4
        self.with_x = with_x

    def joint(self, up, side):
        narrow = lax.axis_size("narrow")
        return [
            (place, ((place // narrow) ^ up) * narrow + ((place % narrow) ^ side))
            for place in range(lax.axis_size("items") * narrow)
        ]

    def fold_one(self, *earlier):
        kept, received = lax.optimization_barrier((self.kept, self.received, *earlier))[:2]
        rows, top = self.parcel.rows, self.top
        if self.with_x:
            mine = bit_of("items", top) * 2 + bit_of("narrow", 1)
            view, shape = (2, 4, rows, LANES), (4, self.parcel.own, LANES)
            partners = [(0, 2), (1 << top, 0), (1 << top, 2)]
            index = lambda part: (part >> 1, 0, part & 1, 0)
        else:
            mine = bit_of("items", top) * 2 + bit_of("items", top + 1)
            view, shape = (4, 2, rows, LANES), (2, rows, LANES)
            partners = [(2 << top, 0), (1 << top, 0), (3 << top, 0)]
            index = lambda part: (part, 0, 0, 0)
        parts = fold_one_call(
            self.name + "_one", mine.reshape(1), kept, received, view, shape, index
        )
        self.parts = [parts[0]] + [
            lax.ppermute(part, ("items", "narrow"), self.joint(*partner))
            for part, partner in zip(parts[1:], partners)
        ]
        return parts[0]

    def fold_two(self, *earlier):
        parts = lax.optimization_barrier((*self.parts, *earlier))[:4]
        parcel = self.parcel
        (parts,) = one_step_call(
            lambda *refs: fold_two(parcel, self.with_x, *refs),
            self.name + "_two",
            list(parts),
            [((4, parcel.own, LANES), low)],
        )
        far = 4 << self.top
        first, second = ((2 << self.top, 0), (far, 0)) if self.with_x else ((far, 0), (0, 2))
        narrow = lax.axis_size("narrow")
        clear = first[0] | second[0]
        side = first[1] | second[1]
        groups = [
            [
                (item | one[0] | two[0]) * narrow + (other | one[1] | two[1])
                for one in ((0, 0), first)
                for two in ((0, 0), second)
            ]
            for item in range(lax.axis_size("items"))
            for other in range(narrow)
            if not item & clear and not other & side
        ]
        self.parts = parts
        self.groups = groups
        return parts

    def send(self, *earlier):
        parts = lax.optimization_barrier((self.parts, *earlier))[0]
        self.parts = lax.all_to_all(
            parts, ("items", "narrow"), 0, 0, axis_index_groups=self.groups, tiled=True
        )

    def end(self, *earlier):
        parts = lax.optimization_barrier((self.parts, *earlier))[0]
        parcel = self.parcel
        outs = [((height // BLOCKS, width // 4), high) for height, width in parcel.shapes]
        outs += [((parcel.extra, LANES), high)] if parcel.extra else []
        outs = list(
            one_step_call(
                lambda *refs: fold_end(parcel, *refs),
                self.name + "_end",
                [parts],
                outs,
            )
        )
        count = len(parcel.shapes)
        extras = outs[count:]
        for bit in range(self.top, 0, -1):
            extras = [piece + swap(piece, "items", 1 << (bit - 1)) for piece in extras]
        return list(lower_bits(outs[:count])) + extras


def exchange(piece):
    return lax.all_to_all(piece, "narrow", split_axis=0, concat_axis=0, tiled=True)


def body(
    tokens,
    memory,
    mem_count,
    cotangent,
    gain_self,
    self_query,
    self_key,
    self_value,
    self_out,
    gain_cross,
    cross_query,
    cross_key,
    cross_value,
    cross_out,
    gain_feed,
    gate_weight,
    up_weight,
    down_weight,
):
    width = tokens.shape[2]
    inner = gate_weight.shape[1]
    gains_in = jnp.stack([gain_self, gain_cross, gain_feed])
    parts = lax.axis_size("narrow")
    mine = lax.axis_index("narrow")
    token_rows = exchange(tokens).reshape(-1, width)
    own_memory, *away_memory = [pick(memory, mine ^ which) for which in range(parts)]
    pieces = [own_memory] + [
        swap(piece, "narrow", which + 1) for which, piece in enumerate(away_memory)
    ]
    cotangent_rows = exchange(cotangent).reshape(-1, width)
    count = pick(mem_count, mine)
    local_mem = memory.shape[1]
    live = count - local_mem * (mine ^ jnp.arange(parts, dtype=jnp.int32))
    kinds = [((2 * local_mem, width), low)] * 3
    near_rows, near_keys, near_values = one_step_call(
        enter_memory,
        "enter_memory_near",
        [pieces[0], pieces[1], cross_key, cross_value],
        kinds,
    )
    (
        normed_one,
        query_one,
        key_one,
        value_one,
        weights_one,
        attended,
        inverse_one,
        hidden_one,
        normed_two,
        query_two,
    ) = self_forward_call(
        after(token_rows, near_keys),
        gains_in,
        cross_query,
        self_query,
        self_key,
        self_value,
        self_out,
    )
    near_weights, near_mixed, near_stats = attend_forward(
        query_two, near_keys, near_values, live, False, 2, "cross_forward_near", False
    )
    far_rows, far_keys, far_values = one_step_call(
        enter_memory,
        "enter_memory_far",
        [after(pieces[2], near_stats), pieces[3], cross_key, cross_value],
        kinds,
    )
    far_weights, crossed, inverse_two = attend_forward(
        query_two,
        far_keys,
        far_values,
        live,
        False,
        2,
        "cross_forward_far",
        True,
        (near_mixed, near_stats),
    )
    square = (width, width)
    feed_parcel = Parcel([(width, inner), (width, inner), (inner, width), square])
    result, grad_hidden_two, branch_two, grad_crossed, grad_gain_feed, *feed_parts = feed_call(
        feed_parcel,
        bit_of("narrow", 0).reshape(1),
        crossed,
        hidden_one,
        cotangent_rows,
        gains_in,
        cross_out,
        gate_weight,
        up_weight,
        down_weight,
    )
    feed_trip = Travel(feed_parcel, *feed_parts, "feed_weights", True)
    result = exchange(result.reshape(tokens.shape))
    far = ()
    ready = feed_trip.kept
    for pairs in ((0, 3), (3, 6)):
        far = attend_backward(
            far_weights,
            inverse_two,
            query_two,
            far_keys,
            far_values,
            crossed,
            after(grad_crossed, ready),
            2,
            2,
            "cross_backward_far_a" if pairs[0] == 0 else "cross_backward_far_b",
            False,
            pairs=pairs,
            filled=far,
        )
        ready = feed_trip.fold_one(far[0]) if pairs[0] == 0 else far[0]
    far_grad_q, far_grad_k, far_grad_v = far
    grad_query_two, near_grad_k, near_grad_v = attend_backward(
        near_weights,
        inverse_two,
        query_two,
        near_keys,
        near_values,
        crossed,
        after(grad_crossed, result),
        2,
        0,
        "cross_backward_near",
        True,
        (far_grad_q,),
    )
    extra = -(-3 * width // LANES // 16) * 16
    self_parcel = Parcel([square] * 5, extra)
    tokens_grad, *self_parts = self_backward_call(
        self_parcel,
        bit_of("narrow", 0).reshape(1),
        grad_query_two,
        hidden_one,
        grad_hidden_two,
        gains_in,
        cross_query,
        self_out,
        grad_gain_feed,
        attended,
        weights_one,
        inverse_one,
        query_one,
        key_one,
        value_one,
        [self_query, self_key, self_value],
        [normed_one, normed_two, token_rows],
    )
    self_trip = Travel(self_parcel, *self_parts, "self_weights", True)
    tokens_grad = exchange(tokens_grad.reshape(tokens.shape))
    ready = feed_trip.fold_two(self_parts[0])
    feed_trip.send()
    ready = self_trip.fold_one(ready)
    cross_parcel = Parcel([square] * 2)
    grad_away, grad_near, *cross_parts = memory_back_call(
        cross_parcel,
        bit_of("narrow", 0).reshape(1),
        [after(far_rows, ready, tokens_grad), far_grad_k, far_grad_v],
        [near_rows, near_grad_k, near_grad_v],
        cross_key,
        cross_value,
    )
    landed_away = swap(grad_away, "narrow", 2)
    cross_trip = Travel(cross_parcel, *cross_parts, "cross_weights", False)
    tokens_grad = tokens_grad.astype(high)
    ready = self_trip.fold_two(grad_away)
    self_trip.send()
    ready = cross_trip.fold_one(ready)
    gate_sum, up_sum, down_sum, cross_out_sum = feed_trip.end(ready)
    ready = gate_sum
    ready = cross_trip.fold_two(ready)
    cross_trip.send()
    grad_near, landed_away = lax.optimization_barrier((grad_near, landed_away, ready))[:2]
    landed_core = swap(grad_near[local_mem:], "narrow", 1)
    landed_far = swap(landed_away[local_mem:], "narrow", 1)
    self_query_sum, self_key_sum, self_value_sum, cross_query_sum, self_out_sum, gains = (
        self_trip.end(ready)
    )
    memory_grad = land_call(
        mine.reshape(1),
        [after(grad_near, self_query_sum), landed_core, landed_away, landed_far],
    )
    cross_key_sum, cross_value_sum = cross_trip.end(memory_grad)
    gains = gains[: 3 * width // LANES].reshape(3, width)
    return (
        result,
        tokens_grad,
        memory_grad,
        gains[0],
        self_query_sum,
        self_key_sum,
        self_value_sum,
        self_out_sum,
        gains[1],
        cross_query_sum,
        cross_key_sum,
        cross_value_sum,
        cross_out_sum,
        gains[2],
        gate_sum,
        up_sum,
        down_sum,
    )


def solution(mesh):
    in_specs = (
        P("items", "narrow", None),
        P("items", "narrow", None),
        P("items"),
        P("items", "narrow", None),
        P(),
        P(),
        P(),
        P(),
        P(),
        P(),
        P(),
        P(),
        P(),
        P(),
        P(),
        P(),
        P(),
        P(),
    )
    out_specs = (
        P("items", "narrow", None),
        P("items", "narrow", None),
        P("items", "narrow", None),
        P(),
        P("items", "narrow"),
        P("items", "narrow"),
        P("items", "narrow"),
        P("items", "narrow"),
        P(),
        P("items", "narrow"),
        P("items", "narrow"),
        P("items", "narrow"),
        P("items", "narrow"),
        P(),
        P("items", "narrow"),
        P("items", "narrow"),
        P("items", "narrow"),
    )
    return jax.shard_map(body, mesh=mesh, in_specs=in_specs, out_specs=out_specs, check_vma=False)
```

```python
import jax
import jax.numpy as jnp
from jax import lax
from jax.experimental import pallas as pl
from jax.experimental.pallas import tpu as pltpu
from jax.sharding import PartitionSpec as P

HD = 64
LANES = 128
BLOCKS = 8

eps = 1e-06
neg_big = -1e30
smallest_total = 1e-25
gelu_scale = 0.7978845608028654
gelu_cubic = 0.044715
low = jnp.bfloat16
high = jnp.float32
vmem_bytes = 60 * 1024 * 1024


def rows_dot(left_side, right_side):
    return lax.dot_general(
        left_side, right_side, (((1,), (1,)), ((), ())), preferred_element_type=high
    )


def cols_dot(left_side, right_side):
    return lax.dot_general(
        left_side, right_side, (((0,), (0,)), ((), ())), preferred_element_type=high
    )


def plain_dot(left_side, right_side):
    return jnp.dot(left_side, right_side, preferred_element_type=high)


def inverse_scale(hidden):
    return lax.rsqrt(jnp.mean(hidden * hidden, axis=-1, keepdims=True) + eps)


def norm_back(hidden, gain, grad):
    scale = inverse_scale(hidden)
    weighted = gain * grad
    middle = jnp.mean(weighted * hidden, axis=-1, keepdims=True)
    to_rows = scale * (weighted - hidden * (scale * scale * middle))
    to_gain = jnp.sum(grad * hidden * scale, axis=0, keepdims=True)
    return to_rows, to_gain


call_time = {
    "enter_memory_near": 2,
    "self_forward": 8,
    "cross_forward_near": 6,
    "enter_memory_far": 2,
    "cross_forward_far": 6,
    "cross_backward_far_b": 100,
    "feed_weights_two": 100,
    "memory_back": 100,
    "self_weights_two": 100,
    "self_weights_end": 100,
}


def cost(name):
    return pl.CostEstimate(
        flops=int(call_time.get(name, 0.001) * 1.15e9), bytes_accessed=1, transcendentals=0
    )


def after(piece, *earlier):
    return lax.optimization_barrier((piece, *earlier))[0]


def row_spec(rows, width):
    return pl.BlockSpec((rows, width), lambda step: (step, 0))


def whole_spec(shape):
    return pl.BlockSpec(
        shape, lambda step: (0,) * len(shape), pipeline_mode=pl.Buffered(1)
    )


def self_forward(
    tokens_ref,
    gains_ref,
    next_query_ref,
    wq_ref,
    wk_ref,
    wv_ref,
    out_ref,
    normed_ref,
    q_ref,
    k_ref,
    v_ref,
    weight_ref,
    mixed_ref,
    inverse_ref,
    hidden_ref,
    next_normed_ref,
    next_q_ref,
    stats_ref,
    part_ref,
):
    pair = pl.program_id(0)

    @pl.when(pair == 0)
    def _():
        hidden = tokens_ref[...].astype(high)
        normed_ref[...] = (hidden * inverse_scale(hidden) * gains_ref[0:1, :]).astype(low)
        hidden_ref[...] = hidden

    weights = jnp.concatenate([wq_ref[...], wk_ref[...], wv_ref[...]], axis=1)
    projected = plain_dot(normed_ref[...], weights).astype(low)
    for at, head_ref in enumerate((q_ref, k_ref, v_ref)):
        head_ref[...] = projected[:, at * LANES : (at + 1) * LANES]
    attend_forward_kernel(
        True,
        1,
        0,
        True,
        None,
        q_ref,
        k_ref,
        v_ref,
        weight_ref,
        mixed_ref,
        inverse_ref,
        stats_ref,
        part_ref,
    )
    hidden_ref[...] += plain_dot(mixed_ref[...], out_ref[...])

    @pl.when(pair == pl.num_programs(0) - 1)
    def _():
        hidden = hidden_ref[...]
        normed = (hidden * inverse_scale(hidden) * gains_ref[1:2, :]).astype(low)
        next_normed_ref[...] = normed
        next_q_ref[...] = plain_dot(normed, next_query_ref[...]).astype(low)


def self_forward_call(tokens, gains, next_query, wq, wk, wv, out_weight):
    rows, width = tokens.shape
    pairs = width // LANES
    whole = pl.BlockSpec((rows, width), lambda pair: (0, 0))
    columns = pl.BlockSpec((rows, LANES), lambda pair: (0, pair))
    stack = lambda height: pl.BlockSpec((1, height, 2 * rows), lambda pair: (pair, 0, 0))
    plain = jax.ShapeDtypeStruct((rows, width), low)
    return pl.pallas_call(
        self_forward,
        grid=(pairs,),
        in_specs=[whole_spec(piece.shape) for piece in (tokens, gains, next_query)]
        + [pl.BlockSpec((width, LANES), lambda pair: (0, pair))] * 3
        + [pl.BlockSpec((LANES, width), lambda pair: (pair, 0))],
        out_specs=[whole, columns, columns, columns, stack(rows), columns, stack(8)] + [whole] * 3,
        out_shape=[
            plain,
            plain,
            plain,
            plain,
            jax.ShapeDtypeStruct((pairs, rows, 2 * rows), low),
            plain,
            jax.ShapeDtypeStruct((pairs, 8, 2 * rows), high),
            jax.ShapeDtypeStruct((rows, width), high),
            plain,
            plain,
        ],
        scratch_shapes=[
            pltpu.VMEM((2, 2 * rows), high),
            pltpu.VMEM((1, LANES, 2 * rows), high),
        ],
        cost_estimate=cost("self_forward"),
        compiler_params=pltpu.CompilerParams(vmem_limit_bytes=vmem_bytes),
        name="self_forward",
    )(tokens, gains, next_query, wq, wk, wv, out_weight)


def enter_memory(first_ref, second_ref, wk_ref, wv_ref, rows_ref, k_ref, v_ref):
    half = first_ref.shape[0]
    for at, piece_ref in ((0, first_ref), (half, second_ref)):
        rows = piece_ref[...]
        rows_ref[at : at + half, :] = rows
        k_ref[at : at + half, :] = plain_dot(rows, wk_ref[...]).astype(low)
        v_ref[at : at + half, :] = plain_dot(rows, wv_ref[...]).astype(low)


def one_step_call(kernel, name, ins, outs, scratch=()):
    vmem = pl.BlockSpec(memory_space=pltpu.VMEM)
    smem = pl.BlockSpec(memory_space=pltpu.SMEM)
    return pl.pallas_call(
        kernel,
        in_specs=[smem if piece.dtype == jnp.int32 else vmem for piece in ins],
        out_specs=[vmem] * len(outs),
        out_shape=[jax.ShapeDtypeStruct(shape, kind) for shape, kind in outs],
        scratch_shapes=list(scratch),
        cost_estimate=cost(name),
        compiler_params=pltpu.CompilerParams(vmem_limit_bytes=vmem_bytes),
        name=name,
    )(*ins)


def put_block(parcel, job, tile, rows_of, out_ref, spot):
    plain, rows = parcel.plain[job], parcel.heights[job]
    if tile < 2 * plain:
        at = (tile // plain) * parcel.own + parcel.at[job] + (tile % plain) * rows
        out_ref[spot, at : at + rows, :] = rows_of
    else:
        half = LANES // 2
        for side in (0, 1):
            at = side * parcel.own + parcel.at[job] + plain * rows
            lanes = slice(side * half, (side + 1) * half)
            out_ref[spot, at : at + rows // 2, :] = jnp.concatenate(
                [rows_of[: rows // 2, lanes], rows_of[rows // 2 :, lanes]], axis=1
            )


def put_rows(parcel, job, product, tile, out_ref, slot):
    rows = parcel.heights[job]
    for block in range(BLOCKS):
        put_block(
            parcel,
            job,
            tile,
            product[block * rows : (block + 1) * rows, slot * LANES : (slot + 1) * LANES],
            out_ref,
            place(block),
        )


def feed_both(
    parcel,
    parts,
    core_ref,
    crossed_ref,
    hidden_in_ref,
    cotangent_ref,
    gain_ref,
    out_ref,
    gate_ref,
    up_ref,
    down_ref,
    result_ref,
    grad_hidden_ref,
    branch_ref,
    grad_crossed_ref,
    grad_gain_ref,
    kept_out_ref,
    sent_out_ref,
    hidden_ref,
    normed_ref,
    turned_ref,
    sum_ref,
    back_ref,
    sides_ref,
    both_ref,
    done_ref,
):
    step = pl.program_id(0)
    core = core_ref[0]
    gain = gain_ref[2:3, :]
    kept_ref, sent_ref = both_ref.at[0], both_ref.at[1]

    @pl.when(step == 0)
    def _():
        hidden = hidden_in_ref[...] + plain_dot(crossed_ref[...], out_ref[...])
        hidden_ref[...] = hidden
        normed = (hidden * inverse_scale(hidden) * gain).astype(low)
        normed_ref[...] = normed
        turned_ref[...] = normed.T
        sum_ref[...] = hidden
        back_ref[...] = jnp.zeros_like(back_ref)
        sides_ref[...] = jnp.concatenate(both_sides(cotangent_ref[...], core), axis=1)

    inner = parcel.at[2]

    def copies(side_ref, out_ref, begin, rows, slot):
        here = (slice(None), pl.ds(begin, rows), slice(None))
        return pltpu.make_async_copy(side_ref.at[here], out_ref.at[here], done_ref.at[slot])

    normed = normed_ref[...]
    cotangent = cotangent_ref[...]
    turned = turned_ref[...]
    sides = sides_ref[...]
    part = gate_ref.shape[1]
    size = part
    output, back_sum = sum_ref[...], back_ref[...]
    grads, mixes = [], []
    for begin in range(0, part, size):
        here = slice(begin, begin + size)
        gate = plain_dot(normed, gate_ref[:, here])
        up = plain_dot(normed, up_ref[:, here])
        back = rows_dot(cotangent, down_ref[here, :])
        square = gate * gate
        curve = jnp.tanh(gelu_scale * (gate + gelu_cubic * gate * square))
        half = 0.5 * (1.0 + curve)
        bent = gate * half
        slope = half + 0.5 * gate * (1.0 - curve * curve) * (
            gelu_scale * (1.0 + 3.0 * gelu_cubic * square)
        )
        mixed = (bent * up).astype(low)
        grad_gate = (back * up * slope).astype(low)
        grad_up = (back * bent).astype(low)
        output = output + plain_dot(mixed, down_ref[here, :])
        back_sum = (
            back_sum
            + rows_dot(grad_gate, gate_ref[:, here])
            + rows_dot(grad_up, up_ref[:, here])
        )
        mixes.append(mixed)
        grads.append((grad_gate, grad_up))
    sum_ref[...] = output
    back_ref[...] = back_sum
    side = (step >> 1) * parcel.own
    other = (step & 1) ^ core
    for job in (0, 1):
        rows = parcel.heights[job]
        for which, pair in enumerate(grads):
            product = plain_dot(turned, pair[job]).astype(low)
            for tile in range(size // LANES):
                at = side + parcel.at[job] + (which * size // LANES + tile) * rows
                at = pl.multiple_of(at, 16)
                for block in range(BLOCKS):
                    both_ref[other, place(block), pl.ds(at, rows), :] = product[
                        block * rows : (block + 1) * rows, tile * LANES : (tile + 1) * LANES
                    ]
    for kind, (side_ref, target_ref) in enumerate(
        ((kept_ref, kept_out_ref), (sent_ref, sent_out_ref))
    ):

        @pl.when(other == kind)
        def _():
            copies(side_ref, target_ref, pl.multiple_of(side, 16), inner, step).start()

    rows = parcel.heights[2]
    tiles = sides.shape[1] // LANES // 2
    for which, mixed in enumerate(mixes):
        product = cols_dot(mixed, sides).astype(low)
        here = product.shape[0] // rows
        for kind, side_ref in enumerate((kept_ref, sent_ref)):
            for tile in range(tiles):
                lane = (kind * tiles + tile) * LANES
                for block in range(here):
                    put_block(
                        parcel,
                        2,
                        tile,
                        product[block * rows : (block + 1) * rows, lane : lane + LANES],
                        side_ref,
                        place(step * here + block),
                    )

    @pl.when(step == pl.num_programs(0) - 1)
    def _():
        hidden = hidden_ref[...]
        result_ref[...] = sum_ref[...].astype(low)
        to_rows, to_gain = norm_back(hidden, gain, back_ref[...])
        grad_gain_ref[...] = to_gain
        grad_hidden = cotangent.astype(high) + to_rows
        grad_hidden_ref[...] = grad_hidden
        branch = grad_hidden.astype(low)
        branch_ref[...] = branch
        grad_crossed_ref[...] = rows_dot(branch, out_ref[...]).astype(low)
        sides = jnp.concatenate(both_sides(branch, core), axis=1)
        product = cols_dot(crossed_ref[...], sides).astype(low)
        for kind, side_ref in enumerate((kept_ref, sent_ref)):
            for tile in range(tiles):
                put_rows(parcel, 3, product, tile, side_ref, kind * tiles + tile)
        spans = ((inner, parcel.own), (parcel.own + inner, parcel.rows))
        last = [
            copies(side_ref, target_ref, begin, end - begin, parts + 2 * kind + which)
            for kind, (side_ref, target_ref) in enumerate(
                ((kept_ref, kept_out_ref), (sent_ref, sent_out_ref))
            )
            for which, (begin, end) in enumerate(spans)
        ]
        for copy in last:
            copy.start()
        for slot in range(parts):
            copies(kept_ref, kept_out_ref, 0, inner, slot).wait()
        for copy in last:
            copy.wait()


def feed_call(
    parcel, core, crossed, hidden, cotangent, gain, out_weight, gate_weight, up_weight, down_weight
):
    tokens, width = crossed.shape
    inner = gate_weight.shape[1]
    parts = lax.axis_size("narrow")
    part = inner // parts
    whole = lambda piece: whole_spec(piece.shape)
    fixed = lambda shape: pl.BlockSpec(shape, lambda step: (0,) * len(shape))
    parcel_shape = (BLOCKS, parcel.rows, LANES)
    return pl.pallas_call(
        lambda *refs: feed_both(parcel, parts, *refs),
        grid=(parts,),
        in_specs=[pl.BlockSpec(memory_space=pltpu.SMEM)]
        + [whole(crossed), whole(hidden), whole(cotangent), whole(gain), whole(out_weight)]
        + [pl.BlockSpec((width, part), lambda step: (0, step))] * 2
        + [pl.BlockSpec((part, width), lambda step: (step, 0))],
        out_specs=[fixed((tokens, width))] * 4
        + [fixed((1, width))]
        + [pl.BlockSpec(memory_space=pl.ANY)] * 2,
        out_shape=[
            jax.ShapeDtypeStruct((tokens, width), low),
            jax.ShapeDtypeStruct((tokens, width), high),
            jax.ShapeDtypeStruct((tokens, width), low),
            jax.ShapeDtypeStruct((tokens, width), low),
            jax.ShapeDtypeStruct((1, width), high),
            jax.ShapeDtypeStruct(parcel_shape, low),
            jax.ShapeDtypeStruct(parcel_shape, low),
        ],
        scratch_shapes=[
            pltpu.VMEM((tokens, width), high),
            pltpu.VMEM((tokens, width), low),
            pltpu.VMEM((width, tokens), low),
            pltpu.VMEM((tokens, width), high),
            pltpu.VMEM((tokens, width), high),
            pltpu.VMEM((tokens, width), low),
            pltpu.VMEM((2, *parcel_shape), low),
            pltpu.SemaphoreType.DMA((parts + 4,)),
        ],
        cost_estimate=cost("feed_both"),
        compiler_params=pltpu.CompilerParams(vmem_limit_bytes=vmem_bytes),
        name="feed_both",
    )(core, crossed, hidden, cotangent, gain, out_weight, gate_weight, up_weight, down_weight)


def lower_bits(sums):
    levels = lax.axis_size("items").bit_length() - 1
    for bit in range(levels - 4, -1, -1):
        mine = bit_of("items", bit)
        halves = [piece.reshape(2, piece.shape[0] // 2, piece.shape[1]) for piece in sums]
        sums = [pick(piece, mine) + swap(pick(piece, 1 - mine), "items", 1 << bit) for piece in halves]
    return sums


def memory_back(parcel, core_ref, *refs):
    wk_ref, wv_ref, away_ref, near_ref, kept_ref, sent_ref, total_ref = refs[6:]
    step = pl.program_id(0)
    steps = pl.num_programs(0)

    def block(rows_ref, grad_k_ref, grad_v_ref, grad_ref, first):
        grad_k, grad_v = grad_k_ref[...], grad_v_ref[...]
        grad_ref[...] = (rows_dot(grad_k, wk_ref[...]) + rows_dot(grad_v, wv_ref[...])).astype(low)
        width = grad_k.shape[1]
        rows = rows_ref[...].T
        parts = plain_dot(rows, grad_k), plain_dot(rows, grad_v)
        for job, part in enumerate(parts):
            columns = slice(job * width, (job + 1) * width)

            if first:

                @pl.when(step == 0)
                def _():
                    total_ref[:, columns] = part

                @pl.when(step > 0)
                def _():
                    total_ref[:, columns] += part

            else:
                total_ref[:, columns] += part

    @pl.when(step < steps // 2)
    def _():
        block(*refs[:3], away_ref, True)

    @pl.when(step >= steps // 2)
    def _():
        block(*refs[3:6], near_ref, False)

    @pl.when(step == steps - 1)
    def _():
        core = core_ref[0]
        for job, (_, width) in enumerate(parcel.shapes):
            total = total_ref[:, job * width : (job + 1) * width].astype(low)
            tiles = both_sides(total, core)
            count = len(tiles) // 2
            for at, product in enumerate(tiles):
                kind, tile = divmod(at, count)
                put_rows(parcel, job, product, tile, (kept_ref, sent_ref)[kind], 0)


def memory_back_call(parcel, core, far, near, wk, wv):
    total, width = far[0].shape
    half = total // 2
    name = "memory_back"
    first = lambda: pl.BlockSpec((half, width), lambda step: (jnp.minimum(step, 1), 0))
    second = lambda: pl.BlockSpec((half, width), lambda step: (jnp.maximum(step - 2, 0), 0))
    parcel_shape = (BLOCKS, parcel.rows, LANES)
    fixed = pl.BlockSpec(parcel_shape, lambda step: (0, 0, 0))
    return pl.pallas_call(
        lambda *refs: memory_back(parcel, *refs),
        grid=(4,),
        in_specs=[pl.BlockSpec(memory_space=pltpu.SMEM)]
        + [first() for _ in far]
        + [second() for _ in near]
        + [whole_spec(piece.shape) for piece in (wk, wv)],
        out_specs=[first(), second(), fixed, fixed],
        out_shape=[jax.ShapeDtypeStruct((total, width), low)] * 2
        + [jax.ShapeDtypeStruct(parcel_shape, low)] * 2,
        scratch_shapes=[pltpu.VMEM((width, 2 * width), high)],
        cost_estimate=cost(name),
        compiler_params=pltpu.CompilerParams(vmem_limit_bytes=vmem_bytes),
        name=name,
    )(core, *far, *near, wk, wv)


def land_memory(place_ref, *refs):
    for which in range(len(refs) - 1):

        @pl.when(pl.program_id(0) == which)
        def _():
            refs[-1][0] = refs[which][...].astype(high)


def land_call(place, pieces):
    rows, width = pieces[1].shape
    return pl.pallas_call(
        land_memory,
        out_shape=jax.ShapeDtypeStruct((len(pieces), rows, width), high),
        grid_spec=pltpu.PrefetchScalarGridSpec(
            num_scalar_prefetch=1,
            grid=(len(pieces),),
            in_specs=[
                pl.BlockSpec((rows, width), lambda step, _: (0, 0), pipeline_mode=pl.Buffered(1))
                for _ in pieces
            ],
            out_specs=pl.BlockSpec((1, rows, width), lambda step, place: (place[0] ^ step, 0, 0)),
        ),
        cost_estimate=cost("land_memory"),
        compiler_params=pltpu.CompilerParams(vmem_limit_bytes=vmem_bytes),
        name="land_memory",
    )(place, *pieces)


def two_heads(rows):
    first = lax.broadcasted_iota(jnp.int32, rows.shape, 1) < HD
    zero = jnp.zeros_like(rows)
    return jnp.concatenate([jnp.where(first, rows, zero), jnp.where(first, zero, rows)], axis=0)


def one_pair(stacked):
    half = stacked.shape[1] // 2
    first = lax.broadcasted_iota(jnp.int32, (stacked.shape[0], half), 0) < HD
    return jnp.where(first, stacked[:, :half], stacked[:, half:]).T


def attend_forward_kernel(causal, chunks, carried, last, live_ref, q_ref, k_ref, v_ref, *refs):
    before, refs = refs[:carried], refs[carried:]
    queries = two_heads(q_ref[...])
    wide = queries.shape[0]
    size = k_ref.shape[0] // chunks

    def weigh(here, scores, peak):
        weights = jnp.exp(scores - peak)
        total = jnp.sum(weights, axis=0, keepdims=True)
        weights = weights.astype(low)
        refs[0][0, here, :] = weights
        return total, cols_dot(v_ref[here, :], weights)

    stats_ref, mixed_ref = refs[-2:]
    squares = queries.astype(high)
    squares = (squares * squares).astype(low)
    lengths = rows_dot(jnp.ones((8, LANES), low), squares)[:1]
    if not causal:
        lane = lax.broadcasted_iota(jnp.int32, queries.shape, 1)
        queries = jnp.concatenate([queries, jnp.where(lane == 0, 1.0, 0.0).astype(low)], axis=1)
    for chunk in range(chunks):
        here = slice(chunk * size, (chunk + 1) * size)
        live = size if causal else live_ref[chunk + (chunks if carried else 0)]

        def scored():
            keys = k_ref[here, :]
            if causal:
                key = lax.broadcasted_iota(jnp.int32, (size, wide), 0) + chunk * size
                token = lax.broadcasted_iota(jnp.int32, (size, wide), 1)
                token = jnp.where(token >= wide // 2, token - wide // 2, token)
                return jnp.where(key <= token, rows_dot(keys, queries), neg_big)
            key = lax.broadcasted_iota(jnp.int32, keys.shape, 0)
            lane = lax.broadcasted_iota(jnp.int32, keys.shape, 1)
            dead = jnp.where((lane == 0) & (key >= live), neg_big, 0.0).astype(low)
            return rows_dot(jnp.concatenate([keys, dead], axis=1), queries)

        def keep(scores, peak):
            total, mix = weigh(here, scores, peak)
            stats_ref[chunk : chunk + 1, :] = peak if causal else jnp.where(live > 0, peak, neg_big)
            stats_ref[chunks + chunk : chunks + chunk + 1, :] = total
            mixed_ref[chunk] = mix
            return total

        squares = k_ref[here, :].astype(high)
        squares = squares * squares
        first = lax.broadcasted_iota(jnp.int32, squares.shape, 1) < HD
        sides = [
            jnp.max(jnp.sum(jnp.where(side, squares, 0.0), axis=1, keepdims=True), axis=0, keepdims=True)
            for side in (first, ~first)
        ]
        column = lax.broadcasted_iota(jnp.int32, (1, wide), 1)
        longest = jnp.where(column < wide // 2, sides[0], sides[1])
        total = keep(scored(), 1.01 * jnp.sqrt(lengths * longest))

        @pl.when((live > 0) & (jnp.min(total) < smallest_total))
        def _():
            scores = scored()
            keep(scores, jnp.max(scores, axis=0, keepdims=True))

    peaks = [stats_ref[at : at + 1] for at in range(chunks)]
    totals = [stats_ref[chunks + at : chunks + at + 1] for at in range(chunks)]
    mixes = [mixed_ref[at] for at in range(chunks)]
    if carried:
        stats_in = before[1][0]
        count = chunks
        peaks = [stats_in[at : at + 1] for at in range(count)] + peaks
        totals = [stats_in[count + at : count + at + 1] for at in range(count)] + totals
    top = peaks[0]
    for peak in peaks[1:]:
        top = jnp.maximum(top, peak)
    scales = [jnp.exp(peak - top) for peak in peaks]
    mixed = sum(mix * scale for mix, scale in zip(mixes, scales[-chunks:]))
    if carried:
        earlier = peaks[0]
        for peak in peaks[1:chunks]:
            earlier = jnp.maximum(earlier, peak)
        mixed = mixed + before[0][0] * jnp.exp(earlier - top)
    if last:
        inverse = 1.0 / sum(total * scale for total, scale in zip(totals, scales))
        refs[1][...] = one_pair(mixed * inverse).astype(low)
        for at, scale in enumerate(scales):
            refs[2][0, at : at + 1, :] = scale * inverse
    else:
        refs[1][0] = mixed
        for at in range(chunks):
            refs[2][0, at : at + 1, :] = peaks[at]
            refs[2][0, chunks + at : chunks + at + 1, :] = totals[at]


def attend_forward(queries, keys, values, live, causal, chunks, name, last=True, before=()):
    tokens, width = queries.shape
    patches = keys.shape[0]
    pairs = width // LANES
    by_pair = lambda rows: pl.BlockSpec((rows, LANES), lambda pair, _: (0, pair))
    stack = lambda rows: pl.BlockSpec((1, rows, 2 * tokens), lambda pair, _: (pair, 0, 0))
    return pl.pallas_call(
        lambda *refs: attend_forward_kernel(causal, chunks, len(before), last, *refs),
        out_shape=(
            jax.ShapeDtypeStruct((pairs, patches, 2 * tokens), low),
            jax.ShapeDtypeStruct((tokens, width), low)
            if last
            else jax.ShapeDtypeStruct((pairs, LANES, 2 * tokens), high),
            jax.ShapeDtypeStruct((pairs, 8, 2 * tokens), high),
        ),
        grid_spec=pltpu.PrefetchScalarGridSpec(
            num_scalar_prefetch=1,
            grid=(pairs,),
            in_specs=[by_pair(tokens), by_pair(patches), by_pair(patches)]
            + [stack(piece.shape[1]) for piece in before],
            out_specs=[stack(patches), by_pair(tokens) if last else stack(LANES), stack(8)],
            scratch_shapes=[
                pltpu.VMEM((2 * chunks, 2 * tokens), high),
                pltpu.VMEM((chunks, LANES, 2 * tokens), high),
            ],
        ),
        cost_estimate=cost(name),
        compiler_params=pltpu.CompilerParams(vmem_limit_bytes=vmem_bytes),
        name=name,
    )(live, queries, keys, values, *before)


def attend_backward_kernel(
    chunks,
    offset,
    carried,
    last,
    weight_ref,
    inverse_ref,
    q_ref,
    k_ref,
    v_ref,
    mixed_ref,
    grad_mixed_ref,
    *refs,
):
    before, (grad_q_ref, grad_k_ref, grad_v_ref) = refs[:carried], refs[-3:]
    queries = two_heads(q_ref[...])
    grads = grad_mixed_ref[...].astype(high).T
    mixed = mixed_ref[...].astype(high).T
    first = lax.broadcasted_iota(jnp.int32, grads.shape, 0) < HD
    zero = jnp.zeros_like(grads)
    grads = jnp.concatenate([jnp.where(first, grads, zero), jnp.where(first, zero, grads)], axis=1)
    mixed = jnp.concatenate([mixed, mixed], axis=1)
    size = k_ref.shape[0] // chunks
    grad_q = jnp.zeros(grads.shape, high)
    for chunk in range(chunks):
        here = slice(chunk * size, (chunk + 1) * size)
        at = offset + chunk
        scaled = (grads * inverse_ref[0, at : at + 1, :]).astype(low)
        wide = scaled.astype(high)
        centre = jnp.sum(wide * mixed, axis=0, keepdims=True)
        rows = wide.T.astype(low)
        weights = weight_ref[0, here, :]
        grad_probs = plain_dot(v_ref[here, :], scaled)
        grad_scores = (weights.astype(high) * (grad_probs - centre)).astype(low)
        grad_v_ref[here, :] = plain_dot(weights, rows).astype(low)
        grad_k_ref[here, :] = plain_dot(grad_scores, queries).astype(low)
        grad_q = grad_q + cols_dot(k_ref[here, :], grad_scores)
    grad_q = one_pair(grad_q)
    if carried:
        grad_q = grad_q + before[0][...]
    grad_q_ref[...] = grad_q.astype(grad_q_ref.dtype)


def attend_backward(
    weights,
    inverse,
    queries,
    keys,
    values,
    mixed,
    grad_mixed,
    chunks,
    offset,
    name,
    last=True,
    before=(),
    pairs=None,
    filled=(),
):
    tokens, width = queries.shape
    patches = keys.shape[0]
    begin, end = pairs or (0, width // LANES)
    by_token = pl.BlockSpec((tokens, LANES), lambda pair: (0, pair + begin))
    by_patch = pl.BlockSpec((patches, LANES), lambda pair: (0, pair + begin))
    return pl.pallas_call(
        lambda *refs: attend_backward_kernel(chunks, offset, len(before), last, *refs),
        out_shape=(
            jax.ShapeDtypeStruct((tokens, width), low if last else high),
            jax.ShapeDtypeStruct((patches, width), low),
            jax.ShapeDtypeStruct((patches, width), low),
        ),
        grid=(end - begin,),
        in_specs=[
            pl.BlockSpec((1, patches, 2 * tokens), lambda pair: (pair + begin, 0, 0)),
            pl.BlockSpec((1, 8, 2 * tokens), lambda pair: (pair + begin, 0, 0)),
            by_token,
            by_patch,
            by_patch,
            by_token,
            by_token,
        ]
        + [by_token] * len(before)
        + [pl.BlockSpec(memory_space=pl.ANY)] * len(filled),
        out_specs=[by_token, by_patch, by_patch],
        input_output_aliases={7 + len(before) + which: which for which in range(len(filled))},
        cost_estimate=cost(name),
        compiler_params=pltpu.CompilerParams(vmem_limit_bytes=vmem_bytes),
        name=name,
    )(weights, inverse, queries, keys, values, mixed, grad_mixed, *before, *filled)


def swap(piece, axis_name, mask):
    size = lax.axis_size(axis_name)
    return lax.ppermute(piece, axis_name, [(place, place ^ mask) for place in range(size)])


def bit_of(axis_name, bit):
    return (lax.axis_index(axis_name) >> bit) & 1


def pick(piece, which):
    return lax.dynamic_index_in_dim(piece, which, 0, keepdims=False)


class Parcel:
    def __init__(self, shapes, extra=0):
        self.shapes = shapes
        self.heights = [height // BLOCKS for height, _ in shapes]
        self.plain = [width // 4 // LANES for _, width in shapes]
        self.at = []
        at = 0
        for (_, width), tiles, height in zip(shapes, self.plain, self.heights):
            self.at.append(at)
            at += tiles * height + (height // 2 if width // 4 % LANES else 0)
        self.extra = extra
        self.own = at + extra
        self.rows = 2 * self.own


def place(block):
    return (block & 1) * 4 + (block & 2) + (block >> 2)


def core_tiles(grad, core):
    quarter = grad.shape[1] // 4
    starts = [core * quarter, 2 * quarter + core * quarter]
    tiles = [
        grad[:, start + at : start + at + LANES]
        for start in starts
        for at in range(0, quarter - LANES + 1, LANES)
    ]
    rest = quarter % LANES
    if rest:
        tiles.append(
            jnp.concatenate(
                [grad[:, start + quarter - rest : start + quarter] for start in starts], axis=1
            )
        )
    return tiles


def both_sides(grad, core):
    first, second = core_tiles(grad, 0), core_tiles(grad, 1)
    own = [jnp.where(core == 0, one, other) for one, other in zip(first, second)]
    return own + [jnp.where(core == 0, other, one) for one, other in zip(first, second)]


def self_backward(
    parcel,
    core_ref,
    grad_q_two_ref,
    hidden_ref,
    grad_in_ref,
    gain_ref,
    cross_query_ref,
    out_weight_ref,
    feed_gain_ref,
    attended_ref,
    weight_ref,
    inverse_ref,
    q_ref,
    k_ref,
    v_ref,
    mixed_ref,
    wq_ref,
    wk_ref,
    wv_ref,
    normed_hbm_ref,
    next_normed_hbm_ref,
    tokens_hbm_ref,
    tokens_grad_ref,
    kept_ref,
    sent_ref,
    grad_hidden_ref,
    branch_ref,
    grad_mixed_ref,
    gains_ref,
    grads_ref,
    back_ref,
    late_ref,
    turned_ref,
    packed_ref,
    done_ref,
):
    pair = pl.program_id(0)
    pairs = pl.num_programs(0)
    late = [
        pltpu.make_async_copy(far_ref, late_ref.at[at], done_ref.at[at])
        for at, far_ref in enumerate((normed_hbm_ref, next_normed_hbm_ref, tokens_hbm_ref))
    ]

    @pl.when(pair == 0)
    def _():
        for copy in late:
            copy.start()
        to_rows, to_gain = norm_back(
            hidden_ref[...], gain_ref[1:2, :], rows_dot(grad_q_two_ref[...], cross_query_ref[...])
        )
        grad_hidden = grad_in_ref[...] + to_rows
        grad_hidden_ref[...] = grad_hidden
        branch = grad_hidden.astype(low)
        branch_ref[...] = branch
        grad_mixed_ref[...] = rows_dot(branch, out_weight_ref[...]).astype(low)
        gains_ref[1:2, :] = to_gain
        gains_ref[2:3, :] = feed_gain_ref[...]
        back_ref[...] = jnp.zeros_like(back_ref)

    here = pl.ds(pl.multiple_of(pair * LANES, LANES), LANES)
    views = [grads_ref.at[at, :, here] for at in range(3)]
    attend_backward_kernel(
        1,
        0,
        0,
        True,
        weight_ref,
        inverse_ref,
        q_ref,
        k_ref,
        v_ref,
        mixed_ref,
        grad_mixed_ref.at[:, here],
        *views,
    )
    grads = jnp.concatenate([view[...] for view in views], axis=1)
    weights = jnp.concatenate([wq_ref[...], wk_ref[...], wv_ref[...]], axis=1)
    back_ref[...] += rows_dot(grads, weights)

    @pl.when(pair == pairs - 1)
    def _():
        for copy in late:
            copy.wait()
        to_rows, to_gain = norm_back(late_ref[2].astype(high), gain_ref[0:1, :], back_ref[...])
        tokens_grad_ref[...] = (grad_hidden_ref[...] + to_rows).astype(low)
        gains_ref[0:1, :] = to_gain
        width = to_gain.shape[1]
        tiles = width // LANES
        packed_ref[...] = jnp.zeros_like(packed_ref)
        for gain in range(3):
            for tile in range(tiles):
                packed_ref[gain * tiles + tile : gain * tiles + tile + 1, :] = gains_ref[
                    gain : gain + 1, tile * LANES : (tile + 1) * LANES
                ]
        packed = packed_ref[...].astype(low)
        for out_ref in (kept_ref, sent_ref):
            for block in range(BLOCKS):
                for end in (parcel.own, parcel.rows):
                    out_ref[block, end - parcel.extra : end, :] = packed
        core = core_ref[0]
        jobs = (
            [(late_ref.at[0], grads_ref[at]) for at in range(3)]
            + [(late_ref.at[1], grad_q_two_ref[...])]
            + [(attended_ref, branch_ref[...])]
        )
        for job, (rows_ref, grad) in enumerate(jobs):
            if job in (0, 3, 4):
                turned_ref[...] = rows_ref[...].T
            tiles = both_sides(grad, core)
            count = len(tiles) // 2
            for begin in range(0, 2 * count, 2):
                product = plain_dot(
                    turned_ref[...], jnp.concatenate(tiles[begin : begin + 2], axis=1)
                ).astype(low)
                for slot in (0, 1):
                    kind, tile = divmod(begin + slot, count)
                    put_rows(parcel, job, product, tile, (kept_ref, sent_ref)[kind], slot)


def self_backward_call(
    parcel,
    core,
    grad_q_two,
    hidden,
    grad_in,
    gain,
    cross_query,
    out_weight,
    feed_gain,
    attended,
    weights,
    inverse,
    queries,
    keys,
    values,
    projections,
    late,
):
    rows, width = hidden.shape
    pairs = width // LANES
    columns = pl.BlockSpec((rows, LANES), lambda pair: (0, pair))
    stack = lambda height: pl.BlockSpec((1, height, 2 * rows), lambda pair: (pair, 0, 0))
    whole = (grad_q_two, hidden, grad_in, gain, cross_query, out_weight, feed_gain, attended)
    fixed = lambda shape: pl.BlockSpec(shape, lambda pair: (0,) * len(shape))
    parcel_shape = (BLOCKS, parcel.rows, LANES)
    return pl.pallas_call(
        lambda *refs: self_backward(parcel, *refs),
        grid=(pairs,),
        in_specs=[pl.BlockSpec(memory_space=pltpu.SMEM)]
        + [whole_spec(piece.shape) for piece in whole]
        + [stack(rows), stack(8), columns, columns, columns, columns]
        + [pl.BlockSpec((width, LANES), lambda pair: (0, pair))] * 3
        + [pl.BlockSpec(memory_space=pl.ANY)] * 3,
        out_specs=[fixed((rows, width)), whole_spec(parcel_shape), whole_spec(parcel_shape)],
        out_shape=[
            jax.ShapeDtypeStruct((rows, width), low),
            jax.ShapeDtypeStruct(parcel_shape, low),
            jax.ShapeDtypeStruct(parcel_shape, low),
        ],
        scratch_shapes=[
            pltpu.VMEM((rows, width), high),
            pltpu.VMEM((rows, width), low),
            pltpu.VMEM((rows, width), low),
            pltpu.VMEM((8, width), high),
            pltpu.VMEM((3, rows, width), low),
            pltpu.VMEM((rows, width), high),
            pltpu.VMEM((3, rows, width), low),
            pltpu.VMEM((width, rows), low),
            pltpu.VMEM((parcel.extra, LANES), high),
            pltpu.SemaphoreType.DMA((3,)),
        ],
        cost_estimate=cost("self_backward"),
        compiler_params=pltpu.CompilerParams(vmem_limit_bytes=vmem_bytes),
        name="self_backward",
    )(
        core,
        *whole,
        weights,
        inverse,
        queries,
        keys,
        values,
        attended,
        *projections,
        *late,
    )


def fold_one(mine_ref, kept_ref, received_ref, *out_refs):
    for which, out_ref in enumerate(out_refs):

        @pl.when(pl.program_id(0) == which)
        def _():
            total = kept_ref[0].astype(high) + received_ref[0].astype(high)
            out_ref[...] = total.astype(low)


def fold_one_call(name, mine, kept, received, view, shape, index):
    block = pl.BlockSpec((1, *shape), lambda step, mine: index(mine[0] ^ step))
    return pl.pallas_call(
        fold_one,
        grid_spec=pltpu.PrefetchScalarGridSpec(
            num_scalar_prefetch=1,
            grid=(4,),
            in_specs=[block, block],
            out_specs=[
                pl.BlockSpec(shape, lambda step, _: (0, 0, 0), pipeline_mode=pl.Buffered(1))
            ]
            * 4,
        ),
        out_shape=[jax.ShapeDtypeStruct(shape, low)] * 4,
        cost_estimate=cost(name),
        compiler_params=pltpu.CompilerParams(vmem_limit_bytes=vmem_bytes),
        name=name,
    )(mine, kept.reshape(view), received.reshape(view))


def sum_of(refs):
    first, second, third, fourth = [ref[...].astype(high) for ref in refs]
    return (first + second) + (third + fourth)


def fold_two(parcel, with_x, first_ref, second_ref, third_ref, fourth_ref, out_ref):
    total = sum_of((first_ref, second_ref, third_ref, fourth_ref)).astype(low)
    if with_x:
        out_ref[...] = total
    else:
        for which in range(4):
            begin = (which & 1) * parcel.own
            out_ref[which] = total[which >> 1, begin : begin + parcel.own, :]


def fold_end(parcel, parts_ref, *outs):
    total = sum_of([parts_ref.at[which] for which in range(4)])
    for job, rows in enumerate(parcel.heights):
        at = parcel.at[job]
        for tile in range(parcel.plain[job]):
            outs[job][:, tile * LANES : (tile + 1) * LANES] = total[at : at + rows]
            at += rows
        begin = parcel.plain[job] * LANES
        rest = outs[job].shape[1] - begin
        if rest:
            outs[job][: rows // 2, begin:] = total[at : at + rows // 2, :rest]
            outs[job][rows // 2 :, begin:] = total[at : at + rows // 2, rest:]
    if parcel.extra:
        outs[-1][...] = total[-parcel.extra :]


class Travel:
    def __init__(self, parcel, kept, sent, name, with_x):
        self.parcel = parcel
        self.name = name
        self.kept = kept
        self.received = swap(sent, "narrow", 1)
        self.top = lax.axis_size("items").bit_length() - 4
        self.with_x = with_x

    def joint(self, up, side):
        narrow = lax.axis_size("narrow")
        return [
            (place, ((place // narrow) ^ up) * narrow + ((place % narrow) ^ side))
            for place in range(lax.axis_size("items") * narrow)
        ]

    def fold_one(self, *earlier):
        kept, received = lax.optimization_barrier((self.kept, self.received, *earlier))[:2]
        rows, top = self.parcel.rows, self.top
        if self.with_x:
            mine = bit_of("items", top) * 2 + bit_of("narrow", 1)
            view, shape = (2, 4, rows, LANES), (4, self.parcel.own, LANES)
            partners = [(0, 2), (1 << top, 0), (1 << top, 2)]
            index = lambda part: (part >> 1, 0, part & 1, 0)
        else:
            mine = bit_of("items", top) * 2 + bit_of("items", top + 1)
            view, shape = (4, 2, rows, LANES), (2, rows, LANES)
            partners = [(2 << top, 0), (1 << top, 0), (3 << top, 0)]
            index = lambda part: (part, 0, 0, 0)
        parts = fold_one_call(
            self.name + "_one", mine.reshape(1), kept, received, view, shape, index
        )
        self.parts = [parts[0]] + [
            lax.ppermute(part, ("items", "narrow"), self.joint(*partner))
            for part, partner in zip(parts[1:], partners)
        ]
        return parts[0]

    def fold_two(self, *earlier):
        parts = lax.optimization_barrier((*self.parts, *earlier))[:4]
        parcel = self.parcel
        (parts,) = one_step_call(
            lambda *refs: fold_two(parcel, self.with_x, *refs),
            self.name + "_two",
            list(parts),
            [((4, parcel.own, LANES), low)],
        )
        far = 4 << self.top
        first, second = ((2 << self.top, 0), (far, 0)) if self.with_x else ((far, 0), (0, 2))
        narrow = lax.axis_size("narrow")
        clear = first[0] | second[0]
        side = first[1] | second[1]
        groups = [
            [
                (item | one[0] | two[0]) * narrow + (other | one[1] | two[1])
                for one in ((0, 0), first)
                for two in ((0, 0), second)
            ]
            for item in range(lax.axis_size("items"))
            for other in range(narrow)
            if not item & clear and not other & side
        ]
        self.parts = parts
        self.groups = groups
        return parts

    def send(self, *earlier):
        parts = lax.optimization_barrier((self.parts, *earlier))[0]
        self.parts = lax.all_to_all(
            parts, ("items", "narrow"), 0, 0, axis_index_groups=self.groups, tiled=True
        )

    def end(self, *earlier):
        parts = lax.optimization_barrier((self.parts, *earlier))[0]
        parcel = self.parcel
        outs = [((height // BLOCKS, width // 4), high) for height, width in parcel.shapes]
        outs += [((parcel.extra, LANES), high)] if parcel.extra else []
        outs = list(
            one_step_call(
                lambda *refs: fold_end(parcel, *refs),
                self.name + "_end",
                [parts],
                outs,
            )
        )
        count = len(parcel.shapes)
        extras = outs[count:]
        for bit in range(self.top, 0, -1):
            extras = [piece + swap(piece, "items", 1 << (bit - 1)) for piece in extras]
        return list(lower_bits(outs[:count])) + extras


def exchange(piece):
    return lax.all_to_all(piece, "narrow", split_axis=0, concat_axis=0, tiled=True)


def body(
    tokens,
    memory,
    mem_count,
    cotangent,
    gain_self,
    self_query,
    self_key,
    self_value,
    self_out,
    gain_cross,
    cross_query,
    cross_key,
    cross_value,
    cross_out,
    gain_feed,
    gate_weight,
    up_weight,
    down_weight,
):
    width = tokens.shape[2]
    inner = gate_weight.shape[1]
    gains_in = jnp.stack([gain_self, gain_cross, gain_feed])
    parts = lax.axis_size("narrow")
    mine = lax.axis_index("narrow")
    token_rows = exchange(tokens).reshape(-1, width)
    own_memory, *away_memory = [pick(memory, mine ^ which) for which in range(parts)]
    pieces = [own_memory] + [
        swap(piece, "narrow", which + 1) for which, piece in enumerate(away_memory)
    ]
    cotangent_rows = exchange(cotangent).reshape(-1, width)
    count = pick(mem_count, mine)
    local_mem = memory.shape[1]
    live = count - local_mem * (mine ^ jnp.arange(parts, dtype=jnp.int32))
    kinds = [((2 * local_mem, width), low)] * 3
    near_rows, near_keys, near_values = one_step_call(
        enter_memory,
        "enter_memory_near",
        [pieces[0], pieces[1], cross_key, cross_value],
        kinds,
    )
    (
        normed_one,
        query_one,
        key_one,
        value_one,
        weights_one,
        attended,
        inverse_one,
        hidden_one,
        normed_two,
        query_two,
    ) = self_forward_call(
        after(token_rows, near_keys),
        gains_in,
        cross_query,
        self_query,
        self_key,
        self_value,
        self_out,
    )
    near_weights, near_mixed, near_stats = attend_forward(
        query_two, near_keys, near_values, live, False, 2, "cross_forward_near", False
    )
    far_rows, far_keys, far_values = one_step_call(
        enter_memory,
        "enter_memory_far",
        [after(pieces[2], near_stats), pieces[3], cross_key, cross_value],
        kinds,
    )
    far_weights, crossed, inverse_two = attend_forward(
        query_two,
        far_keys,
        far_values,
        live,
        False,
        2,
        "cross_forward_far",
        True,
        (near_mixed, near_stats),
    )
    square = (width, width)
    feed_parcel = Parcel([(width, inner), (width, inner), (inner, width), square])
    result, grad_hidden_two, branch_two, grad_crossed, grad_gain_feed, *feed_parts = feed_call(
        feed_parcel,
        bit_of("narrow", 0).reshape(1),
        crossed,
        hidden_one,
        cotangent_rows,
        gains_in,
        cross_out,
        gate_weight,
        up_weight,
        down_weight,
    )
    feed_trip = Travel(feed_parcel, *feed_parts, "feed_weights", True)
    result = exchange(result.reshape(tokens.shape))
    far = ()
    ready = feed_trip.kept
    for pairs in ((0, 3), (3, 6)):
        far = attend_backward(
            far_weights,
            inverse_two,
            query_two,
            far_keys,
            far_values,
            crossed,
            after(grad_crossed, ready),
            2,
            2,
            "cross_backward_far_a" if pairs[0] == 0 else "cross_backward_far_b",
            False,
            pairs=pairs,
            filled=far,
        )
        ready = feed_trip.fold_one(far[0]) if pairs[0] == 0 else far[0]
    far_grad_q, far_grad_k, far_grad_v = far
    grad_query_two, near_grad_k, near_grad_v = attend_backward(
        near_weights,
        inverse_two,
        query_two,
        near_keys,
        near_values,
        crossed,
        after(grad_crossed, result),
        2,
        0,
        "cross_backward_near",
        True,
        (far_grad_q,),
    )
    extra = -(-3 * width // LANES // 16) * 16
    self_parcel = Parcel([square] * 5, extra)
    tokens_grad, *self_parts = self_backward_call(
        self_parcel,
        bit_of("narrow", 0).reshape(1),
        grad_query_two,
        hidden_one,
        grad_hidden_two,
        gains_in,
        cross_query,
        self_out,
        grad_gain_feed,
        attended,
        weights_one,
        inverse_one,
        query_one,
        key_one,
        value_one,
        [self_query, self_key, self_value],
        [normed_one, normed_two, token_rows],
    )
    self_trip = Travel(self_parcel, *self_parts, "self_weights", True)
    tokens_grad = exchange(tokens_grad.reshape(tokens.shape))
    ready = feed_trip.fold_two(self_parts[0])
    feed_trip.send()
    ready = self_trip.fold_one(ready)
    cross_parcel = Parcel([square] * 2)
    grad_away, grad_near, *cross_parts = memory_back_call(
        cross_parcel,
        bit_of("narrow", 0).reshape(1),
        [after(far_rows, ready, tokens_grad), far_grad_k, far_grad_v],
        [near_rows, near_grad_k, near_grad_v],
        cross_key,
        cross_value,
    )
    landed_away = swap(grad_away, "narrow", 2)
    cross_trip = Travel(cross_parcel, *cross_parts, "cross_weights", False)
    tokens_grad = tokens_grad.astype(high)
    ready = self_trip.fold_two(grad_away)
    self_trip.send()
    ready = cross_trip.fold_one(ready)
    gate_sum, up_sum, down_sum, cross_out_sum = feed_trip.end(ready)
    ready = gate_sum
    ready = cross_trip.fold_two(ready)
    cross_trip.send()
    grad_near, landed_away = lax.optimization_barrier((grad_near, landed_away, ready))[:2]
    landed_core = swap(grad_near[local_mem:], "narrow", 1)
    landed_far = swap(landed_away[local_mem:], "narrow", 1)
    self_query_sum, self_key_sum, self_value_sum, cross_query_sum, self_out_sum, gains = (
        self_trip.end(ready)
    )
    memory_grad = land_call(
        mine.reshape(1),
        [after(grad_near, self_query_sum), landed_core, landed_away, landed_far],
    )
    cross_key_sum, cross_value_sum = cross_trip.end(memory_grad)
    gains = gains[: 3 * width // LANES].reshape(3, width)
    return (
        result,
        tokens_grad,
        memory_grad,
        gains[0],
        self_query_sum,
        self_key_sum,
        self_value_sum,
        self_out_sum,
        gains[1],
        cross_query_sum,
        cross_key_sum,
        cross_value_sum,
        cross_out_sum,
        gains[2],
        gate_sum,
        up_sum,
        down_sum,
    )


def solution(mesh):
    in_specs = (
        P("items", "narrow", None),
        P("items", "narrow", None),
        P("items"),
        P("items", "narrow", None),
        P(),
        P(),
        P(),
        P(),
        P(),
        P(),
        P(),
        P(),
        P(),
        P(),
        P(),
        P(),
        P(),
        P(),
    )
    out_specs = (
        P("items", "narrow", None),
        P("items", "narrow", None),
        P("items", "narrow", None),
        P(),
        P("items", "narrow"),
        P("items", "narrow"),
        P("items", "narrow"),
        P("items", "narrow"),
        P(),
        P("items", "narrow"),
        P("items", "narrow"),
        P("items", "narrow"),
        P("items", "narrow"),
        P(),
        P("items", "narrow"),
        P("items", "narrow"),
        P("items", "narrow"),
    )
    return jax.shard_map(body, mesh=mesh, in_specs=in_specs, out_specs=out_specs, check_vma=False)
```
